32 devices in a mesh: dp: 8 (over y, x, core), tensor: 4 (over z).
Axes of the slice: x: 2, y: 2, z: 4, core: 2. Of those that a mesh axis runs over, the one named last changes fastest.
Arguments:
- tokens: bfloat16 [8, 2048, 768], P('dp', 'tensor'), may hold values from -6 to 6
- lengths: int32 [8, 24], P('dp'), may hold values from 1 to 1024, 2048 in all within a row
- w_qkv: bfloat16 [768, 3, 768], P(None, None, 'tensor'), may hold values from -0.21875 to 0.21875
- w_out: bfloat16 [768, 768], P('tensor'), may hold values from -1.25 to 1.25
- norm1_scale: float32 [768], replicated, may hold values from 0.25 to 1.75
- norm1_shift: float32 [768], replicated, may hold values from -3 to 3
- w_gate_up: bfloat16 [768, 2, 3072], P(None, None, 'tensor'), may hold values from -0.21875 to 0.21875
- w_down: bfloat16 [3072, 768], P('tensor'), may hold values from -0.109375 to 0.109375
- norm2_scale: float32 [768], replicated, may hold values from 0.25 to 1.75
- norm2_shift: float32 [768], replicated, may hold values from -3 to 3
- cotangent: bfloat16 [8, 2048, 768], P('dp', 'tensor'), may hold values from -15 to 15
Outputs:
- layer_out: bfloat16 [8, 2048, 768], P('dp', 'tensor')
- grad_tokens: float32 [8, 2048, 768], P('dp', 'tensor')
- grad_w_qkv: float32 [768, 3, 768], P(None, None, 'tensor')
- grad_w_out: float32 [768, 768], P('tensor')
- grad_norm1_scale: float32 [768], replicated
- grad_norm1_shift: float32 [768], replicated
- grad_w_gate_up: float32 [768, 2, 3072], P(None, None, 'tensor')
- grad_w_down: float32 [3072, 768], P('tensor')
- grad_norm2_scale: float32 [768], replicated
- grad_norm2_shift: float32 [768], replicated
The draws below stay inside these ranges and needn't reach their ends.
Inputs may be any that keep to these rules, and one draw needn't show every extreme that they name: Each row holds 24 lengths that sum to 2048: the first 23 are the row's documents in order, the last is the padding at its end.
All inputs are finite; a program needn't handle non-finite values.
Results may differ from the reference program's by a relative error of at most 0.019.
Values may be sent and summed in bfloat16 or wider, within the bound.
No kernel may reach another device: no remote copies, remote signals or barrier semaphores. Data moves between devices by JAX's collectives and lax.ppermute only.
A program may use at most 192 MiB of HBM per device.

```python
import math
import jax
import jax.numpy as jnp
import numpy as np
from jax import lax

D = 768
HEADS = 12
HD = 64
FF = 3072
SEQ = 2048
DOCS = 24
LONGEST = 1024
ROWS = 8


def draw_cotangent(key, part):
    key_base, key_token = jax.random.split(key, 2)
    row_place = jnp.arange(ROWS, dtype=jnp.float32)[:, None, None]
    rising = 3.0 ** (row_place / max(ROWS - 1, 1))
    token_scale = jnp.exp(jax.random.uniform(key_token, (ROWS, SEQ, 1), jnp.float32, -0.7, 0.7))
    base_draw = jax.random.truncated_normal(key_base, -4.0, 4.0, (ROWS, SEQ, D), jnp.float32)
    return (base_draw * rising * token_scale / 1.7).astype(jnp.bfloat16)


def steps_of(stream_key, dims, cuts, smallest, top_value):
    def one(axis_at, shards_of):
        steps = jax.random.uniform(jax.random.fold_in(jax.random.fold_in(stream_key, 6), axis_at), (shards_of,), jnp.float32, smallest / len(cuts), top_value / len(cuts))
        return jnp.repeat(jnp.exp(steps), dims[axis_at] // shards_of).reshape((-1,) + (1,) * (len(dims) - axis_at - 1))

    loudness = one(*cuts[0])
    for cut in cuts[1:]:
        loudness = loudness * one(*cut)
    return loudness


def length_profile(amount, total, most, skew):
    weights = [(1 << 20) // math.isqrt(standing ** skew) + 1 for standing in range(2, amount + 1)]
    rest, counts = total - most - (amount - 1), [1] * (amount - 1)
    while rest > 0:
        free = [i for i in range(amount - 1) if counts[i] < most]
        pool, left = sum([weights[i] for i in free]), rest
        for i in free:
            more = min(most - counts[i], max(1, left * weights[i] // pool), rest)
            counts[i] = counts[i] + more
            rest = rest - more
    return np.array([most] + counts)


def uneven_parts(own_key, count, total, reach, lean):
    if count == 2:
        one = jax.random.randint(own_key, (), max(1, total - reach), min(reach, total - 1) + 1)
        return jnp.stack([one, total - one])
    sizes = jnp.asarray(length_profile(count, total, reach, lean), jnp.int32)
    couples = (count - 1) // 2
    source_of, sink = sizes[1:1 + 2 * couples:2], sizes[2:2 + 2 * couples:2]
    margin = jnp.minimum(source_of - 1, reach - sink)
    passed = jax.random.randint(jax.random.fold_in(own_key, 1), (couples,), 0, 1 << 20) % (margin + 1)
    sizes = sizes.at[1:1 + 2 * couples:2].set(source_of - passed).at[2:2 + 2 * couples:2].set(sink + passed)
    return sizes[jax.random.permutation(jax.random.fold_in(own_key, 2), count)]


def gaussian(rng, shape, width, limit, pieces=(), held_as=jnp.bfloat16):
    drawn = jax.random.normal(rng, shape, jnp.float32) * width
    if len(pieces) > 0:
        drawn = steps_of(rng, shape, pieces, -0.22, 0.18) * drawn
    return jnp.clip(drawn, min=-limit, max=limit).astype(held_as)


def setup_inputs(seed: int = 0) -> dict:
    keys = jax.random.split(jax.random.key(seed), 12)
    return {
        "tokens": gaussian(keys[0], (ROWS, SEQ, D), 1.0, 6.0, ((0, 8), (1, 4))),
        "lengths": jax.vmap(lambda own: uneven_parts(own, DOCS, SEQ, LONGEST, 2))(jax.random.split(keys[1], ROWS)).reshape((ROWS, DOCS)).astype(jnp.int32),
        "w_qkv": gaussian(keys[2], (D, 3, D), D ** -0.5, 0.21875, ((2, 4),)),
        "w_out": gaussian(keys[3], (D, D), (D // 32) ** -0.5, 1.25, ((0, 4),)),
        "norm1_scale": jnp.clip(1.0 + 0.15 * jax.random.normal(keys[4], (D,), jnp.float32), 0.25, 1.75),
        "norm1_shift": gaussian(keys[5], (D,), 0.5, 3.0, (), jnp.float32),
        "w_gate_up": gaussian(keys[6], (D, 2, FF), D ** -0.5, 0.21875, ((2, 4),)),
        "w_down": gaussian(keys[7], (FF, D), FF ** -0.5, 0.109375, ((0, 4),)),
        "norm2_scale": jnp.clip(1.0 + 0.15 * jax.random.normal(keys[8], (D,), jnp.float32), 0.25, 1.75),
        "norm2_shift": gaussian(keys[9], (D,), 0.5, 3.0, (), jnp.float32),
        "cotangent": draw_cotangent(jax.random.fold_in(keys[11], 71), 0),
    }


@jax.custom_vjp
def low(v):
    return lax.optimization_barrier(v.astype(jnp.bfloat16)).astype(jnp.float32)

@jax.custom_vjp
def low_back(v):
    return v

def low_keep(v):
    return (low(v), None)

def low_pass(kept, grad):
    return (grad,)

def back_keep(v):
    return (v, None)

def back_low(kept, grad):
    return (low(grad),)
low.defvjp(low_keep, low_pass)
low_back.defvjp(back_keep, back_low)
EPSILON = 1e-05
ROPE_BASE = 1000.0
MASKED = -1e+30

def matmul(left, right):
    return jnp.dot(left, right, precision=lax.Precision.HIGHEST, preferred_element_type=jnp.float32)

def doc_layout(row_lengths):
    row_lengths = row_lengths.astype(jnp.int32)
    doc_ends = jnp.cumsum(row_lengths).astype(jnp.int32)
    starts = (doc_ends - row_lengths).astype(jnp.int32)
    places = jnp.arange(SEQ, dtype=jnp.int32)
    segment = lax.optimization_barrier(jnp.sum((places[:, None] >= doc_ends[None, :]).astype(jnp.int32), axis=1)).astype(jnp.int32)
    member = segment[:, None] == jnp.arange(DOCS, dtype=jnp.int32)[None, :]
    offset = lax.optimization_barrier(jnp.sum(jnp.where(member, starts[None, :], 0), axis=1)).astype(jnp.int32)
    position = (places - offset).astype(jnp.float32)
    valid_row = (segment < DOCS - 1).astype(jnp.float32)
    return (segment, position, valid_row)

def rope_tables(position):
    half_dim = HD // 2
    inverse = ROPE_BASE ** (-2.0 * jnp.arange(half_dim, dtype=jnp.float32) / HD)
    angles = position[:, None] * inverse[None, :]
    return (jnp.cos(angles), jnp.sin(angles))

def rotate(heads_values, cosine_table, sine_table):
    half_dim = heads_values.shape[-1] // 2
    first_half = heads_values[..., :half_dim]
    second_half = heads_values[..., half_dim:]
    cos_part = cosine_table[:, None, :]
    sin_part = sine_table[:, None, :]
    return jnp.concatenate([first_half * cos_part - second_half * sin_part, second_half * cos_part + first_half * sin_part], axis=-1)

def attention(queries, keys_all, values, segment):
    block_rows = min(512, SEQ)
    scale_factor = HD ** (-0.5)

    def one_block(block_index):
        first_row = block_index * block_rows
        query_block = lax.dynamic_slice_in_dim(queries, first_row, block_rows, 0)
        seg_block = lax.dynamic_slice_in_dim(segment, first_row, block_rows, 0)
        scores = low_back(scale_factor * jnp.einsum('qhe,khe->hqk', query_block, keys_all, precision=lax.Precision.HIGHEST))
        same_doc = seg_block[:, None] == segment[None, :]
        scores = jnp.where(same_doc[None], scores, MASKED)
        attn_probs = low(jax.nn.softmax(scores, axis=-1))
        return jnp.einsum('hqk,khe->qhe', attn_probs, values, precision=lax.Precision.HIGHEST)
    blocks_out = lax.map(jax.checkpoint(one_block), jnp.arange(SEQ // block_rows, dtype=jnp.int32))
    return blocks_out.reshape(SEQ, HEADS, HD)

def layer_norm(values, scale_vec, shift_vec):
    centered = values - lax.optimization_barrier(jnp.mean(values, axis=-1, keepdims=True))
    variance = lax.optimization_barrier(jnp.mean(centered * centered, axis=-1, keepdims=True))
    return centered * lax.rsqrt(variance + EPSILON) * scale_vec + shift_vec

def layer(tokens_row, w_qkv, w_out, norm1_scale, norm1_shift, w_gate_up, w_down, norm2_scale, norm2_shift, segment, cosine_table, sine_table, valid_row):
    projected = low_back(matmul(low(tokens_row), w_qkv.reshape(D, 3 * D))).reshape(SEQ, 3, HEADS, HD)
    queries = low(low_back(rotate(projected[:, 0], cosine_table, sine_table)))
    keys_all = low(low_back(rotate(projected[:, 1], cosine_table, sine_table)))
    values = low(projected[:, 2])
    attended = attention(queries, keys_all, values, segment) * valid_row[:, None, None]
    mixed_heads = low_back(low(attended)).reshape(SEQ, D)
    branch = low_back(matmul(mixed_heads, w_out))
    normed = layer_norm(tokens_row + branch, norm1_scale, norm1_shift)
    hidden_pre = low_back(matmul(low(normed), w_gate_up.reshape(D, 2 * FF))).reshape(SEQ, 2, FF)
    active = low(jax.nn.silu(hidden_pre[:, 0]) * hidden_pre[:, 1])
    feed_out = low_back(matmul(active, w_down))
    return layer_norm(normed + feed_out, norm2_scale, norm2_shift)

def reference(tokens, lengths, w_qkv, w_out, norm1_scale, norm1_shift, w_gate_up, w_down, norm2_scale, norm2_shift, cotangent):
    weights = tuple((member.astype(jnp.float32) for member in (w_qkv, w_out, norm1_scale, norm1_shift, w_gate_up, w_down, norm2_scale, norm2_shift)))

    def row_step(running, row_items):
        tokens_row, row_lengths, cot_row = row_items
        segment, position, valid_row = doc_layout(row_lengths)
        cosine_table, sine_table = rope_tables(position)

        def forward(tokens_value, *params):
            return layer(tokens_value, *params, segment, cosine_table, sine_table, valid_row)
        output, pullback = jax.vjp(forward, tokens_row.astype(jnp.float32), *weights)
        gradients = pullback(cot_row.astype(jnp.float32))
        running = tuple((acc + gradient for acc, gradient in zip(running, gradients[1:])))
        return (running, (output.astype(jnp.bfloat16), gradients[0]))
    zeros = tuple((jnp.zeros_like(member) for member in weights))
    running, (outputs, input_grads) = lax.scan(row_step, zeros, (tokens, lengths, cotangent))
    return (outputs, input_grads, running[0], running[1], running[2], running[3], running[4], running[5], running[6], running[7])
```

```python
import functools

import jax
import jax.numpy as jnp
from jax import lax
from jax.experimental import pallas as pl
from jax.experimental.pallas import tpu as pltpu
from jax.sharding import PartitionSpec as P

TILE = 256
HALF = 32
BIG = 1e30
f32, bf16 = jnp.float32, jnp.bfloat16

def nt(a, b):
    return lax.dot_general(a, b, (((1,), (1,)), ((), ())), preferred_element_type=f32)

def nn(a, b):
    return jnp.dot(a, b, preferred_element_type=f32)

def attn_fwd_kernel(info, tok, wqk, wv, wvt, cos, sin, seg, qh, ka, va, mixed, lse, vt, acc, top, *, docs, heads):
    seq = tok.shape[0]
    nt_ = seq // TILE
    lane = lax.broadcasted_iota(jnp.int32, (TILE, 128), 1)
    used = heads * HALF

    def project(c, _):
        rows = pl.ds(pl.multiple_of(c * TILE, TILE), TILE)
        x = tok[rows, :]
        p = nn(x, wqk[...])
        co, si = cos[rows, :], sin[rows, :]
        qa, qb, k_a, k_b = p[:, :128], p[:, 128:256], p[:, 256:384], p[:, 384:]
        hit = (lane - used) == seg[rows, :]
        aug = (lane >= used) & (lane < used + docs)
        ra = (qa * co - qb * si).astype(bf16).astype(f32) * 0.125
        rb = (qb * co + qa * si).astype(bf16).astype(f32) * 0.125
        for h in range(heads):
            keep = (lane >= HALF * h) & (lane < HALF * (h + 1))
            qh[h, rows, :128] = jnp.where(keep, ra, jnp.where(hit, -BIG, 0.0)).astype(bf16)
            qh[h, rows, 128:] = jnp.where(keep, rb, 0.0).astype(bf16)
        ka[rows, :128] = jnp.where(lane < used, k_a * co - k_b * si, jnp.where(aug & ~hit, 1.0, 0.0)).astype(bf16)
        ka[rows, 128:] = (k_b * co + k_a * si).astype(bf16)
        va[rows, :] = nn(x, wv[...]).astype(bf16)
        t = nt(wvt[...], x)
        r = lax.broadcasted_iota(jnp.int32, t.shape, 0)
        one = r == 64
        for h in range(1, heads):
            one = one | (r == 80 * h + 64)
        vt[:, rows] = jnp.where(one, 1.0, t).astype(bf16)
        return 0

    lax.fori_loop(0, nt_, project, 0)
    base = info[2 * nt_]

    def q_tile(c, _):
        a = lax.rem(c + base, nt_)
        lo, hi = info[a], info[nt_ + a]
        rows = pl.ds(pl.multiple_of(c * TILE, TILE), TILE)
        acc[...] = jnp.zeros_like(acc)
        top[...] = jnp.full_like(top, -3e38)

        def k_tile(t, _):
            cols = pl.ds(pl.multiple_of(lax.rem(t - base + nt_, nt_) * TILE, TILE), TILE)
            kk = ka[cols, :]
            for h in range(heads):
                s = nt(kk, qh[h, rows, :])
                old = top[h:h + 1, :]
                new = jnp.maximum(old, jnp.max(s, axis=0, keepdims=True))
                p = jnp.exp(s - new).astype(bf16)
                top[h:h + 1, :] = new
                acc[h] = acc[h] * jnp.exp(old - new) + nn(vt[80 * h:80 * h + 80, cols], p)
            return 0

        lax.fori_loop(lo, hi, k_tile, 0)
        live = hi > lo
        col = lax.broadcasted_iota(jnp.int32, (TILE, 1), 0)
        good = (seg[rows, :] < docs - 1) & live
        outs, stats = [], []
        for h in range(heads):
            total = jnp.where(live, acc[h, 64:65, :], 1.0)
            outs.append(acc[h, :64, :] / total)
            stats.append(top[h:h + 1, :] + jnp.log(total))
        o = jnp.concatenate(outs, axis=0).T
        mixed[rows, :] = jnp.where(good, o, 0.0).astype(bf16)
        lse[:, rows] = jnp.concatenate(stats + [jnp.zeros((8 - heads, TILE), f32)], axis=0)
        return 0

    lax.fori_loop(0, nt_, q_tile, 0)

def attn_fwd(info, tok, wqk, wv, wvt, cos, sin, seg, docs, heads):
    seq = tok.shape[0]
    vm = pl.BlockSpec(memory_space=pltpu.VMEM)
    return pl.pallas_call(
        functools.partial(attn_fwd_kernel, docs=docs, heads=heads),
        out_shape=(jax.ShapeDtypeStruct((heads, seq, 256), bf16), jax.ShapeDtypeStruct((seq, 256), bf16),
                   jax.ShapeDtypeStruct((seq, 64 * heads), bf16), jax.ShapeDtypeStruct((seq, 64 * heads), bf16),
                   jax.ShapeDtypeStruct((8, seq), f32)),
        in_specs=[pl.BlockSpec(memory_space=pltpu.SMEM)] + [vm] * 7,
        out_specs=(vm,) * 5,
        scratch_shapes=[pltpu.VMEM((80 * heads, seq), bf16), pltpu.VMEM((heads, 80, TILE), f32), pltpu.VMEM((8, TILE), f32)],
        compiler_params=pltpu.CompilerParams(vmem_limit_bytes=40 << 20),
        cost_estimate=pl.CostEstimate(flops=8 << 30, bytes_accessed=14 << 20, transcendentals=4 << 20),
        name="attn_fwd",
    )(info, tok, wqk, wv, wvt, cos, sin, seg)

def attn_bwd_kernel(info, qh, ka, va, mixed, do, lse, cos, sin, seg, out, doh, kt, dqt, delta, dk, dv, *, docs, heads):
    seq = ka.shape[0]
    nt_ = seq // TILE
    width = 64 * heads
    used = heads * HALF
    base = info[2 * nt_]
    ones = jnp.ones((8, width), f32)
    wlane = lax.broadcasted_iota(jnp.int32, (TILE, width), 1)
    lane = lax.broadcasted_iota(jnp.int32, (TILE, 128), 1)
    dqt[...] = jnp.zeros_like(dqt)

    def prepare(c, _):
        rows = pl.ds(pl.multiple_of(c * TILE, TILE), TILE)
        d = jnp.where(seg[rows, :] < docs - 1, do[rows, :].astype(f32), 0.0)
        o = mixed[rows, :].astype(f32)
        for h in range(heads):
            m = jnp.where((wlane >= 64 * h) & (wlane < 64 * h + 64), d, 0.0)
            doh[h, rows, :] = m.astype(bf16)
            delta[h:h + 1, rows] = lax.dot_general(ones, m * o, (((1,), (1,)), ((), ())), precision=lax.Precision.HIGHEST, preferred_element_type=f32)[:1]
        t = ka[rows, :].astype(f32).T
        for h in range(heads):
            kt[h, :, rows] = jnp.concatenate([t[HALF * h:HALF * h + HALF], t[128 + HALF * h:128 + HALF * h + HALF]], axis=0).astype(bf16)
        return 0

    lax.fori_loop(0, nt_, prepare, 0)

    def unrotate(a, b, rows):
        a, b = a.astype(bf16).astype(f32), b.astype(bf16).astype(f32)
        co, si = cos[rows, :], sin[rows, :]
        keep = lane < used
        return (jnp.where(keep, a * co + b * si, 0.0).astype(bf16), jnp.where(keep, b * co - a * si, 0.0).astype(bf16))

    def k_tile(c, _):
        t = lax.rem(c + base, nt_)
        rows = pl.ds(pl.multiple_of(c * TILE, TILE), TILE)
        dk[...] = jnp.zeros_like(dk)
        dv[...] = jnp.zeros_like(dv)
        kk, vv = ka[rows, :], va[rows, :]

        def q_tile(u, _):
            cols = pl.ds(pl.multiple_of(lax.rem(u - base + nt_, nt_) * TILE, TILE), TILE)
            for h in range(heads):
                q, d = qh[h, cols, :], doh[h, cols, :]
                p = jnp.exp(nt(kk, q) - lse[h:h + 1, cols])
                ds = (p * (nt(vv, d) - delta[h:h + 1, cols])).astype(bf16)
                dv[...] += nn(p.astype(bf16), d)
                dk[...] += nn(ds, q)
                g = nn(kt[h, :, rows], ds)
                dqt[HALF * h:HALF * h + HALF, cols] += g[:HALF]
                dqt[128 + HALF * h:128 + HALF * h + HALF, cols] += g[HALF:]
            return 0

        lax.fori_loop(info[t], info[nt_ + t], q_tile, 0)
        a, b = unrotate(dk[:, :128], dk[:, 128:], rows)
        out[rows, 256:384] = a
        out[rows, 384:512] = b
        out[rows, 512:512 + width] = dv[...].astype(bf16)
        out[rows, 512 + width:] = jnp.zeros((TILE, 256 - width), bf16)
        return 0

    lax.fori_loop(0, nt_, k_tile, 0)

    def finish(c, _):
        rows = pl.ds(pl.multiple_of(c * TILE, TILE), TILE)
        g = dqt[:, rows].T * 0.125
        a, b = unrotate(g[:, :128], g[:, 128:], rows)
        out[rows, :128] = a
        out[rows, 128:256] = b
        return 0

    lax.fori_loop(0, nt_, finish, 0)

def attn_bwd(info, qh, ka, va, mixed, do, lse, cos, sin, seg, docs):
    heads, seq = qh.shape[:2]
    width = 64 * heads
    vm = pl.BlockSpec(memory_space=pltpu.VMEM)
    return pl.pallas_call(
        functools.partial(attn_bwd_kernel, docs=docs, heads=heads),
        out_shape=jax.ShapeDtypeStruct((seq, 768), bf16),
        in_specs=[pl.BlockSpec(memory_space=pltpu.SMEM)] + [vm] * 9,
        out_specs=vm,
        scratch_shapes=[pltpu.VMEM((heads, seq, width), bf16), pltpu.VMEM((heads, 64, seq), bf16), pltpu.VMEM((256, seq), f32),
                        pltpu.VMEM((8, seq), f32), pltpu.VMEM((TILE, 256), f32), pltpu.VMEM((TILE, width), f32)],
        compiler_params=pltpu.CompilerParams(vmem_limit_bytes=40 << 20),
        cost_estimate=pl.CostEstimate(flops=16 << 30, bytes_accessed=14 << 20, transcendentals=4 << 20),
        name="attn_bwd",
    )(info, qh, ka, va, mixed, do, lse, cos, sin, seg)

def doc_tables(lengths, seq, base_row):
    docs = lengths.shape[0]
    ends = jnp.cumsum(lengths)
    starts = ends - lengths
    place = lax.rem(jnp.arange(seq, dtype=jnp.int32) + base_row, seq)
    segment = jnp.sum((place[:, None] >= ends[None, :]).astype(jnp.int32), axis=1)
    member = segment[:, None] == jnp.arange(docs, dtype=jnp.int32)[None, :]
    offset = jnp.sum(jnp.where(member, starts[None, :], 0), axis=1)
    position = (place - offset).astype(f32)
    n = seq // TILE
    first = jnp.arange(n, dtype=jnp.int32) * TILE
    live = ends[docs - 2]
    last = jnp.minimum(first + TILE, live) - 1
    lo = jnp.max(jnp.where(starts[None, :] <= first[:, None], starts[None, :], 0), axis=1)
    hi = jnp.min(jnp.where(ends[None, :] > last[:, None], ends[None, :], seq), axis=1)
    lo = lo // TILE
    hi = (jnp.minimum(hi, live) + TILE - 1) // TILE
    hi = jnp.where(first < live, hi, lo)
    info = jnp.concatenate([lo, hi, jnp.reshape(base_row // TILE, (1,))]).astype(jnp.int32)
    return segment, position, info

HD = 64
EPSILON = 1e-05
ROPE_BASE = 1000.0


def rotate_axis(size, step):
    return [(i, (i + step) % size) for i in range(size)]


def flip_axis(size, bit):
    return [(i, i ^ bit) for i in range(size)]


def norm_forward(values, scale_vec, shift_vec):
    centered = values - jnp.mean(values, axis=-1, keepdims=True)
    inv_std = lax.rsqrt(jnp.mean(centered * centered, axis=-1, keepdims=True) + EPSILON)
    unit_rows = centered * inv_std
    return (unit_rows * scale_vec + shift_vec, unit_rows, inv_std)


def norm_backward(upstream, unit_rows, inv_std, scale_vec):
    scaled = upstream * scale_vec
    result = inv_std * (
        scaled
        - jnp.mean(scaled, axis=-1, keepdims=True)
        - unit_rows * jnp.mean(scaled * unit_rows, axis=-1, keepdims=True)
    )
    return (result, jnp.sum(upstream * unit_rows, axis=0), jnp.sum(upstream, axis=0))


def tn(left, right):
    return lax.dot_general(left, right, (((0,), (0,)), ((), ())), preferred_element_type=f32)


def take(array, index, axis):
    return lax.dynamic_index_in_dim(array, index, axis, keepdims=False)


def reduce_over_dp(parts, me, size):
    bits = size.bit_length() - 1
    blocks, rows, cols = parts.shape[1:]
    if bits == 0:
        return parts[0]
    view = parts.reshape(size // 2, 2, blocks, rows, cols)
    mine = me & 1
    got = lax.ppermute(take(view, 1 - mine, 1), "dp", flip_axis(size, 1))
    kept = (take(view, mine, 1).astype(f32) + got.astype(f32)).astype(bf16)
    kept = kept.reshape((2,) * (bits - 1) + (blocks, rows, cols))
    half = blocks // 2 if blocks > 1 else 0
    pieces = []
    if half:
        todo = [(kept[..., :half, :, :], False), (kept[..., half:, :, :], True)]
    else:
        todo = [(kept[..., : rows // 2, :], False), (kept[..., rows // 2 :, :], True)]
    for piece, low_first in todo:
        left = list(range(bits - 1, 0, -1))
        order = list(range(1, bits)) if not low_first else list(range(bits - 1, 0, -1))
        for bit in order:
            axis = left.index(bit)
            left.remove(bit)
            own = (me >> bit) & 1
            got = lax.ppermute(take(piece, 1 - own, axis), "dp", flip_axis(size, 1 << bit))
            piece = (take(piece, own, axis).astype(f32) + got.astype(f32)).astype(bf16)
        pieces.append(piece)
    return jnp.concatenate(pieces, axis=0 if half else 1)


def reduce_over_tensor(parts, z, size):
    total = take(parts, z, 0).astype(f32)
    for step in range(1, size):
        sent = take(parts, lax.rem(z + step, size), 0)
        total = total + lax.ppermute(sent, "tensor", rotate_axis(size, step)).astype(f32)
    return total


def body(
    dp_size,
    tp_size,
    tokens,
    lengths,
    w_qkv,
    w_out,
    norm1_scale,
    norm1_shift,
    w_gate_up,
    w_down,
    norm2_scale,
    norm2_shift,
    cotangent,
):
    own = tokens[0]
    rows_here, width = own.shape
    docs = lengths.shape[1]
    seq = rows_here * tp_size
    cols_here = w_qkv.shape[2]
    heads = cols_here // HD
    units = w_gate_up.shape[2]
    share = units // dp_size
    me = lax.axis_index("dp")
    z = lax.axis_index("tensor")

    gate_slice = lax.dynamic_slice_in_dim(w_gate_up, me * share, share, 2)
    down_slice = lax.dynamic_slice_in_dim(w_down, me * share, share, 0)
    out_slice = lax.dynamic_slice_in_dim(w_out, me * (width // dp_size), width // dp_size, 1)
    piece = jnp.concatenate([gate_slice[:, 0].T, gate_slice[:, 1].T, down_slice, out_slice.T], axis=1)
    weights = lax.all_gather(piece, ("dp", "tensor"), axis=0, tiled=True)

    slots = [own]
    for step in range(1, tp_size):
        slots.append(lax.ppermute(own, "tensor", rotate_axis(tp_size, -step)))
    row_tokens = jnp.concatenate(slots, axis=0)

    segment, position, info = doc_tables(lengths[0], seq, z * rows_here)
    inverse = ROPE_BASE ** (-2.0 * jnp.arange(HALF, dtype=f32) / HD)
    angles = position[:, None] * inverse[None, :]
    cosine, sine = jnp.tile(jnp.cos(angles), (1, 4)), jnp.tile(jnp.sin(angles), (1, 4))
    seg_col = segment[:, None]

    def rope_order(matrix):
        halves = matrix.reshape(width, heads, 2, HALF).transpose(0, 2, 1, 3).reshape(width, 2, heads * HALF)
        return jnp.pad(halves, ((0, 0), (0, 0), (0, 128 - heads * HALF))).reshape(width, 256)

    w_qk = jnp.concatenate([rope_order(w_qkv[:, 0]), rope_order(w_qkv[:, 1])], axis=1)
    w_v = w_qkv[:, 2]
    w_vt = jnp.pad(w_v.T.reshape(heads, HD, width), ((0, 0), (0, 16), (0, 0))).reshape(heads * 80, width)
    w_all = jnp.concatenate([w_qk, jnp.pad(w_v, ((0, 0), (0, 256 - cols_here)))], axis=1)

    qh, ka, va, mixed, lse = attn_fwd(info, row_tokens, w_qk, w_v, w_vt, cosine, sine, seg_col, docs, heads)

    mixed_slots = mixed.reshape(tp_size, rows_here, cols_here)
    mixed_rel = [mixed_slots[0]]
    for step in range(1, tp_size):
        mixed_rel.append(lax.ppermute(mixed_slots[step], "tensor", rotate_axis(tp_size, step)))
    mixed_here = jnp.concatenate(mixed_rel, axis=1)

    out_abs = weights[:, 3 * width :].reshape(dp_size, tp_size, width // dp_size, cols_here)
    out_abs = out_abs.transpose(1, 3, 0, 2).reshape(tp_size, cols_here, width)
    out_rel = jnp.concatenate([take(out_abs, lax.rem(z - s + tp_size, tp_size), 0) for s in range(tp_size)], axis=0)
    branch = jnp.dot(mixed_here, out_rel, preferred_element_type=f32)
    normed, unit_one, inv_one = norm_forward(own.astype(f32) + branch, norm1_scale, norm1_shift)
    normed_low = normed.astype(bf16)

    w_gate, w_up, w_dn = weights[:, :width], weights[:, width : 2 * width], weights[:, 2 * width : 3 * width]
    gate = nt(normed_low, w_gate)
    up = nt(normed_low, w_up)
    sigma = jax.nn.sigmoid(gate)
    active = (gate * sigma * up).astype(bf16)
    feed = nn(active, w_dn)
    result, unit_two, inv_two = norm_forward(normed + feed, norm2_scale, norm2_shift)
    layer_out = result.astype(bf16)[None]
    upstream = cotangent[0].astype(f32)
    grad_two, scale2_grad, shift2_grad = norm_backward(upstream, unit_two, inv_two, norm2_scale)
    feed_low = grad_two.astype(bf16)
    down_grad = tn(active, feed_low).astype(bf16)
    active_grad = nt(feed_low, w_dn)
    gate_grad = (active_grad * up * sigma * (1.0 + gate * (1.0 - sigma))).astype(bf16)
    up_grad = (active_grad * gate * sigma).astype(bf16)
    gate_w_grad = tn(gate_grad, normed_low).astype(bf16)
    up_w_grad = tn(up_grad, normed_low).astype(bf16)
    normed_grad = nn(gate_grad, w_gate) + nn(up_grad, w_up) + grad_two
    grad_one, scale1_grad, shift1_grad = norm_backward(normed_grad, unit_one, inv_one, norm1_scale)
    branch_low = grad_one.astype(bf16)

    small = jnp.concatenate([scale1_grad, shift1_grad, scale2_grad, shift2_grad])
    small_high = small.astype(bf16)
    small_low = (small - small_high.astype(f32)).astype(bf16)
    small_rows = jnp.concatenate([small_high, small_low]).reshape(-1, cols_here)
    mixed_grad = nt(branch_low, out_rel).astype(bf16)
    back = [mixed_grad[:, :cols_here]]
    small_sum = small
    count = small.shape[0]
    for step in range(1, tp_size):
        block = (tp_size - step) % tp_size
        sent = jnp.concatenate([mixed_grad[:, block * cols_here : (block + 1) * cols_here], small_rows], axis=0)
        got = lax.ppermute(sent, "tensor", rotate_axis(tp_size, step))
        back.append(got[:rows_here])
        extra = got[rows_here:].reshape(-1).astype(f32)
        small_sum = small_sum + (extra[:count] + extra[count:])
    mixed_back = jnp.concatenate([back[(tp_size - s) % tp_size] for s in range(tp_size)], axis=0)

    out_grads = tn(branch_low, mixed_here).astype(bf16).reshape(width, tp_size, cols_here)
    out_grads = jnp.stack([take(out_grads, lax.rem(z - t + tp_size, tp_size), 1) for t in range(tp_size)], axis=0)
    out_grads = out_grads.reshape(tp_size, dp_size, width // dp_size, cols_here).transpose(1, 0, 2, 3)

    shape4 = (dp_size, tp_size, share)
    group_one = jnp.concatenate([down_grad.reshape(shape4 + (width,)), out_grads], axis=-1)
    group_two = jnp.concatenate([gate_w_grad.reshape(shape4 + (width,)), up_w_grad.reshape(shape4 + (width,))], axis=-1)
    share_one = reduce_over_tensor(reduce_over_dp(group_one, me, dp_size), z, tp_size).astype(bf16)
    share_two = reduce_over_tensor(reduce_over_dp(group_two, me, dp_size), z, tp_size).astype(bf16)

    dqkv = attn_bwd(info, qh, ka, va, mixed, mixed_back, lse, cosine, sine, seg_col, docs)
    qkv_grad = tn(row_tokens, dqkv).astype(bf16)
    rows_share = width // dp_size
    small_share = small_sum.reshape(dp_size, 1, 1, count // dp_size)
    small_share = jnp.pad(small_share.astype(bf16), ((0, 0), (0, 0), (0, 15), (0, width - count // dp_size)))
    group_three = jnp.concatenate([qkv_grad.reshape(dp_size, 1, rows_share, width), small_share], axis=2)
    share_three = reduce_over_dp(group_three, me, dp_size)[0]

    input_part = nt(dqkv, w_all).astype(bf16).reshape(tp_size, rows_here, width)
    input_grad = grad_one + input_part[0].astype(f32)
    for step in range(1, tp_size):
        input_grad = input_grad + lax.ppermute(input_part[step], "tensor", rotate_axis(tp_size, step)).astype(f32)

    final = jnp.concatenate([share_one, share_two, share_three[:rows_share]], axis=1)
    final = jnp.concatenate([final, jnp.pad(share_three[rows_share:], ((0, 0), (0, final.shape[1] - width)))], axis=0)
    final = lax.all_gather(final, "dp", axis=0, tiled=False)
    main = final[:, :share].reshape(units, -1).astype(f32)
    small_out = final[:, share, : count // dp_size].astype(f32).reshape(4, width)
    down_sum = main[:, :width]
    out_sum = main[:, width : width + cols_here].T
    start = width + cols_here
    gate_up_sum = jnp.stack([main[:, start : start + width].T, main[:, start + width : start + 2 * width].T], axis=1)
    q3 = main[:, start + 2 * width :]

    def rope_back(matrix):
        halves = matrix.reshape(width, 2, 128)[:, :, : heads * HALF].reshape(width, 2, heads, HALF)
        return halves.transpose(0, 2, 1, 3).reshape(width, cols_here)

    qkv_sum = jnp.stack([rope_back(q3[:, :256]), rope_back(q3[:, 256:512]), q3[:, 512 : 512 + cols_here]], axis=1)
    return (
        layer_out,
        input_grad[None],
        qkv_sum,
        out_sum,
        small_out[0],
        small_out[1],
        gate_up_sum,
        down_sum,
        small_out[2],
        small_out[3],
    )


def solution(mesh):
    in_specs = (
        P("dp", "tensor", None),
        P("dp", None),
        P(None, None, "tensor"),
        P("tensor", None),
        P(),
        P(),
        P(None, None, "tensor"),
        P("tensor", None),
        P(),
        P(),
        P("dp", "tensor", None),
    )
    out_specs = (
        P("dp", "tensor", None),
        P("dp", "tensor", None),
        P(None, None, "tensor"),
        P("tensor", None),
        P(),
        P(),
        P(None, None, "tensor"),
        P("tensor", None),
        P(),
        P(),
    )
    return jax.shard_map(
        functools.partial(body, mesh.shape["dp"], mesh.shape["tensor"]),
        mesh=mesh,
        in_specs=in_specs,
        out_specs=out_specs,
        check_vma=False,
    )
```

```python
import functools

import jax
import jax.numpy as jnp
from jax import lax
from jax.experimental import pallas as pl
from jax.experimental.pallas import tpu as pltpu
from jax.sharding import PartitionSpec as P

TILE = 256
HALF = 32
HD = 64
BIG = 1e30
f32, bf16 = jnp.float32, jnp.bfloat16


def nt(a, b):
    return lax.dot_general(a, b, (((1,), (1,)), ((), ())), preferred_element_type=f32)


def nn(a, b):
    return jnp.dot(a, b, preferred_element_type=f32)


def tile_rows(tile, base, count):
    return pl.ds(pl.multiple_of(lax.rem(tile - base + count, count) * TILE, TILE), TILE)


def attn_fwd_kernel(info, *refs, docs, heads, slots):
    toks = refs[:slots]
    w, cos, sin, seg, qh, ka, va, lse, mixed, tok, vt, acc, top = refs[slots:]
    here, width = toks[0].shape
    seq = here * slots
    count = seq // TILE
    used = heads * HALF
    cols = heads * HD
    lo, hi, base = info[0], info[1], info[2]

    @pl.when(pl.program_id(0) == 0)
    def _():
        for s in range(slots):
            tok[s * here : (s + 1) * here, :] = toks[s][...]
        r = lax.broadcasted_iota(jnp.int32, vt.shape, 0)
        one = r == HD
        for h in range(1, heads):
            one = one | (r == 80 * h + HD)
        vt[...] = jnp.where(one, 1.0, 0.0).astype(bf16)

    def weight(start, stop):
        return w[:, 0, :, start:stop].reshape(width, stop - start)

    lane = lax.broadcasted_iota(jnp.int32, (TILE, 128), 1)

    def queries(c, _):
        rows = pl.ds(pl.multiple_of(c * TILE, TILE), TILE)
        p = nn(tok[rows, :], weight(0, 256))
        co, si = cos[rows, :], sin[rows, :]
        hit = (lane - used) == seg[rows, :]
        ra = (p[:, :128] * co - p[:, 128:] * si).astype(bf16).astype(f32) * HD**-0.5
        rb = (p[:, 128:] * co + p[:, :128] * si).astype(bf16).astype(f32) * HD**-0.5
        for h in range(heads):
            keep = (lane >= HALF * h) & (lane < HALF * (h + 1))
            qh[0, h, rows, :128] = jnp.where(keep, ra, jnp.where(hit, -BIG, 0.0)).astype(bf16)
            qh[0, h, rows, 128:] = jnp.where(keep, rb, 0.0).astype(bf16)
        return 0

    lax.fori_loop(0, here // TILE, queries, 0)

    def keys(t, _):
        rows = tile_rows(t, base, count)
        x = tok[rows, :]
        p = nn(x, weight(256, 512))
        co, si = cos[rows, :], sin[rows, :]
        other = (lane >= used) & (lane < used + docs) & ((lane - used) != seg[rows, :])
        ra, rb = p[:, :128] * co - p[:, 128:] * si, p[:, 128:] * co + p[:, :128] * si
        ka[0, rows, :128] = jnp.where(lane < used, ra, jnp.where(other, 1.0, 0.0)).astype(bf16)
        ka[0, rows, 128:] = rb.astype(bf16)
        v = nn(x, weight(512 + cols, 512 + 2 * cols))
        va[0, rows, :] = v.astype(bf16)
        vtt = v.T.astype(bf16)
        for h in range(heads):
            vt[80 * h : 80 * h + HD, rows] = vtt[HD * h : HD * (h + 1), :]
        return 0

    lax.fori_loop(lo, hi, keys, 0)
    acc[...] = jnp.zeros_like(acc)
    top[...] = jnp.full_like(top, -3e38)

    def k_tile(t, _):
        rows = tile_rows(t, base, count)
        kk = ka[0, rows, :]
        for h in range(heads):
            s = nt(kk, qh[0, h])
            old = top[h : h + 1, :]
            new = jnp.maximum(old, jnp.max(s, axis=0, keepdims=True))
            p = jnp.exp(s - new).astype(bf16)
            top[h : h + 1, :] = new
            acc[h] = acc[h] * jnp.exp(old - new) + nn(vt[80 * h : 80 * h + 80, rows], p)
        return 0

    lax.fori_loop(lo, hi, k_tile, 0)
    good = seg[:here, :] < docs - 1
    total = [jnp.where(top[h : h + 1, :] > -1e29, acc[h, HD : HD + 1, :], 1.0) for h in range(heads)]
    outs = jnp.concatenate([acc[h, :HD, :] / total[h] for h in range(heads)], axis=0).T
    mixed[0] = jnp.where(good, outs, 0.0).astype(bf16)
    stats = [top[h : h + 1, :] + jnp.log(total[h]) for h in range(heads)]
    lse[0] = jnp.concatenate(stats + [jnp.zeros((8 - heads, here), f32)], axis=0)


def attn_fwd(info, toks, w, cos, sin, seg, docs, heads):
    slots = len(toks)
    here, width = toks[0].shape
    seq = here * slots
    cols = heads * HD

    def whole(shape):
        return pl.BlockSpec(shape, lambda g: (0,) * len(shape))

    def part(shape):
        return pl.BlockSpec((1,) + shape, lambda g: (g,) + (0,) * len(shape))

    shapes = [((heads, here, 256), bf16), ((seq, 256), bf16), ((seq, cols), bf16), ((8, here), f32), ((here, cols), bf16)]
    return pl.pallas_call(
        functools.partial(attn_fwd_kernel, docs=docs, heads=heads, slots=slots),
        grid=(slots,),
        out_shape=tuple(jax.ShapeDtypeStruct((slots,) + s, d) for s, d in shapes),
        in_specs=[pl.BlockSpec(memory_space=pltpu.SMEM)]
        + [whole((here, width))] * slots
        + [pl.BlockSpec((w.shape[0], 1) + w.shape[2:], lambda g: (0, g, 0, 0)), whole(cos.shape), whole(sin.shape), whole(seg.shape)],
        out_specs=tuple(part(s) for s, _ in shapes),
        scratch_shapes=[
            pltpu.VMEM((seq, width), bf16),
            pltpu.VMEM((80 * heads, seq), bf16),
            pltpu.VMEM((heads, 80, here), f32),
            pltpu.VMEM((8, here), f32),
        ],
        compiler_params=pltpu.CompilerParams(vmem_limit_bytes=50 << 20),
        cost_estimate=pl.CostEstimate(flops=20 << 30, bytes_accessed=20 << 20, transcendentals=4 << 20),
        name="attn_fwd",
    )(info, *toks, w, cos, sin, seg)


def attn_bwd_kernel(info, *refs, docs, heads, slots, pieces):
    toks = refs[:slots]
    w, cos, sin, seg, qh, ka, va, lse, mixed, do = refs[slots : slots + 10]
    dw, dx_out = refs[slots + 10], refs[slots + 11 : 2 * slots + 11]
    tokt, dx, dqt, dwa, doh, delta = refs[2 * slots + 11 :]
    here, width = toks[0].shape
    seq = here * slots
    count = seq // TILE
    used = heads * HALF
    cols = heads * HD
    lo, hi, base, me = info[0], info[1], info[2], info[3]

    @pl.when(pl.program_id(0) == 0)
    def _():
        dx[...] = jnp.zeros_like(dx)
        for s in range(slots):
            for c in range(here // TILE):
                start = s * here + c * TILE
                tokt[:, start : start + TILE] = toks[s][c * TILE : (c + 1) * TILE, :].astype(f32).T.astype(bf16)

    def weight(start, stop):
        return w[:, 0, :, start:stop].reshape(width, stop - start)

    wlane = lax.broadcasted_iota(jnp.int32, (here, cols), 1)
    lane = lax.broadcasted_iota(jnp.int32, (TILE, 128), 1)
    ones = jnp.ones((8, cols), f32)
    dqt[...] = jnp.zeros_like(dqt)
    dwa[...] = jnp.zeros_like(dwa)
    d = jnp.where(seg[:here, :] < docs - 1, do[0].astype(f32), 0.0)
    o = mixed[0].astype(f32)
    for h in range(heads):
        m = jnp.where((wlane >= HD * h) & (wlane < HD * (h + 1)), d, 0.0)
        doh[h] = m.astype(bf16)
        sums = lax.dot_general(ones, m * o, (((1,), (1,)), ((), ())), precision=lax.Precision.HIGHEST, preferred_element_type=f32)
        delta[h : h + 1, :] = sums[:1]

    def unrotate(a, b, rows):
        a, b = a.astype(bf16).astype(f32), b.astype(bf16).astype(f32)
        co, si = cos[rows, :], sin[rows, :]
        keep = lane < used
        both = [jnp.where(keep, a * co + b * si, 0.0), jnp.where(keep, b * co - a * si, 0.0)]
        return jnp.concatenate(both, axis=1).astype(bf16)

    def k_tile(t, _):
        rows = tile_rows(t, base, count)
        kk, vv = ka[0, rows, :], va[0, rows, :]
        kt = kk.astype(f32).T.astype(bf16)
        dk = jnp.zeros((TILE, 256), f32)
        dv = jnp.zeros((TILE, cols), f32)
        for h in range(heads):
            q, dd = qh[0, h], doh[h]
            p = jnp.exp(nt(kk, q) - lse[0, h : h + 1, :])
            ds = (p * (nt(vv, dd) - delta[h : h + 1, :])).astype(bf16)
            dv = dv + nn(p.astype(bf16), dd)
            dk = dk + nn(ds, q)
            kth = jnp.concatenate([kt[HALF * h : HALF * (h + 1)], kt[128 + HALF * h : 128 + HALF * (h + 1)]], axis=0)
            g = nn(kth, ds)
            dqt[HALF * h : HALF * (h + 1), :] += g[:HALF]
            dqt[128 + HALF * h : 128 + HALF * (h + 1), :] += g[HALF:]
        dkl = unrotate(dk[:, :128], dk[:, 128:], rows)
        dvl = dv.astype(bf16)
        dx[rows, :] += nt(dkl, weight(256, 512)) + nt(dvl, weight(512 + cols, 512 + 2 * cols))
        dwa[:, 256:512] += nn(tokt[:, rows], dkl)
        dwa[:, 512 : 512 + cols] += nn(tokt[:, rows], dvl)
        return 0

    lax.fori_loop(lo, hi, k_tile, 0)
    for c in range(here // TILE):
        rows = slice(c * TILE, (c + 1) * TILE)
        g = dqt[:, rows].T * HD**-0.5
        dql = unrotate(g[:, :128], g[:, 128:], rows)
        dx[rows, :] += nt(dql, weight(0, 256))
        dwa[:, :256] += nn(tokt[:, rows], dql)
    share = width // pieces
    for r in range(pieces):
        p = jnp.bitwise_xor(me, r)
        dw[r, 0] = dwa[pl.ds(pl.multiple_of(p * share, 8), share), :].astype(bf16)

    @pl.when(pl.program_id(0) == slots - 1)
    def _():
        for s in range(slots):
            dx_out[s][...] = dx[s * here : (s + 1) * here, :].astype(dx_out[s].dtype)


def attn_bwd(info, toks, w, cos, sin, seg, saved, do, docs, heads, pieces):
    slots = len(toks)
    here, width = toks[0].shape
    seq = here * slots
    cols = heads * HD
    span = -(-(512 + cols) // 128) * 128

    def whole(shape):
        return pl.BlockSpec(shape, lambda g: (0,) * len(shape))

    def part(array):
        return pl.BlockSpec((1,) + array.shape[1:], lambda g: (g,) + (0,) * (array.ndim - 1))

    return pl.pallas_call(
        functools.partial(attn_bwd_kernel, docs=docs, heads=heads, slots=slots, pieces=pieces),
        grid=(slots,),
        out_shape=(jax.ShapeDtypeStruct((pieces, slots, width // pieces, span), bf16), jax.ShapeDtypeStruct((here, width), f32))
        + (jax.ShapeDtypeStruct((here, width), bf16),) * (slots - 1),
        in_specs=[pl.BlockSpec(memory_space=pltpu.SMEM)]
        + [whole((here, width))] * slots
        + [pl.BlockSpec((w.shape[0], 1) + w.shape[2:], lambda g: (0, g, 0, 0)), whole(cos.shape), whole(sin.shape), whole(seg.shape)]
        + [part(a) for a in (*saved, do)],
        out_specs=(pl.BlockSpec((pieces, 1, width // pieces, span), lambda g: (0, g, 0, 0)),) + (whole((here, width)),) * slots,
        scratch_shapes=[
            pltpu.VMEM((width, seq), bf16),
            pltpu.VMEM((seq, width), f32),
            pltpu.VMEM((256, here), f32),
            pltpu.VMEM((width, span), f32),
            pltpu.VMEM((heads, here, cols), bf16),
            pltpu.VMEM((8, here), f32),
        ],
        compiler_params=pltpu.CompilerParams(vmem_limit_bytes=56 << 20),
        cost_estimate=pl.CostEstimate(flops=40 << 30, bytes_accessed=24 << 20, transcendentals=4 << 20),
        name="attn_bwd",
    )(info, *toks, w, cos, sin, seg, *saved, do)


def doc_tables(lengths, seq, first, here):
    docs = lengths.shape[0]
    ends = jnp.cumsum(lengths)
    starts = ends - lengths
    place = lax.rem(jnp.arange(seq, dtype=jnp.int32) + first, seq)
    segment = jnp.sum((place[:, None] >= ends[None, :]).astype(jnp.int32), axis=1)
    member = segment[:, None] == jnp.arange(docs, dtype=jnp.int32)[None, :]
    offset = jnp.sum(jnp.where(member, starts[None, :], 0), axis=1)
    position = (place - offset).astype(f32)
    live = ends[docs - 2]
    last = jnp.minimum(first + here, live) - 1
    lo = jnp.max(jnp.where(starts <= first, starts, 0))
    hi = jnp.minimum(jnp.min(jnp.where(ends > last, ends, seq)), live)
    lo = lo // TILE
    hi = jnp.where(first < live, (hi + TILE - 1) // TILE, lo)
    return segment, position, lo, hi, first // TILE


EPSILON = 1e-05
ROWS = 256


def tn(left, right):
    return lax.dot_general(left, right, (((0,), (0,)), ((), ())), preferred_element_type=f32)


def row_mean(values):
    return jnp.mean(values, axis=-1, keepdims=True)


def normalise(values):
    centered = values - row_mean(values)
    inv = lax.rsqrt(row_mean(centered * centered) + EPSILON)
    return centered * inv, inv


def norm_back(upstream, unit, inv, scale):
    scaled = upstream * scale
    return inv * (scaled - row_mean(scaled) - unit * row_mean(scaled * unit))


def ffn_kernel(*refs, slots, pieces, share):
    own, cot, s1, b1, s2, b2, rel, w1_hbm, wown_hbm, w2_hbm = refs[:10]
    layer_out, grad_one, nlow, flow, brt, back, small, act_hbm, gg_hbm, ug_hbm = refs[10:20]
    w, wo, ws, g, u, normed, unit1, inv1, acc, stage, wsem, psem, osem, ssem = refs[20:]
    tokens, width = own.shape
    heads_cols = rel.shape[2]
    blk = slots * share
    rows_share = width // pieces

    def load_own(p):
        return pltpu.make_async_copy(wown_hbm.at[p], w.at[p, pl.ds(0, share)], psem.at[p])

    def load(p):
        return pltpu.make_async_copy(w2_hbm.at[p], w.at[p, pl.ds(share, blk - share)], wsem.at[p])

    first = pltpu.make_async_copy(w1_hbm.at[:, :, :, pl.ds(512, wo.shape[3])], wo, osem)
    first.start()
    for p in range(pieces):
        load_own(p).start()
        load(p).start()
    first.wait()
    for s in range(slots):
        for p in range(pieces):
            ws[s, p * rows_share : (p + 1) * rows_share, :] = wo[p, s, :, :heads_cols]
    small[...] = jnp.zeros_like(small)

    def head(c, _):
        rows = pl.ds(pl.multiple_of(c * ROWS, ROWS), ROWS)
        h = own[rows, :].astype(f32)
        for s in range(slots):
            h = h + nt(rel[s, rows, :], ws[s])
        unit, inv = normalise(h)
        n = unit * s1[...] + b1[...]
        unit1[rows, :] = unit
        inv1[rows, :] = inv
        normed[rows, :] = n
        nlow[rows, :] = n.astype(bf16)
        acc[rows, :] = n
        return 0

    lax.fori_loop(0, tokens // ROWS, head, 0)

    def out_copy(which, target, p, slot):
        return pltpu.make_async_copy(stage.at[which, slot], target.at[:, pl.ds(pl.multiple_of(p * blk, 128), blk)], ssem.at[which, slot])

    def forward(p, _):
        slot = lax.rem(p, 2)
        cols = pl.ds(pl.multiple_of(p * blk, 128), blk)
        load_own(p).wait()
        load(p).wait()

        @pl.when(p >= 2)
        def _():
            out_copy(0, act_hbm, p - 2, slot).wait()

        x = nlow[...]
        gp = nt(x, w[p, :, :width])
        up = nt(x, w[p, :, width : 2 * width])
        g[:, cols] = gp
        u[:, cols] = up
        a = (gp * jax.nn.sigmoid(gp) * up).astype(bf16)
        stage[0, slot] = a
        out_copy(0, act_hbm, p, slot).start()
        acc[...] += nn(a, w[p, :, 2 * width :])
        return 0

    lax.fori_loop(0, pieces, forward, 0)

    def middle(c, _):
        rows = pl.ds(pl.multiple_of(c * ROWS, ROWS), ROWS)
        unit, inv = normalise(acc[rows, :])
        layer_out[rows, :] = (unit * s2[...] + b2[...]).astype(bf16)
        up = cot[rows, :].astype(f32)
        d = norm_back(up, unit, inv, s2[...])
        small[2:3, :] += jnp.sum(up * unit, axis=0, keepdims=True)
        small[3:4, :] += jnp.sum(up, axis=0, keepdims=True)
        flow[rows, :] = d.astype(bf16)
        acc[rows, :] = d
        return 0

    lax.fori_loop(0, tokens // ROWS, middle, 0)
    for p in range(max(pieces - 2, 0), pieces):
        out_copy(0, act_hbm, p, p % 2).wait()

    def backward(p, _):
        slot = lax.rem(p, 2)
        cols = pl.ds(pl.multiple_of(p * blk, 128), blk)

        @pl.when(p >= 2)
        def _():
            out_copy(0, gg_hbm, p - 2, slot).wait()
            out_copy(1, ug_hbm, p - 2, slot).wait()

        da = nt(flow[...], w[p, :, 2 * width :])
        gp, up = g[:, cols], u[:, cols]
        sig = jax.nn.sigmoid(gp)
        dg = (da * up * sig * (1.0 + gp * (1.0 - sig))).astype(bf16)
        du = (da * gp * sig).astype(bf16)
        stage[0, slot] = dg
        stage[1, slot] = du
        out_copy(0, gg_hbm, p, slot).start()
        out_copy(1, ug_hbm, p, slot).start()
        acc[...] += nn(dg, w[p, :, :width]) + nn(du, w[p, :, width : 2 * width])
        return 0

    lax.fori_loop(0, pieces, backward, 0)

    def tail(c, _):
        rows = pl.ds(pl.multiple_of(c * ROWS, ROWS), ROWS)
        up, unit = acc[rows, :], unit1[rows, :]
        d = norm_back(up, unit, inv1[rows, :], s1[...])
        small[0:1, :] += jnp.sum(up * unit, axis=0, keepdims=True)
        small[1:2, :] += jnp.sum(up, axis=0, keepdims=True)
        grad_one[rows, :] = d
        low = d.astype(bf16)
        brt[:, rows] = d.T.astype(bf16)
        for s in range(slots):
            back[s, rows, :] = nn(low, ws[s]).astype(bf16)
        return 0

    lax.fori_loop(0, tokens // ROWS, tail, 0)
    for p in range(max(pieces - 2, 0), pieces):
        out_copy(0, gg_hbm, p, p % 2).wait()
        out_copy(1, ug_hbm, p, p % 2).wait()


def ffn_layer(own, cot, norms, rel, w1, w_own, w2):
    slots, tokens, cols = rel.shape
    width = own.shape[1]
    pieces, share = w_own.shape[:2]
    units = pieces * slots * share
    vm, hbm = pl.BlockSpec(memory_space=pltpu.VMEM), pl.BlockSpec(memory_space=pl.ANY)
    wide = jax.ShapeDtypeStruct((tokens, width), bf16)
    hidden = jax.ShapeDtypeStruct((tokens, units), bf16)
    return pl.pallas_call(
        functools.partial(ffn_kernel, slots=slots, pieces=pieces, share=share),
        out_shape=(wide, jax.ShapeDtypeStruct((tokens, width), f32), wide, wide, jax.ShapeDtypeStruct((width, tokens), bf16))
        + (jax.ShapeDtypeStruct((slots, tokens, cols), bf16), jax.ShapeDtypeStruct((8, width), f32), hidden, hidden, hidden),
        in_specs=[vm] * 7 + [hbm] * 3,
        out_specs=(vm,) * 7 + (hbm,) * 3,
        scratch_shapes=[
            pltpu.VMEM((pieces, slots * share, 3 * width), bf16),
            pltpu.VMEM((pieces, slots, width // pieces, 256), bf16),
            pltpu.VMEM((slots, width, cols), bf16),
            pltpu.VMEM((tokens, units), f32),
            pltpu.VMEM((tokens, units), f32),
            pltpu.VMEM((tokens, width), f32),
            pltpu.VMEM((tokens, width), f32),
            pltpu.VMEM((tokens, 1), f32),
            pltpu.VMEM((tokens, width), f32),
            pltpu.VMEM((2, 2, tokens, slots * share), bf16),
            pltpu.SemaphoreType.DMA((pieces,)),
            pltpu.SemaphoreType.DMA((pieces,)),
            pltpu.SemaphoreType.DMA,
            pltpu.SemaphoreType.DMA((2, 2)),
        ],
        compiler_params=pltpu.CompilerParams(vmem_limit_bytes=60 << 20),
        cost_estimate=pl.CostEstimate(flops=16 << 30, bytes_accessed=30 << 20, transcendentals=3 << 20),
        name="ffn_layer",
    )(own, cot, *norms, rel, w1, w_own, w2)


def wgrad_kernel(*refs, slots, share, add):
    gg, ug, act, brt, nlow, flow, rel, small = refs[1:9]
    got = refs[9] if add else None
    out = refs[-1]
    width = nlow.shape[1]
    cols = rel.shape[2]
    edge = 3 * width + cols
    room = out.shape[2] - edge

    def put(rows, lanes, value):
        if add:
            value = value + got[0, rows, lanes].astype(f32)
        out[0, rows, lanes] = value.astype(bf16)

    every = slice(0, out.shape[1])
    put(every, slice(0, width), tn(gg[...], nlow[...]))
    put(every, slice(width, 2 * width), tn(ug[...], nlow[...]))
    put(every, slice(2 * width, 3 * width), tn(act[...], flow[...]))
    for s in range(slots):
        put(slice(s * share, (s + 1) * share), slice(3 * width, edge), nn(brt[...], rel[s]))
        put(slice(s * share, (s + 1) * share), slice(edge, edge + room), jnp.concatenate([small[0], jnp.zeros((share - 16, room), f32)], axis=0))


def wgrad(me, first, count, gg, ug, act, brt, nlow, flow, rel, small, got, pieces, share, span):
    slots = rel.shape[0]
    tokens, width = nlow.shape
    blk = slots * share

    def piece(i, me):
        return jnp.bitwise_xor(2 * i + first, me[0])

    out_block = pl.BlockSpec((1, blk, span), lambda i, me: (i, 0, 0))
    in_specs = [pl.BlockSpec((tokens, blk), lambda i, me: (0, piece(i, me)))] * 3
    in_specs += [pl.BlockSpec((width // pieces, tokens), lambda i, me: (piece(i, me), 0))]
    in_specs += [pl.BlockSpec((tokens, width), lambda i, me: (0, 0))] * 2
    in_specs += [pl.BlockSpec(rel.shape, lambda i, me: (0, 0, 0)), pl.BlockSpec((1,) + small.shape[1:], lambda i, me: (piece(i, me), 0, 0))]
    args = [gg, ug, act, brt, nlow, flow, rel, small]
    if got is not None:
        in_specs.append(out_block)
        args.append(got)
    return pl.pallas_call(
        functools.partial(wgrad_kernel, slots=slots, share=share, add=got is not None),
        out_shape=jax.ShapeDtypeStruct((count, blk, span), bf16),
        grid_spec=pltpu.PrefetchScalarGridSpec(num_scalar_prefetch=1, grid=(count,), in_specs=in_specs, out_specs=out_block),
        compiler_params=pltpu.CompilerParams(vmem_limit_bytes=40 << 20),
        cost_estimate=pl.CostEstimate(flops=count << 30, bytes_accessed=count * 5 << 20, transcendentals=0),
        name="wgrad",
    )(me, *args)


ROPE_BASE = 1000.0


def rotate_axis(size, step):
    return [(i, (i + step) % size) for i in range(size)]


def line_axis(size, step):
    return [(i, i + step) for i in range(size) if 0 <= i + step < size]


def flip_axis(size, bit):
    return [(i, i ^ bit) for i in range(size)]


def after(value, *others):
    return lax.optimization_barrier((value, *others))[0]


def low_sum(left, right):
    return (left.astype(f32) + right.astype(f32)).astype(bf16)


def body(
    dp_size,
    tp_size,
    tokens,
    lengths,
    w_qkv,
    w_out,
    norm1_scale,
    norm1_shift,
    w_gate_up,
    w_down,
    norm2_scale,
    norm2_shift,
    cotangent,
):
    own = tokens[0]
    rows_here, width = own.shape
    docs = lengths.shape[1]
    seq = rows_here * tp_size
    cols_here = w_qkv.shape[2]
    heads = cols_here // HD
    units = w_gate_up.shape[2]
    pieces = min(dp_size, 8)
    groups = None if pieces == dp_size else [list(range(i, i + pieces)) for i in range(0, dp_size, pieces)]
    share = units // pieces
    rows_share = width // pieces
    span = -(-(3 * width + cols_here) // 128) * 128
    me = lax.rem(lax.axis_index("dp"), pieces)
    z = lax.axis_index("tensor")

    def flip(array, bit):
        return lax.ppermute(array, "dp", flip_axis(dp_size, bit))

    def shift(array, step):
        return lax.ppermute(array, "tensor", rotate_axis(tp_size, step))

    def along(array, step):
        return lax.ppermute(array, "tensor", line_axis(tp_size, step))

    def gather_dp(array):
        return lax.all_gather(array, "dp", axis=0, axis_index_groups=groups)

    def rope_order(matrix):
        halves = matrix.reshape(rows_share, heads, 2, HALF).transpose(0, 2, 1, 3).reshape(rows_share, 2, heads * HALF)
        return jnp.pad(halves, ((0, 0), (0, 0), (0, 128 - heads * HALF))).reshape(rows_share, 256)

    qkv_slice = lax.dynamic_slice_in_dim(w_qkv, me * rows_share, rows_share, 0)
    out_slice = lax.dynamic_slice_in_dim(w_out, me * rows_share, rows_share, 1)
    piece_one = jnp.concatenate([rope_order(qkv_slice[:, 0]), rope_order(qkv_slice[:, 1]), out_slice.T, qkv_slice[:, 2]], axis=1)
    gate_slice = lax.dynamic_slice_in_dim(w_gate_up, me * share, share, 2)
    down_slice = lax.dynamic_slice_in_dim(w_down, me * share, share, 0)
    piece_two = jnp.concatenate([gate_slice[:, 0].T, gate_slice[:, 1].T, down_slice], axis=1)
    piece_one, piece_two = lax.optimization_barrier((piece_one, piece_two))
    ones = [piece_one] + [shift(piece_one, s) for s in range(1, tp_size)]
    piece_two = after(piece_two, *ones[1:])
    twos = [shift(piece_two, s) for s in range(1, tp_size)]
    w1 = gather_dp(jnp.stack(ones))
    w2 = gather_dp(jnp.concatenate(twos, axis=0))

    own_late = after(own, *ones[1:])
    before, behind = along(own_late, 1), along(own_late, -1)
    before2, behind2 = along(before, 1), along(behind, -1)
    toks = [own, behind, jnp.where(z < tp_size // 2, behind2, before2), before]

    row_lengths, gate_up_late, down_late = after(lengths[0], ones[-1]), after(w_gate_up, ones[-1]), after(w_down, ones[-1])
    w_own = jnp.concatenate([gate_up_late[:, 0].T, gate_up_late[:, 1].T, down_late], axis=1).reshape(pieces, share, 3 * width)

    segment, position, lo, hi, base = doc_tables(row_lengths, seq, z * rows_here, rows_here)
    info = jnp.stack([lo, hi, base, me]).astype(jnp.int32)
    inverse = ROPE_BASE ** (-2.0 * lax.rem(jnp.arange(128), HALF).astype(f32) / HD)
    angles = position[:, None] * inverse[None, :]
    cosine, sine = jnp.cos(angles), jnp.sin(angles)
    seg_col = segment[:, None]

    saved = attn_fwd(info, toks, w1, cosine, sine, seg_col, docs, heads)
    rel = saved[4]
    norms = [v.reshape(1, width) for v in (norm1_scale, norm1_shift, norm2_scale, norm2_shift)]
    layer_out, grad_one, nlow, flow, brt, back, small, act, gg, ug = ffn_layer(own, cotangent[0], norms, rel, w1, w_own, w2)

    half = tp_size // 2

    def meet(one, two, bit):
        return low_sum(one, flip(two, bit))

    def reduce_slots(parts):
        total = parts[0].astype(f32)
        for s in range(1, tp_size):
            total = total + shift(parts[s], -s).astype(f32)
        return total.astype(bf16)

    me_array = me.reshape(1).astype(jnp.int32)
    room = span - 3 * width - cols_here
    chunk = small[:4].reshape(pieces, 4 * width // pieces // room, room)
    chunk = jnp.pad(chunk, ((0, 0), (0, 16 - chunk.shape[1]), (0, 0)))
    fixed = (gg, ug, act, brt, nlow, flow, rel, chunk)
    far_sent = wgrad(me_array, 5, 2, *fixed, None, pieces, share, span)
    near_sent = wgrad(after(me_array, far_sent), 1, 2, *fixed, None, pieces, share, span)
    far = wgrad(after(me_array, near_sent), 4, 2, *fixed, flip(far_sent, 1), pieces, share, span)
    near = wgrad(after(me_array, far), 0, 2, *fixed, flip(near_sent, 1), pieces, share, span)
    far, near = (v.reshape(2, tp_size, share, span) for v in (far, near))
    far_a, far_b, near_a, near_b = far[:, :half], far[:, half:], near[:, :half], near[:, half:]
    out_b, out_a = far_b, jnp.stack([near_a[1], far_a[1]])

    back, out_a, out_b = lax.optimization_barrier((back, out_a, out_b))
    next_b = meet(near_b, out_b, 4)
    next_a = meet(jnp.stack([near_a[0], far_a[0]]), out_a, 2)
    bwd = attn_bwd(info, toks, w1, cosine, sine, seg_col, saved, back, docs, heads, pieces)
    dw, dx = bwd[0], bwd[1:]
    right, left = along(dx[1], 1), along(dx[3], -1)
    across_half = lax.ppermute(dx[2], "tensor", rotate_axis(tp_size, half))
    input_grad = grad_one + dx[0] + right.astype(f32) + left.astype(f32) + across_half.astype(f32)

    last_b = meet(next_b[0], next_b[1], 2)
    last_a = meet(next_a[0], next_a[1], 4)
    last_a, last_b, right, left, across_half = lax.optimization_barrier((last_a, last_b, right, left, across_half))
    share_two = reduce_slots([last_a[i] for i in range(half)] + [last_b[i] for i in range(tp_size - half)])

    pairs = dw.reshape((pieces // 2, 2) + dw.shape[1:])
    pairs = meet(pairs[:, 0], pairs[:, 1], 1).reshape((2, 2) + dw.shape[1:])
    next_a = meet(pairs[:, 0, :half], pairs[:, 1, :half], 2)
    next_b = meet(pairs[0, :, half:], pairs[1, :, half:], 4)
    last_a, last_b = meet(next_a[0], next_a[1], 4), meet(next_b[0], next_b[1], 2)
    last_a, last_b, share_two = lax.optimization_barrier((last_a, last_b, share_two))
    share_one = reduce_slots([last_a[i] for i in range(half)] + [last_b[i] for i in range(tp_size - half)])

    def finish(array):
        if groups is not None:
            across = [[g * pieces + i for g in range(dp_size // pieces)] for i in range(pieces)]
            array = lax.psum(array.astype(f32), "dp", axis_index_groups=across).astype(bf16)
        return gather_dp(array)

    main = finish(share_two).reshape(units, span).astype(f32)
    down_sum = main[:, 2 * width : 3 * width]
    out_sum = main[:, 3 * width : 3 * width + cols_here].T
    gate_up_sum = jnp.stack([main[:, :width].T, main[:, width : 2 * width].T], axis=1)
    q3 = finish(share_one).reshape(width, -1).astype(f32)

    def rope_back(matrix):
        halves = matrix.reshape(width, 2, 128)[:, :, : heads * HALF].reshape(width, 2, heads, HALF)
        return halves.transpose(0, 2, 1, 3).reshape(width, cols_here)

    qkv_sum = jnp.stack([rope_back(q3[:, :256]), rope_back(q3[:, 256:512]), q3[:, 512 : 512 + cols_here]], axis=1)
    small_out = main.reshape(pieces, share, span)[:, : 4 * width // pieces // room, span - room :].reshape(4, width)
    return (
        layer_out[None],
        input_grad[None],
        qkv_sum,
        out_sum,
        small_out[0],
        small_out[1],
        gate_up_sum,
        down_sum,
        small_out[2],
        small_out[3],
    )


def solution(mesh):
    in_specs = (
        P("dp", "tensor", None),
        P("dp", None),
        P(None, None, "tensor"),
        P("tensor", None),
        P(),
        P(),
        P(None, None, "tensor"),
        P("tensor", None),
        P(),
        P(),
        P("dp", "tensor", None),
    )
    out_specs = (
        P("dp", "tensor", None),
        P("dp", "tensor", None),
        P(None, None, "tensor"),
        P("tensor", None),
        P(),
        P(),
        P(None, None, "tensor"),
        P("tensor", None),
        P(),
        P(),
    )
    return jax.shard_map(
        functools.partial(body, mesh.shape["dp"], mesh.shape["tensor"]),
        mesh=mesh,
        in_specs=in_specs,
        out_specs=out_specs,
        check_vma=False,
    )
```

```python
import functools

import jax
import jax.numpy as jnp
from jax import lax
from jax.experimental import pallas as pl
from jax.experimental.pallas import tpu as pltpu
from jax.sharding import PartitionSpec as P

TILE = 256
HALF = 32
HD = 64
BIG = 1e30
f32, bf16 = jnp.float32, jnp.bfloat16


def nt(a, b):
    return lax.dot_general(a, b, (((1,), (1,)), ((), ())), preferred_element_type=f32)


def nn(a, b):
    return jnp.dot(a, b, preferred_element_type=f32)


def tile_rows(tile, base, count):
    return pl.ds(pl.multiple_of(lax.rem(tile - base + count, count) * TILE, TILE), TILE)


def over_tiles(info, lo, hi, tiles, scan):
    def one(t, _):
        live = [(t >= info[3 + u]) & (t < info[3 + tiles + u]) for u in range(tiles)]
        every = functools.reduce(jnp.logical_and, live)

        @pl.when(every)
        def _():
            scan(t, slice(0, tiles * TILE))

        @pl.when(jnp.logical_not(every))
        def _():
            def single(u, _):
                @pl.when((t >= info[3 + u]) & (t < info[3 + tiles + u]))
                def _():
                    scan(t, pl.ds(pl.multiple_of(u * TILE, TILE), TILE))

                return 0

            lax.fori_loop(0, tiles, single, 0)

        return 0

    lax.fori_loop(lo, hi, one, 0)


def attn_fwd_kernel(info, *refs, docs, heads, slots):
    toks = refs[:slots]
    w, cos, sin, seg, qh, ka, va, lse, mixed, tok, vt, acc, top = refs[slots:]
    here, width = toks[0].shape
    seq = here * slots
    count = seq // TILE
    used = heads * HALF
    cols = heads * HD
    lo, hi, base = info[0], info[1], info[2]
    tiles = here // TILE

    @pl.when(pl.program_id(0) == 0)
    def _():
        for s in range(slots):
            tok[s * here : (s + 1) * here, :] = toks[s][...]
        r = lax.broadcasted_iota(jnp.int32, vt.shape, 0)
        one = r == HD
        for h in range(1, heads):
            one = one | (r == 80 * h + HD)
        vt[...] = jnp.where(one, 1.0, 0.0).astype(bf16)

    def weight(start, stop):
        return w[:, 0, :, start:stop].reshape(width, stop - start)

    lane = lax.broadcasted_iota(jnp.int32, (TILE, 128), 1)

    def queries(c, _):
        rows = pl.ds(pl.multiple_of(c * TILE, TILE), TILE)
        p = nn(tok[rows, :], weight(0, 256))
        co, si = cos[rows, :], sin[rows, :]
        hit = (lane - used) == seg[rows, :]
        ra = (p[:, :128] * co - p[:, 128:] * si).astype(bf16).astype(f32) * HD**-0.5
        rb = (p[:, 128:] * co + p[:, :128] * si).astype(bf16).astype(f32) * HD**-0.5
        for h in range(heads):
            keep = (lane >= HALF * h) & (lane < HALF * (h + 1))
            qh[0, h, rows, :128] = jnp.where(keep, ra, jnp.where(hit, -BIG, 0.0)).astype(bf16)
            qh[0, h, rows, 128:] = jnp.where(keep, rb, 0.0).astype(bf16)
        return 0

    lax.fori_loop(0, here // TILE, queries, 0)

    def keys(t, _):
        rows = tile_rows(t, base, count)
        x = tok[rows, :]
        p = nn(x, weight(256, 512))
        co, si = cos[rows, :], sin[rows, :]
        other = (lane >= used) & (lane < used + docs) & ((lane - used) != seg[rows, :])
        ra, rb = p[:, :128] * co - p[:, 128:] * si, p[:, 128:] * co + p[:, :128] * si
        ka[0, rows, :128] = jnp.where(lane < used, ra, jnp.where(other, 1.0, 0.0)).astype(bf16)
        ka[0, rows, 128:] = rb.astype(bf16)
        v = nn(x, weight(512 + cols, 512 + 2 * cols))
        va[0, rows, :] = v.astype(bf16)
        vtt = v.T.astype(bf16)
        for h in range(heads):
            vt[80 * h : 80 * h + HD, rows] = vtt[HD * h : HD * (h + 1), :]
        return 0

    lax.fori_loop(lo, hi, keys, 0)
    acc[...] = jnp.zeros_like(acc)
    top[...] = jnp.full_like(top, -3e38)

    def scan(t, mine):
        rows = tile_rows(t, base, count)
        kk = ka[0, rows, :]
        scores = [nt(kk, qh[0, h, mine, :]) for h in range(heads)]
        olds = [top[h : h + 1, mine] for h in range(heads)]
        news = [jnp.maximum(olds[h], jnp.max(scores[h], axis=0, keepdims=True)) for h in range(heads)]
        probs = [jnp.exp(scores[h] - news[h]).astype(bf16) for h in range(heads)]
        adds = [nn(vt[80 * h : 80 * h + 80, rows], probs[h]) for h in range(heads)]
        for h in range(heads):
            top[h : h + 1, mine] = news[h]
            acc[h, :, mine] = acc[h, :, mine] * jnp.exp(olds[h] - news[h]) + adds[h]

    over_tiles(info, lo, hi, tiles, scan)
    good = seg[:here, :] < docs - 1
    total = [jnp.where(top[h : h + 1, :] > -1e29, acc[h, HD : HD + 1, :], 1.0) for h in range(heads)]
    outs = jnp.concatenate([acc[h, :HD, :] / total[h] for h in range(heads)], axis=0).T
    mixed[0] = jnp.where(good, outs, 0.0).astype(bf16)
    stats = [top[h : h + 1, :] + jnp.log(total[h]) for h in range(heads)]
    lse[0] = jnp.concatenate(stats + [jnp.zeros((8 - heads, here), f32)], axis=0)


def attn_fwd(info, toks, w, cos, sin, seg, docs, heads):
    slots = len(toks)
    here, width = toks[0].shape
    seq = here * slots
    cols = heads * HD

    def whole(shape):
        return pl.BlockSpec(shape, lambda g: (0,) * len(shape))

    def part(shape):
        return pl.BlockSpec((1,) + shape, lambda g: (g,) + (0,) * len(shape))

    shapes = [((heads, here, 256), bf16), ((seq, 256), bf16), ((seq, cols), bf16), ((8, here), f32), ((here, cols), bf16)]
    return pl.pallas_call(
        functools.partial(attn_fwd_kernel, docs=docs, heads=heads, slots=slots),
        grid=(slots,),
        out_shape=tuple(jax.ShapeDtypeStruct((slots,) + s, d) for s, d in shapes),
        in_specs=[pl.BlockSpec(memory_space=pltpu.SMEM)]
        + [whole((here, width))] * slots
        + [pl.BlockSpec((w.shape[0], 1) + w.shape[2:], lambda g: (0, g, 0, 0)), whole(cos.shape), whole(sin.shape), whole(seg.shape)],
        out_specs=tuple(part(s) for s, _ in shapes),
        scratch_shapes=[
            pltpu.VMEM((seq, width), bf16),
            pltpu.VMEM((80 * heads, seq), bf16),
            pltpu.VMEM((heads, 80, here), f32),
            pltpu.VMEM((8, here), f32),
        ],
        compiler_params=pltpu.CompilerParams(vmem_limit_bytes=50 << 20),
        cost_estimate=pl.CostEstimate(flops=20 << 30, bytes_accessed=20 << 20, transcendentals=4 << 20),
        name="attn_fwd",
    )(info, *toks, w, cos, sin, seg)


def attn_bwd_kernel(info, *refs, docs, heads, slots, pieces):
    toks = refs[:slots]
    w, cos, sin, seg, qh, ka, va, lse, mixed, do = refs[slots : slots + 10]
    dw, dx_out = refs[slots + 10], refs[slots + 11 : 2 * slots + 11]
    tokt, dkv, dq, dqt, dwa, doh, delta, dka, dva = refs[2 * slots + 11 :]
    here, width = toks[0].shape
    seq = here * slots
    count = seq // TILE
    used = heads * HALF
    cols = heads * HD
    tiles = here // TILE
    lo, hi, base, me = info[0], info[1], info[2], info[3 + 2 * tiles]

    @pl.when(pl.program_id(0) == 0)
    def _():
        dkv[...] = jnp.zeros_like(dkv)
        dwa[:, 512 + cols :] = jnp.zeros((width, dwa.shape[1] - 512 - cols), f32)
        for s in range(slots):
            for c in range(here // TILE):
                start = s * here + c * TILE
                tokt[:, start : start + TILE] = toks[s][c * TILE : (c + 1) * TILE, :].astype(f32).T.astype(bf16)

    g = pl.program_id(0)

    def weight(group, start, stop):
        return w[:, group, :, start:stop].reshape(width, stop - start)

    wlane = lax.broadcasted_iota(jnp.int32, (here, cols), 1)
    lane = lax.broadcasted_iota(jnp.int32, (TILE, 128), 1)
    dqt[...] = jnp.zeros_like(dqt)
    d = jnp.where(seg[:here, :] < docs - 1, do[0].astype(f32), 0.0)
    prod = d * mixed[0].astype(f32)
    prod_high = prod.astype(bf16)
    prod_low = (prod - prod_high.astype(f32)).astype(bf16)
    pick = (lax.broadcasted_iota(jnp.int32, (8, cols), 1) // HD == lax.broadcasted_iota(jnp.int32, (8, cols), 0)).astype(bf16)
    delta[...] = nt(pick, prod_high) + nt(pick, prod_low)
    for h in range(heads):
        doh[h] = jnp.where((wlane >= HD * h) & (wlane < HD * (h + 1)), d, 0.0).astype(bf16)

    def unrotate(a, b, rows):
        a, b = a.astype(bf16).astype(f32), b.astype(bf16).astype(f32)
        co, si = cos[rows, :], sin[rows, :]
        keep = lane < used
        both = [jnp.where(keep, a * co + b * si, 0.0), jnp.where(keep, b * co - a * si, 0.0)]
        return jnp.concatenate(both, axis=1).astype(bf16)

    def scan(t, mine):
        rows = tile_rows(t, base, count)
        kk, vv = ka[0, rows, :], va[0, rows, :]
        kt = kk.astype(f32).T.astype(bf16)
        qs, dd = [qh[0, h, mine, :] for h in range(heads)], [doh[h, mine, :] for h in range(heads)]
        probs = [jnp.exp(nt(kk, qs[h]) - lse[0, h : h + 1, mine]) for h in range(heads)]
        ds = [(probs[h] * (nt(vv, dd[h]) - delta[h : h + 1, mine])).astype(bf16) for h in range(heads)]
        dva[...] += sum(nn(probs[h].astype(bf16), dd[h]) for h in range(heads))
        dka[...] += sum(nn(ds[h], qs[h]) for h in range(heads))
        for h in range(heads):
            kth = jnp.concatenate([kt[HALF * h : HALF * (h + 1)], kt[128 + HALF * h : 128 + HALF * (h + 1)]], axis=0)
            g = nn(kth, ds[h])
            dqt[HALF * h : HALF * (h + 1), mine] += g[:HALF]
            dqt[128 + HALF * h : 128 + HALF * (h + 1), mine] += g[HALF:]

    def k_tile(t, _):
        rows = tile_rows(t, base, count)
        dka[...] = jnp.zeros_like(dka)
        dva[...] = jnp.zeros_like(dva)
        over_tiles(info, t, t + 1, tiles, scan)
        dkv[g, rows, :256] = unrotate(dka[:, :128], dka[:, 128:], rows)
        dkv[g, rows, 256:] = dva[...].astype(bf16)
        return 0

    lax.fori_loop(lo, hi, k_tile, 0)
    for c in range(here // TILE):
        rows = slice(c * TILE, (c + 1) * TILE)
        gq = dqt[:, rows].T * HD**-0.5
        dq[g, rows, :] = unrotate(gq[:, :128], gq[:, 128:], rows)
    dwa[:, :256] = nn(tokt[:, :here], dq[g])
    dwa[:, 256 : 512 + cols] = nn(tokt[...], dkv[g])
    share = width // pieces
    for r in range(pieces):
        p = jnp.bitwise_xor(me, r)
        dw[r, 0] = dwa[pl.ds(pl.multiple_of(p * share, 8), share), :].astype(bf16)

    @pl.when(g == slots - 1)
    def _():
        for s in range(slots):
            dx_out[s][...] = jnp.zeros_like(dx_out[s])
        for s in range(slots):
            begin = lax.rem(base + s * tiles, count)

            @pl.when((begin + tiles > lo) & (begin < hi))
            def _(s=s):
                rows = slice(s * here, (s + 1) * here)
                total = sum(
                    nt(dkv[group, rows, :256], weight(group, 256, 512)) + nt(dkv[group, rows, 256:], weight(group, 512 + cols, 512 + 2 * cols))
                    for group in range(slots)
                )
                if s == 0:
                    total = total + sum(nt(dq[group], weight(group, 0, 256)) for group in range(slots))
                dx_out[s][...] = total.astype(dx_out[s].dtype)


def attn_bwd(info, toks, w, cos, sin, seg, saved, do, docs, heads, pieces):
    slots = len(toks)
    here, width = toks[0].shape
    seq = here * slots
    cols = heads * HD
    span = -(-(512 + cols) // 128) * 128

    def whole(shape):
        return pl.BlockSpec(shape, lambda g: (0,) * len(shape))

    def part(array):
        return pl.BlockSpec((1,) + array.shape[1:], lambda g: (g,) + (0,) * (array.ndim - 1))

    return pl.pallas_call(
        functools.partial(attn_bwd_kernel, docs=docs, heads=heads, slots=slots, pieces=pieces),
        grid=(slots,),
        out_shape=(jax.ShapeDtypeStruct((pieces, slots, width // pieces, span), bf16), jax.ShapeDtypeStruct((here, width), f32))
        + (jax.ShapeDtypeStruct((here, width), bf16),) * (slots - 1),
        in_specs=[pl.BlockSpec(memory_space=pltpu.SMEM)]
        + [whole((here, width))] * slots
        + [whole(w.shape), whole(cos.shape), whole(sin.shape), whole(seg.shape)]
        + [part(a) for a in (*saved, do)],
        out_specs=(pl.BlockSpec((pieces, 1, width // pieces, span), lambda g: (0, g, 0, 0)),) + (whole((here, width)),) * slots,
        scratch_shapes=[
            pltpu.VMEM((width, seq), bf16),
            pltpu.VMEM((slots, seq, 256 + cols), bf16),
            pltpu.VMEM((slots, here, 256), bf16),
            pltpu.VMEM((256, here), f32),
            pltpu.VMEM((width, span), f32),
            pltpu.VMEM((heads, here, cols), bf16),
            pltpu.VMEM((8, here), f32),
            pltpu.VMEM((TILE, 256), f32),
            pltpu.VMEM((TILE, cols), f32),
        ],
        compiler_params=pltpu.CompilerParams(vmem_limit_bytes=56 << 20),
        cost_estimate=pl.CostEstimate(flops=40 << 30, bytes_accessed=24 << 20, transcendentals=4 << 20),
        name="attn_bwd",
    )(info, *toks, w, cos, sin, seg, *saved, do)


def doc_tables(lengths, seq, first, here):
    docs = lengths.shape[0]
    ends = jnp.cumsum(lengths)
    starts = ends - lengths
    place = lax.rem(jnp.arange(seq, dtype=jnp.int32) + first, seq)
    segment = jnp.sum((place[:, None] >= ends[None, :]).astype(jnp.int32), axis=1)
    member = segment[:, None] == jnp.arange(docs, dtype=jnp.int32)[None, :]
    offset = jnp.sum(jnp.where(member, starts[None, :], 0), axis=1)
    position = (place - offset).astype(f32)
    live = ends[docs - 2]
    tops = first + TILE * jnp.arange(here // TILE, dtype=jnp.int32)
    last = jnp.minimum(tops + TILE, live) - 1
    lo = jnp.max(jnp.where(starts[None, :] <= tops[:, None], starts[None, :], 0), axis=1) // TILE
    hi = jnp.minimum(jnp.min(jnp.where(ends[None, :] > last[:, None], ends[None, :], seq), axis=1), live)
    hi = jnp.where(tops < live, (hi + TILE - 1) // TILE, lo)
    span = [jnp.min(jnp.where(hi > lo, lo, seq), keepdims=True), jnp.max(jnp.where(hi > lo, hi, 0), keepdims=True)]
    return segment, position, jnp.concatenate([*span, jnp.reshape(first // TILE, (1,)), lo, hi])


def make_info(tables, me):
    return jnp.concatenate([tables[2], jnp.reshape(me, (1,))]).astype(jnp.int32)


EPSILON = 1e-05
ROWS = 256


def tn(left, right):
    return lax.dot_general(left, right, (((0,), (0,)), ((), ())), preferred_element_type=f32)


def row_mean(values):
    return jnp.mean(values, axis=-1, keepdims=True)


def normalise(values):
    centered = values - row_mean(values)
    inv = lax.rsqrt(row_mean(centered * centered) + EPSILON)
    return centered * inv, inv


def norm_back(upstream, unit, inv, scale):
    scaled = upstream * scale
    return inv * (scaled - row_mean(scaled) - unit * row_mean(scaled * unit))


def ffn_kernel(*refs, slots, pieces, share):
    own, cot, s1, b1, s2, b2, rel, w1_hbm, wown_hbm, w2_hbm = refs[:10]
    layer_out, grad_one, nlow, flow, brt, back, chunk, act_hbm, gg_hbm, ug_hbm = refs[10:20]
    w, wo, ws, g, u, normed, unit1, inv1, acc, small, stage, wsem, psem, osem, ssem = refs[20:]
    tokens, width = own.shape
    heads_cols = rel.shape[2]
    blk = slots * share
    pair = 2 if pieces % 2 == 0 else 1
    steps, wide = pieces // pair, pair * blk
    rows_share = width // pieces

    def load_own(p):
        return pltpu.make_async_copy(wown_hbm.at[p], w.at[p // pair, pl.ds(p % pair * blk, share)], psem.at[p])

    def load(p):
        return pltpu.make_async_copy(w2_hbm.at[p], w.at[p // pair, pl.ds(p % pair * blk + share, blk - share)], wsem.at[p])

    first = pltpu.make_async_copy(w1_hbm.at[:, :, :, pl.ds(512, wo.shape[3])], wo, osem)
    first.start()
    for p in range(pieces):
        load_own(p).start()
        load(p).start()
    first.wait()
    for s in range(slots):
        for p in range(pieces):
            ws[s, p * rows_share : (p + 1) * rows_share, :] = wo[p, s, :, :heads_cols]
    small[...] = jnp.zeros_like(small)

    def head(c, _):
        rows = pl.ds(pl.multiple_of(c * ROWS, ROWS), ROWS)
        h = own[rows, :].astype(f32)
        for s in range(slots):
            h = h + nt(rel[s, rows, :], ws[s])
        unit, inv = normalise(h)
        n = unit * s1[...] + b1[...]
        unit1[rows, :] = unit
        inv1[rows, :] = inv
        normed[rows, :] = n
        nlow[rows, :] = n.astype(bf16)
        acc[rows, :] = n
        return 0

    lax.fori_loop(0, tokens // ROWS, head, 0)

    def out_copy(which, target, p, slot):
        return pltpu.make_async_copy(stage.at[which, slot], target.at[:, pl.ds(pl.multiple_of(p * wide, 128), wide)], ssem.at[which, slot])

    def forward(p, _):
        slot = lax.rem(p, 2)
        cols = pl.ds(pl.multiple_of(p * wide, 128), wide)
        for i in range(pair):
            load_own(p * pair + i).wait()
            load(p * pair + i).wait()

        @pl.when(p >= 2)
        def _():
            out_copy(0, act_hbm, p - 2, slot).wait()

        halves = [slice(i, i + tokens // 2) for i in range(0, tokens, tokens // 2)]
        gates = [nt(nlow[r, :], w[p, :, :width]) for r in halves]
        ups = [nt(nlow[r, :], w[p, :, width : 2 * width]) for r in halves]
        for r, gp, up in zip(halves, gates, ups):
            g[r, cols] = gp
            u[r, cols] = up
            a = (gp * jax.nn.sigmoid(gp) * up).astype(bf16)
            stage[0, slot, r, :] = a
            acc[r, :] += nn(a, w[p, :, 2 * width :])
        out_copy(0, act_hbm, p, slot).start()
        return 0

    lax.fori_loop(0, steps, forward, 0)

    def middle(c, _):
        rows = pl.ds(pl.multiple_of(c * ROWS, ROWS), ROWS)
        unit, inv = normalise(acc[rows, :])
        layer_out[rows, :] = (unit * s2[...] + b2[...]).astype(bf16)
        up = cot[rows, :].astype(f32)
        d = norm_back(up, unit, inv, s2[...])
        small[2:3, :] += jnp.sum(up * unit, axis=0, keepdims=True)
        small[3:4, :] += jnp.sum(up, axis=0, keepdims=True)
        flow[rows, :] = d.astype(bf16)
        acc[rows, :] = d
        return 0

    lax.fori_loop(0, tokens // ROWS, middle, 0)
    for p in range(max(steps - 2, 0), steps):
        out_copy(0, act_hbm, p, p % 2).wait()

    def backward(p, _):
        slot = lax.rem(p, 2)
        cols = pl.ds(pl.multiple_of(p * wide, 128), wide)

        @pl.when(p >= 2)
        def _():
            out_copy(0, gg_hbm, p - 2, slot).wait()
            out_copy(1, ug_hbm, p - 2, slot).wait()

        halves = [slice(i, i + tokens // 2) for i in range(0, tokens, tokens // 2)]
        outer = [nt(flow[r, :], w[p, :, 2 * width :]) for r in halves]
        for r, da in zip(halves, outer):
            gp, up = g[r, cols], u[r, cols]
            sig = jax.nn.sigmoid(gp)
            both = da * sig
            dg = (both * up * (1.0 + gp * (1.0 - sig))).astype(bf16)
            du = (both * gp).astype(bf16)
            stage[0, slot, r, :] = dg
            stage[1, slot, r, :] = du
            acc[r, :] += nn(dg, w[p, :, :width]) + nn(du, w[p, :, width : 2 * width])
        out_copy(0, gg_hbm, p, slot).start()
        out_copy(1, ug_hbm, p, slot).start()
        return 0

    lax.fori_loop(0, steps, backward, 0)

    def tail(c, _):
        rows = pl.ds(pl.multiple_of(c * ROWS, ROWS), ROWS)
        up, unit = acc[rows, :], unit1[rows, :]
        d = norm_back(up, unit, inv1[rows, :], s1[...])
        small[0:1, :] += jnp.sum(up * unit, axis=0, keepdims=True)
        small[1:2, :] += jnp.sum(up, axis=0, keepdims=True)
        grad_one[rows, :] = d
        low = d.astype(bf16)
        brt[:, rows] = d.T.astype(bf16)
        for s in range(slots):
            back[s, rows, :] = nn(low, ws[s]).astype(bf16)
        return 0

    lax.fori_loop(0, tokens // ROWS, tail, 0)
    chunk[...] = jnp.zeros_like(chunk)
    room = chunk.shape[2]
    each = 4 * width // pieces // room
    for n in range(pieces * each):
        j, lane = divmod(n * room, width)
        chunk[n // each, n % each : n % each + 1, :] = small[j : j + 1, lane : lane + room]
    for p in range(max(steps - 2, 0), steps):
        out_copy(0, gg_hbm, p, p % 2).wait()
        out_copy(1, ug_hbm, p, p % 2).wait()


def ffn_layer(own, cot, norms, rel, w1, w_own, w2, room):
    slots, tokens, cols = rel.shape
    width = own.shape[1]
    pieces, share = w_own.shape[:2]
    units = pieces * slots * share
    pair = 2 if pieces % 2 == 0 else 1
    vm, hbm = pl.BlockSpec(memory_space=pltpu.VMEM), pl.BlockSpec(memory_space=pl.ANY)
    wide = jax.ShapeDtypeStruct((tokens, width), bf16)
    hidden = jax.ShapeDtypeStruct((tokens, units), bf16)
    return pl.pallas_call(
        functools.partial(ffn_kernel, slots=slots, pieces=pieces, share=share),
        out_shape=(wide, jax.ShapeDtypeStruct((tokens, width), f32), wide, wide, jax.ShapeDtypeStruct((width, tokens), bf16))
        + (jax.ShapeDtypeStruct((slots, tokens, cols), bf16), jax.ShapeDtypeStruct((pieces, 16, room), f32), hidden, hidden, hidden),
        in_specs=[vm] * 7 + [hbm] * 3,
        out_specs=(vm,) * 7 + (hbm,) * 3,
        scratch_shapes=[
            pltpu.VMEM((pieces // pair, pair * slots * share, 3 * width), bf16),
            pltpu.VMEM((pieces, slots, width // pieces, 256), bf16),
            pltpu.VMEM((slots, width, cols), bf16),
            pltpu.VMEM((tokens, units), f32),
            pltpu.VMEM((tokens, units), f32),
            pltpu.VMEM((tokens, width), f32),
            pltpu.VMEM((tokens, width), f32),
            pltpu.VMEM((tokens, 1), f32),
            pltpu.VMEM((tokens, width), f32),
            pltpu.VMEM((8, width), f32),
            pltpu.VMEM((2, 2, tokens, pair * slots * share), bf16),
            pltpu.SemaphoreType.DMA((pieces,)),
            pltpu.SemaphoreType.DMA((pieces,)),
            pltpu.SemaphoreType.DMA,
            pltpu.SemaphoreType.DMA((2, 2)),
        ],
        compiler_params=pltpu.CompilerParams(vmem_limit_bytes=60 << 20),
        cost_estimate=pl.CostEstimate(flops=16 << 30, bytes_accessed=30 << 20, transcendentals=3 << 20),
        name="ffn_layer",
    )(own, cot, *norms, rel, w1, w_own, w2)


def wgrad_kernel(*refs, slots, share, add):
    gg, ug, act, brt, nlow, flow, rel, small = refs[1:9]
    got = refs[9] if add else None
    width = nlow.shape[1]
    cols = rel.shape[2]
    edge = 3 * width + cols
    blk = slots * share
    out = refs[-1] if add else refs[-1].at[0]
    room = out.shape[1] - edge

    def put(rows, lanes, value):
        if add:
            value = value + got[0, rows, lanes].astype(f32)
        out[rows, lanes] = value.astype(bf16)

    terms = [tn(gg[...], nlow[...]), tn(ug[...], nlow[...]), tn(act[...], flow[...])]
    for s in range(slots):
        place = lax.rem(refs[0][1] - s + slots, slots)
        rows = pl.ds(pl.multiple_of(place * share, 32 if share % 32 == 0 else 4), share)
        for i in range(3):
            put(rows, slice(i * width, (i + 1) * width), terms[i][s * share : (s + 1) * share])
        put(rows, slice(3 * width, edge), nn(brt[...], rel[s]))
        put(rows, slice(edge, edge + room), jnp.concatenate([small[0], jnp.zeros((share - 16, room), f32)], axis=0))
    if add:
        first, second, rest = refs[10:13]
        top = first.shape[0]

        @pl.when(pl.program_id(0) == 0)
        def _():
            first[...] = out[:top, :]

        @pl.when(pl.program_id(0) == 1)
        def _():
            second[...] = out[:top, :]

        rest[0] = out[top:, :]


def wgrad(me, start, gg, ug, act, brt, nlow, flow, rel, small, got, pieces, share, span):
    slots = rel.shape[0]
    tokens, width = nlow.shape
    blk = slots * share
    top = slots // 2 * share

    def piece(i, me):
        return jnp.bitwise_xor(2 * i + start, me[0])

    def stay(array):
        return pltpu.with_memory_space_constraint(array, pltpu.HBM)

    both = pl.BlockSpec((1, blk, span), lambda i, me: (i, 0, 0))
    in_specs = [pl.BlockSpec((tokens, blk), lambda i, me: (0, piece(i, me)))] * 3
    in_specs += [pl.BlockSpec((width // pieces, tokens), lambda i, me: (piece(i, me), 0))]
    in_specs += [pl.BlockSpec((tokens, width), lambda i, me: (0, 0))] * 2
    in_specs += [pl.BlockSpec(rel.shape, lambda i, me: (0, 0, 0)), pl.BlockSpec((1,) + small.shape[1:], lambda i, me: (piece(i, me), 0, 0))]
    args = [stay(gg), stay(ug), stay(act), brt, nlow, flow, rel, small]
    if got is None:
        out_shape, out_specs, scratch = jax.ShapeDtypeStruct((2, blk, span), bf16), both, []
    else:
        in_specs.append(both)
        args.append(got)
        half = jax.ShapeDtypeStruct((top, span), bf16)
        out_shape = (half, half, jax.ShapeDtypeStruct((2, blk - top, span), bf16))
        fixed = pl.BlockSpec((top, span), lambda i, me: (0, 0))
        out_specs = (fixed, fixed, pl.BlockSpec((1, blk - top, span), lambda i, me: (i, 0, 0)))
        scratch = [pltpu.VMEM((blk, span), bf16)]
    return pl.pallas_call(
        functools.partial(wgrad_kernel, slots=slots, share=share, add=got is not None),
        out_shape=out_shape,
        grid_spec=pltpu.PrefetchScalarGridSpec(num_scalar_prefetch=1, grid=(2,), in_specs=in_specs, out_specs=out_specs, scratch_shapes=scratch),
        compiler_params=pltpu.CompilerParams(vmem_limit_bytes=40 << 20),
        cost_estimate=pl.CostEstimate(flops=2 << 30, bytes_accessed=10 << 20, transcendentals=0),
        name="wgrad",
    )(me, *args)


def final_ffn_kernel(gate, up, out):
    out[:, 0, :] = gate[...].astype(f32).T
    out[:, 1, :] = up[...].astype(f32).T


def final_ffn(main, width, lanes):
    units = main.shape[0]
    steps = width // lanes
    return pl.pallas_call(
        final_ffn_kernel,
        grid=(steps,),
        out_shape=jax.ShapeDtypeStruct((width, 2, units), f32),
        in_specs=[pl.BlockSpec((units, lanes), lambda i: (0, i)), pl.BlockSpec((units, lanes), lambda i: (0, i + steps))],
        out_specs=pl.BlockSpec((lanes, 2, units), lambda i: (i, 0, 0)),
        cost_estimate=pl.CostEstimate(flops=1 << 20, bytes_accessed=8 << 20, transcendentals=0),
        name="final_ffn",
    )(main, main)


def final_qkv_kernel(query, key, value, out, *, heads):
    cols = heads * HD
    for k, source in enumerate((query, key)):
        turned = source[...].astype(f32).T
        for h in range(heads):
            for half in range(2):
                start = 128 * half + HALF * h
                out[k, HD * h + HALF * half : HD * h + HALF * (half + 1), :] = turned[start : start + HALF, :]
    out[2, :, :] = value[...].astype(f32).T[:cols]


def final_qkv(main, start, heads, rows):
    width = main.shape[0]
    cols = heads * HD
    return pl.pallas_call(
        functools.partial(final_qkv_kernel, heads=heads),
        grid=(width // rows,),
        out_shape=jax.ShapeDtypeStruct((3, cols, width), f32),
        in_specs=[pl.BlockSpec((rows, 256), lambda i, k=k: (i, start // 256 + k)) for k in range(3)],
        out_specs=pl.BlockSpec((3, cols, rows), lambda i: (0, 0, i)),
        cost_estimate=pl.CostEstimate(flops=1 << 20, bytes_accessed=4 << 20, transcendentals=0),
        name="final_qkv",
    )(main, main, main)


ROPE_BASE = 1000.0


def rotate_axis(size, step):
    return [(i, (i + step) % size) for i in range(size)]


def line_axis(size, step):
    return [(i, i + step) for i in range(size) if 0 <= i + step < size]


def flip_axis(size, bit):
    return [(i, i ^ bit) for i in range(size)]


def after(value, *others):
    return lax.optimization_barrier((value, *others))[0]


def low_sum(left, right):
    return (left.astype(f32) + right.astype(f32)).astype(bf16)


def body(
    dp_size,
    tp_size,
    tokens,
    lengths,
    w_qkv,
    w_out,
    norm1_scale,
    norm1_shift,
    w_gate_up,
    w_down,
    norm2_scale,
    norm2_shift,
    cotangent,
):
    own = tokens[0]
    rows_here, width = own.shape
    docs = lengths.shape[1]
    seq = rows_here * tp_size
    cols_here = w_qkv.shape[2]
    heads = cols_here // HD
    units = w_gate_up.shape[2]
    pieces = min(dp_size, 8)
    groups = None if pieces == dp_size else [list(range(i, i + pieces)) for i in range(0, dp_size, pieces)]
    share = units // pieces
    rows_share = width // pieces
    span = -(-(3 * width + cols_here) // 128) * 128
    me = lax.rem(lax.axis_index("dp"), pieces)
    z = lax.axis_index("tensor")

    def flip(array, bit):
        return lax.ppermute(array, "dp", flip_axis(dp_size, bit))

    def shift(array, step):
        return lax.ppermute(array, "tensor", rotate_axis(tp_size, step))

    def along(array, step):
        return lax.ppermute(array, "tensor", line_axis(tp_size, step))

    def gather_dp(array):
        return lax.all_gather(array, "dp", axis=0, axis_index_groups=groups)

    def rope_order(matrix):
        halves = matrix.reshape(rows_share, heads, 2, HALF).transpose(0, 2, 1, 3).reshape(rows_share, 2, heads * HALF)
        return jnp.pad(halves, ((0, 0), (0, 0), (0, 128 - heads * HALF))).reshape(rows_share, 256)

    qkv_slice = lax.dynamic_slice_in_dim(w_qkv, me * rows_share, rows_share, 0)
    out_slice = lax.dynamic_slice_in_dim(w_out, me * rows_share, rows_share, 1)
    piece_one = jnp.concatenate([rope_order(qkv_slice[:, 0]), rope_order(qkv_slice[:, 1]), out_slice.T, qkv_slice[:, 2]], axis=1)
    gate_slice = lax.dynamic_slice_in_dim(w_gate_up, me * share, share, 2)
    down_slice = lax.dynamic_slice_in_dim(w_down, me * share, share, 0)
    piece_two = jnp.concatenate([gate_slice[:, 0].T, gate_slice[:, 1].T, down_slice], axis=1)
    piece_one, piece_two = lax.optimization_barrier((piece_one, piece_two))
    ones = [piece_one] + [shift(piece_one, s) for s in range(1, tp_size)]
    piece_two = after(piece_two, *ones[1:])
    twos = [shift(piece_two, s) for s in range(1, tp_size)]
    w1 = gather_dp(jnp.stack(ones))
    w2 = gather_dp(jnp.concatenate(twos, axis=0))

    own_late = after(own, *ones[1:])
    before, behind = along(own_late, 1), along(own_late, -1)
    before2, behind2 = along(before, 1), along(behind, -1)
    toks = [own, behind, jnp.where(z < tp_size // 2, behind2, before2), before]

    row_lengths, gate_up_late, down_late = after(lengths[0], ones[-1]), after(w_gate_up, ones[-1]), after(w_down, ones[-1])
    w_own = jnp.concatenate([gate_up_late[:, 0].T, gate_up_late[:, 1].T, down_late], axis=1).reshape(pieces, share, 3 * width)

    tables = doc_tables(row_lengths, seq, z * rows_here, rows_here)
    segment, position = tables[:2]
    info = make_info(tables, me)
    inverse = ROPE_BASE ** (-2.0 * lax.rem(jnp.arange(128), HALF).astype(f32) / HD)
    angles = position[:, None] * inverse[None, :]
    cosine, sine = jnp.cos(angles), jnp.sin(angles)
    seg_col = segment[:, None]

    saved = attn_fwd(info, toks, w1, cosine, sine, seg_col, docs, heads)
    rel = saved[4]
    norms = [v.reshape(1, width) for v in (norm1_scale, norm1_shift, norm2_scale, norm2_shift)]
    room = span - 3 * width - cols_here
    layer_out, grad_one, nlow, flow, brt, back, chunk, act, gg, ug = ffn_layer(own, cotangent[0], norms, rel, w1, w_own, w2, room)

    half = tp_size // 2

    me_array = jnp.stack([me, z]).astype(jnp.int32)
    fixed = (gg, ug, act, brt, nlow, flow, rel, chunk)
    far_sent = wgrad(me_array, 5, *fixed, None, pieces, share, span)
    near_sent = wgrad(after(me_array, far_sent), 1, *fixed, None, pieces, share, span)
    far_keep, far_give, far_rest = wgrad(after(me_array, near_sent), 4, *fixed, flip(far_sent, 1), pieces, share, span)
    near_keep, near_give, near_rest = wgrad(after(me_array, far_rest), 0, *fixed, flip(near_sent, 1), pieces, share, span)

    back, far_give, far_rest, near_give = lax.optimization_barrier((back, far_give, far_rest, near_give))
    got = [flip(far_give, 2), flip(far_rest, 4), flip(near_give, 2)]
    bwd = attn_bwd(info, toks, w1, cosine, sine, seg_col, saved, back, docs, heads, pieces)
    got, bwd = lax.optimization_barrier((got, bwd))
    dw, dx = bwd[0], bwd[1:]
    next_b = low_sum(near_rest, got[1])
    got_a, got_b = flip(low_sum(far_keep, got[0]), 4), flip(next_b[1], 2)
    next_a = low_sum(near_keep, got[2])
    pairs = dw.reshape((pieces // 2, 2) + dw.shape[1:])
    got_pairs = flip(pairs[:, 1], 1)
    from_left = lax.ppermute(dx[2], "tensor", [(i, i + 1) for i in range(half)])
    from_right = lax.ppermute(dx[2], "tensor", [(i + half, i + half - 1) for i in range(half)])
    got_a, got_b, got_pairs, from_left, from_right = lax.optimization_barrier((got_a, got_b, got_pairs, from_left, from_right))

    def by_slot(low, high):
        low, high = low.reshape(half, -1, low.shape[-1]), high.reshape(tp_size - half, -1, high.shape[-1])
        return [low[i] for i in range(half)] + [high[i] for i in range(tp_size - half)]

    parts_two = jnp.concatenate([low_sum(next_a, got_a), low_sum(next_b[0], got_b)], axis=0)
    share_two = lax.psum_scatter(parts_two, "tensor", scatter_dimension=0, tiled=True)
    pairs = low_sum(pairs[:, 0], got_pairs).reshape((2, 2) + dw.shape[1:])
    got_a, got_b = flip(pairs[:, 1, :half], 2), flip(pairs[1, :, half:], 4)
    near_right, near_left = low_sum(dx[1], from_left), low_sum(dx[3], from_right)
    next_a, next_b = low_sum(pairs[:, 0, :half], got_a), low_sum(pairs[0, :, half:], got_b)
    got_a, got_b = flip(next_a[1], 4), flip(next_b[1], 2)

    def total(own_part, moved):
        return functools.reduce(lambda x, y: x + y.astype(f32), moved, own_part.astype(f32)).astype(bf16)

    parts_one = by_slot(low_sum(next_a[0], got_a), low_sum(next_b[0], got_b))
    moved_one = [shift(parts_one[s], -s) for s in range(1, tp_size)]
    share_one = total(parts_one[0], moved_one)
    share_two, share_one, near_right, near_left = lax.optimization_barrier((share_two, share_one, near_right, near_left))
    input_grad = grad_one + dx[0] + along(near_right, 1).astype(f32) + along(near_left, -1).astype(f32)

    def finish(array):
        if groups is not None:
            across = [[g * pieces + i for g in range(dp_size // pieces)] for i in range(pieces)]
            array = lax.psum(array.astype(f32), "dp", axis_index_groups=across).astype(bf16)
        return gather_dp(array)

    main = finish(jnp.concatenate([share_two, share_one], axis=1)).reshape(units, -1)
    down_sum = main[:, 2 * width : 3 * width].astype(f32)
    out_sum = main[:, 3 * width : 3 * width + cols_here].astype(f32).T
    gate_up_sum = final_ffn(main, width, 128)
    qkv_sum = final_qkv(main, span, heads, 256).transpose(2, 0, 1)
    small_out = main.reshape(pieces, share, -1)[:, : 4 * width // pieces // room, span - room : span].astype(f32).reshape(4, width)
    return (
        layer_out[None],
        input_grad[None],
        qkv_sum,
        out_sum,
        small_out[0],
        small_out[1],
        gate_up_sum,
        down_sum,
        small_out[2],
        small_out[3],
    )


def solution(mesh):
    in_specs = (
        P("dp", "tensor", None),
        P("dp", None),
        P(None, None, "tensor"),
        P("tensor", None),
        P(),
        P(),
        P(None, None, "tensor"),
        P("tensor", None),
        P(),
        P(),
        P("dp", "tensor", None),
    )
    out_specs = (
        P("dp", "tensor", None),
        P("dp", "tensor", None),
        P(None, None, "tensor"),
        P("tensor", None),
        P(),
        P(),
        P(None, None, "tensor"),
        P("tensor", None),
        P(),
        P(),
    )
    return jax.shard_map(
        functools.partial(body, mesh.shape["dp"], mesh.shape["tensor"]),
        mesh=mesh,
        in_specs=in_specs,
        out_specs=out_specs,
        check_vma=False,
    )
```

```python
import functools

import jax
import jax.numpy as jnp
from jax import lax
from jax.experimental import pallas as pl
from jax.experimental.pallas import tpu as pltpu
from jax.sharding import PartitionSpec as P

TILE = 256
HALF = 32
HD = 64
BIG = 1e30
f32, bf16 = jnp.float32, jnp.bfloat16


def nt(a, b):
    return lax.dot_general(a, b, (((1,), (1,)), ((), ())), preferred_element_type=f32)


def nn(a, b):
    return jnp.dot(a, b, preferred_element_type=f32)


def stay(array):
    return pltpu.with_memory_space_constraint(array, pltpu.HBM)


def tile_rows(tile, base, count):
    return pl.ds(pl.multiple_of(lax.rem(tile - base + count, count) * TILE, TILE), TILE)


def over_tiles(info, lo, hi, tiles, scan):
    def one(t, _):
        live = [(t >= info[3 + u]) & (t < info[3 + tiles + u]) for u in range(tiles)]
        every = functools.reduce(jnp.logical_and, live)

        @pl.when(every)
        def _():
            scan(t, slice(0, tiles * TILE))

        @pl.when(jnp.logical_not(every))
        def _():
            def single(u, _):
                @pl.when((t >= info[3 + u]) & (t < info[3 + tiles + u]))
                def _():
                    scan(t, pl.ds(pl.multiple_of(u * TILE, TILE), TILE))

                return 0

            lax.fori_loop(0, tiles, single, 0)

        return 0

    lax.fori_loop(lo, hi, one, 0)


def project_kernel(*refs, docs, heads, slot):
    tok, w, cos, sin, seg = refs[:5]
    outs = refs[5:] if slot == 0 else refs[8:]
    ka, va, vt = outs[:3]
    here, width = tok.shape
    used = heads * HALF
    cols = heads * HD
    lane = lax.broadcasted_iota(jnp.int32, (TILE, 128), 1)
    filler = lax.broadcasted_iota(jnp.int32, (80 - HD, here), 0)

    def weight(start, stop):
        return w[:, 0, :, start:stop].reshape(width, stop - start)

    for h in range(heads):
        vt[0, 0, 80 * h + HD : 80 * (h + 1), :] = jnp.where(filler == 0, 1.0, 0.0).astype(bf16)

    def tile(c, _):
        rows = pl.ds(pl.multiple_of(c * TILE, TILE), TILE)
        x = tok[rows, :]
        co, si = cos[rows, :], sin[rows, :]
        hit = (lane - used) == seg[rows, :]
        if slot == 0:
            p = nn(x, weight(0, 256))
            ra = (p[:, :128] * co - p[:, 128:] * si).astype(bf16).astype(f32) * HD**-0.5
            rb = (p[:, 128:] * co + p[:, :128] * si).astype(bf16).astype(f32) * HD**-0.5
            for h in range(heads):
                keep = (lane >= HALF * h) & (lane < HALF * (h + 1))
                outs[3][0, h, rows, :128] = jnp.where(keep, ra, jnp.where(hit, -BIG, 0.0)).astype(bf16)
                outs[3][0, h, rows, 128:] = jnp.where(keep, rb, 0.0).astype(bf16)
        p = nn(x, weight(256, 512))
        other = (lane >= used) & (lane < used + docs) & jnp.logical_not(hit)
        ra, rb = p[:, :128] * co - p[:, 128:] * si, p[:, 128:] * co + p[:, :128] * si
        ka[0, 0, rows, :128] = jnp.where(lane < used, ra, jnp.where(other, 1.0, 0.0)).astype(bf16)
        ka[0, 0, rows, 128:] = rb.astype(bf16)
        v = nn(x, weight(512 + cols, 512 + 2 * cols))
        va[0, 0, rows, :] = v.astype(bf16)
        turned = v.T.astype(bf16)
        for h in range(heads):
            vt[0, 0, 80 * h : 80 * h + HD, rows] = turned[HD * h : HD * (h + 1), :]
        return 0

    lax.fori_loop(0, here // TILE, tile, 0)


def project(tok, w, cos, sin, seg, docs, heads, slot, slots, held=()):
    here, width = tok.shape
    cols = heads * HD
    shapes = [(here, 256), (here, cols), (80 * heads, here)]
    out_shape = [pltpu.HBM((slots, slots) + s, bf16) for s in shapes]
    out_specs = [pl.BlockSpec((1, 1) + s, lambda g: (g, slot, 0, 0)) for s in shapes]
    if slot == 0:
        out_shape.append(pltpu.HBM((slots, heads, here, 256), bf16))
        out_specs.append(pl.BlockSpec((1, heads, here, 256), lambda g: (g, 0, 0, 0)))
    rows = pl.BlockSpec((here, cos.shape[1]), lambda g: (slot, 0))
    return pl.pallas_call(
        functools.partial(project_kernel, docs=docs, heads=heads, slot=slot),
        grid=(slots,),
        out_shape=tuple(out_shape),
        in_specs=[
            pl.BlockSpec((here, width), lambda g: (0, 0)),
            pl.BlockSpec((w.shape[0], 1) + w.shape[2:], lambda g: (0, g, 0, 0)),
            rows,
            rows,
            pl.BlockSpec((here, 1), lambda g: (slot, 0)),
        ]
        + [pl.BlockSpec(memory_space=pl.ANY)] * len(held),
        out_specs=tuple(out_specs),
        input_output_aliases={5 + n: n for n in range(len(held))},
        compiler_params=pltpu.CompilerParams(vmem_limit_bytes=30 << 20),
        cost_estimate=pl.CostEstimate(flops=2 << 30, bytes_accessed=8 << 20, transcendentals=0),
        name="project",
    )(tok, w, cos, sin, seg, *[stay(a) for a in held])


def attn_fwd_kernel(info, seg, qh, ka, vt, lse, mixed, acc, top, *, docs, heads):
    here = qh.shape[2]
    tiles = here // TILE
    count = ka.shape[1] * tiles
    lo, hi, base = info[0], info[1], info[2]
    acc[...] = jnp.zeros_like(acc)
    top[...] = jnp.full_like(top, -3e38)

    def scan(t, mine):
        c = lax.rem(t - base + count, count)
        slot = c // tiles
        rows = pl.ds(pl.multiple_of(lax.rem(c, tiles) * TILE, TILE), TILE)
        kk = ka[0, slot, rows, :]
        scores = [nt(kk, qh[0, h, mine, :]) for h in range(heads)]
        olds = [top[h : h + 1, mine] for h in range(heads)]
        news = [jnp.maximum(olds[h], jnp.max(scores[h], axis=0, keepdims=True)) for h in range(heads)]
        probs = [jnp.exp(scores[h] - news[h]).astype(bf16) for h in range(heads)]
        adds = [nn(vt[0, slot, 80 * h : 80 * h + 80, rows], probs[h]) for h in range(heads)]
        for h in range(heads):
            top[h : h + 1, mine] = news[h]
            acc[h, :, mine] = acc[h, :, mine] * jnp.exp(olds[h] - news[h]) + adds[h]

    over_tiles(info, lo, hi, tiles, scan)
    good = seg[...] < docs - 1
    total = [jnp.where(top[h : h + 1, :] > -1e29, acc[h, HD : HD + 1, :], 1.0) for h in range(heads)]
    outs = jnp.concatenate([acc[h, :HD, :] / total[h] for h in range(heads)], axis=0).T
    mixed[0] = jnp.where(good, outs, 0.0).astype(bf16)
    stats = [top[h : h + 1, :] + jnp.log(total[h]) for h in range(heads)]
    lse[0] = jnp.concatenate(stats + [jnp.zeros((8 - heads, here), f32)], axis=0)


def attn_fwd(info, seg, qh, ka, vt, docs):
    slots, heads, here = qh.shape[:3]
    cols = heads * HD

    def part(shape):
        return pl.BlockSpec((1,) + shape[1:], lambda g: (g,) + (0,) * (len(shape) - 1))

    shapes = [((slots, 8, here), f32), ((slots, here, cols), bf16)]
    return pl.pallas_call(
        functools.partial(attn_fwd_kernel, docs=docs, heads=heads),
        grid=(slots,),
        out_shape=tuple(jax.ShapeDtypeStruct(s, d) for s, d in shapes),
        in_specs=[pl.BlockSpec(memory_space=pltpu.SMEM), pl.BlockSpec((here, 1), lambda g: (0, 0))] + [part(a.shape) for a in (qh, ka, vt)],
        out_specs=tuple(part(s) for s, _ in shapes),
        scratch_shapes=[pltpu.VMEM((heads, 80, here), f32), pltpu.VMEM((8, here), f32)],
        compiler_params=pltpu.CompilerParams(vmem_limit_bytes=40 << 20),
        cost_estimate=pl.CostEstimate(flops=12 << 30, bytes_accessed=12 << 20, transcendentals=4 << 20),
        name="attn_fwd",
    )(info, seg, stay(qh), stay(ka), stay(vt))


def attn_bwd_kernel(info, *refs, docs, heads, slots, pieces, start, stop):
    toks = refs[:slots]
    w, cos, sin, seg, qh, ka, va, lse, mixed, do = refs[slots : slots + 10]
    refs = refs[slots + 10 :]
    last = stop == slots
    if start:
        old_dkv, old_dq, refs = refs[0], refs[1], refs[2:]
    dw, refs = refs[0], refs[1:]
    if last:
        dx_out, refs = refs[:slots], refs[slots:]
    dkv, dq, tokt, dqt, dwa, doh, delta, dka, dva = refs
    here, width = toks[0].shape
    seq = here * slots
    count = seq // TILE
    used = heads * HALF
    cols = heads * HD
    tiles = here // TILE
    lo, hi, base, me = info[0], info[1], info[2], info[3 + 2 * tiles]

    @pl.when(pl.program_id(0) == 0)
    def _():
        dkv[...] = jnp.zeros_like(dkv)
        dwa[:, 512 + cols :] = jnp.zeros((width, dwa.shape[1] - 512 - cols), f32)
        for s in range(slots):
            for c in range(here // TILE):
                start = s * here + c * TILE
                tokt[:, start : start + TILE] = toks[s][c * TILE : (c + 1) * TILE, :].astype(f32).T.astype(bf16)

    g = pl.program_id(0)

    def weight(group, start, stop):
        return w[:, group, :, start:stop].reshape(width, stop - start)

    wlane = lax.broadcasted_iota(jnp.int32, (here, cols), 1)
    lane = lax.broadcasted_iota(jnp.int32, (TILE, 128), 1)
    dqt[...] = jnp.zeros_like(dqt)
    d = jnp.where(seg[:here, :] < docs - 1, do[0].astype(f32), 0.0)
    prod = d * mixed[0].astype(f32)
    prod_high = prod.astype(bf16)
    prod_low = (prod - prod_high.astype(f32)).astype(bf16)
    pick = (lax.broadcasted_iota(jnp.int32, (8, cols), 1) // HD == lax.broadcasted_iota(jnp.int32, (8, cols), 0)).astype(bf16)
    delta[...] = nt(pick, prod_high) + nt(pick, prod_low)
    for h in range(heads):
        doh[h] = jnp.where((wlane >= HD * h) & (wlane < HD * (h + 1)), d, 0.0).astype(bf16)

    def unrotate(a, b, rows):
        a, b = a.astype(bf16).astype(f32), b.astype(bf16).astype(f32)
        co, si = cos[rows, :], sin[rows, :]
        keep = lane < used
        both = [jnp.where(keep, a * co + b * si, 0.0), jnp.where(keep, b * co - a * si, 0.0)]
        return jnp.concatenate(both, axis=1).astype(bf16)

    def scan(t, mine):
        rows = tile_rows(t, base, count)
        kk, vv = ka[0, rows, :], va[0, rows, :]
        kt = kk.astype(f32).T.astype(bf16)
        qs, dd = [qh[0, h, mine, :] for h in range(heads)], [doh[h, mine, :] for h in range(heads)]
        probs = [jnp.exp(nt(kk, qs[h]) - lse[0, h : h + 1, mine]) for h in range(heads)]
        ds = [(probs[h] * (nt(vv, dd[h]) - delta[h : h + 1, mine])).astype(bf16) for h in range(heads)]
        dva[...] += sum(nn(probs[h].astype(bf16), dd[h]) for h in range(heads))
        dka[...] += sum(nn(ds[h], qs[h]) for h in range(heads))
        for h in range(heads):
            kth = jnp.concatenate([kt[HALF * h : HALF * (h + 1)], kt[128 + HALF * h : 128 + HALF * (h + 1)]], axis=0)
            g = nn(kth, ds[h])
            dqt[HALF * h : HALF * (h + 1), mine] += g[:HALF]
            dqt[128 + HALF * h : 128 + HALF * (h + 1), mine] += g[HALF:]

    def k_tile(t, _):
        rows = tile_rows(t, base, count)
        dka[...] = jnp.zeros_like(dka)
        dva[...] = jnp.zeros_like(dva)
        over_tiles(info, t, t + 1, tiles, scan)
        dkv[g, rows, :256] = unrotate(dka[:, :128], dka[:, 128:], rows)
        dkv[g, rows, 256:] = dva[...].astype(bf16)
        return 0

    lax.fori_loop(lo, hi, k_tile, 0)
    for c in range(here // TILE):
        rows = slice(c * TILE, (c + 1) * TILE)
        gq = dqt[:, rows].T * HD**-0.5
        dq[g, rows, :] = unrotate(gq[:, :128], gq[:, 128:], rows)
    dwa[:, :256] = nn(tokt[:, :here], dq[g])
    dwa[:, 256 : 512 + cols] = nn(tokt[...], dkv[g])
    share = width // pieces
    for r in range(pieces):
        p = jnp.bitwise_xor(me, r)
        dw[r, 0] = dwa[pl.ds(pl.multiple_of(p * share, 8), share), :].astype(bf16)

    if not last:
        return

    def key_grads(group, rows, cut):
        return old_dkv[group, rows, cut] if group < start else dkv[group - start, rows, cut]

    @pl.when(g == stop - start - 1)
    def _():
        for s in range(slots):
            dx_out[s][...] = jnp.zeros_like(dx_out[s])
        for s in range(slots):
            begin = lax.rem(base + s * tiles, count)

            @pl.when((begin + tiles > lo) & (begin < hi))
            def _(s=s):
                rows = slice(s * here, (s + 1) * here)
                total = sum(
                    nt(key_grads(group, rows, slice(0, 256)), weight(group, 256, 512))
                    + nt(key_grads(group, rows, slice(256, 256 + cols)), weight(group, 512 + cols, 512 + 2 * cols))
                    for group in range(slots)
                )
                if s == 0:
                    total = total + sum(nt(old_dq[group] if group < start else dq[group - start], weight(group, 0, 256)) for group in range(slots))
                dx_out[s][...] = total.astype(dx_out[s].dtype)


def attn_bwd(info, toks, w, cos, sin, seg, saved, do, docs, heads, pieces, start, stop, carry=()):
    slots = len(toks)
    here, width = toks[0].shape
    seq = here * slots
    cols = heads * HD
    span = -(-(512 + cols) // 128) * 128
    count = stop - start
    last = stop == slots

    def whole(shape):
        return pl.BlockSpec(shape, lambda g: (0,) * len(shape))

    def part(array):
        return pl.BlockSpec((1,) + array.shape[1:], lambda g: (g + start,) + (0,) * (array.ndim - 1))

    kept = [((count, seq, 256 + cols), bf16), ((count, here, 256), bf16)]
    out_shape = [jax.ShapeDtypeStruct((pieces, count, width // pieces, span), bf16)]
    out_specs = [pl.BlockSpec((pieces, 1, width // pieces, span), lambda g: (0, g, 0, 0))]
    if last:
        out_shape += [jax.ShapeDtypeStruct((here, width), f32)] + [jax.ShapeDtypeStruct((here, width), bf16)] * (slots - 1)
        out_specs += [whole((here, width))] * slots
    else:
        out_shape += [jax.ShapeDtypeStruct(s, d) for s, d in kept]
        out_specs += [whole(s) for s, _ in kept]
    return pl.pallas_call(
        functools.partial(attn_bwd_kernel, docs=docs, heads=heads, slots=slots, pieces=pieces, start=start, stop=stop),
        grid=(count,),
        out_shape=tuple(out_shape),
        in_specs=[pl.BlockSpec(memory_space=pltpu.SMEM)]
        + [whole((here, width))] * slots
        + [whole(w.shape), whole(cos.shape), whole(sin.shape), whole(seg.shape)]
        + [part(a) for a in (*saved, do)]
        + [whole(a.shape) for a in carry],
        out_specs=tuple(out_specs),
        scratch_shapes=([pltpu.VMEM(s, d) for s, d in kept] if last else [])
        + [
            pltpu.VMEM((width, seq), bf16),
            pltpu.VMEM((256, here), f32),
            pltpu.VMEM((width, span), f32),
            pltpu.VMEM((heads, here, cols), bf16),
            pltpu.VMEM((8, here), f32),
            pltpu.VMEM((TILE, 256), f32),
            pltpu.VMEM((TILE, cols), f32),
        ],
        compiler_params=pltpu.CompilerParams(vmem_limit_bytes=56 << 20),
        cost_estimate=pl.CostEstimate(flops=10 * count << 30, bytes_accessed=6 * count << 20, transcendentals=count << 20),
        name="attn_bwd",
    )(info, *toks, w, cos, sin, seg, *saved, do, *carry)


def doc_tables(lengths, seq, first, here):
    docs = lengths.shape[0]
    ends = jnp.cumsum(lengths)
    starts = ends - lengths
    place = lax.rem(jnp.arange(seq, dtype=jnp.int32) + first, seq)
    segment = jnp.sum((place[:, None] >= ends[None, :]).astype(jnp.int32), axis=1)
    member = segment[:, None] == jnp.arange(docs, dtype=jnp.int32)[None, :]
    offset = jnp.sum(jnp.where(member, starts[None, :], 0), axis=1)
    position = (place - offset).astype(f32)
    live = ends[docs - 2]
    tops = first + TILE * jnp.arange(here // TILE, dtype=jnp.int32)
    last = jnp.minimum(tops + TILE, live) - 1
    lo = jnp.max(jnp.where(starts[None, :] <= tops[:, None], starts[None, :], 0), axis=1) // TILE
    hi = jnp.minimum(jnp.min(jnp.where(ends[None, :] > last[:, None], ends[None, :], seq), axis=1), live)
    hi = jnp.where(tops < live, (hi + TILE - 1) // TILE, lo)
    span = [jnp.min(jnp.where(hi > lo, lo, seq), keepdims=True), jnp.max(jnp.where(hi > lo, hi, 0), keepdims=True)]
    return segment, position, jnp.concatenate([*span, jnp.reshape(first // TILE, (1,)), lo, hi])


def make_info(tables, me):
    return jnp.concatenate([tables[2], jnp.reshape(me, (1,))]).astype(jnp.int32)


EPSILON = 1e-05
ROWS = 256


def tn(left, right):
    return lax.dot_general(left, right, (((0,), (0,)), ((), ())), preferred_element_type=f32)


def row_mean(values):
    return jnp.mean(values, axis=-1, keepdims=True)


def normalise(values):
    centered = values - row_mean(values)
    inv = lax.rsqrt(row_mean(centered * centered) + EPSILON)
    return centered * inv, inv


def norm_back(upstream, unit, inv, scale):
    scaled = upstream * scale
    return inv * (scaled - row_mean(scaled) - unit * row_mean(scaled * unit))


def ffn_kernel(*refs, slots, pieces, share):
    own, cot, s1, b1, s2, b2, rel, w1_hbm, wown_hbm, w2_hbm = refs[:10]
    layer_out, grad_one, nlow, flow, brt, back, chunk, act_hbm, gg_hbm, ug_hbm = refs[10:20]
    w, wo, ws, g, u, normed, unit1, inv1, acc, small, stage, wsem, psem, osem, ssem = refs[20:]
    tokens, width = own.shape
    heads_cols = rel.shape[2]
    blk = slots * share
    pair = 2 if pieces % 2 == 0 else 1
    steps, wide = pieces // pair, pair * blk
    rows_share = width // pieces

    def load_own(p):
        return pltpu.make_async_copy(wown_hbm.at[p], w.at[p // pair, pl.ds(p % pair * blk, share)], psem.at[p])

    def load(p):
        return pltpu.make_async_copy(w2_hbm.at[p], w.at[p // pair, pl.ds(p % pair * blk + share, blk - share)], wsem.at[p])

    first = pltpu.make_async_copy(w1_hbm.at[:, :, :, pl.ds(512, wo.shape[3])], wo, osem)
    first.start()
    for p in range(pieces):
        load_own(p).start()
        load(p).start()
    first.wait()
    for s in range(slots):
        for p in range(pieces):
            ws[s, p * rows_share : (p + 1) * rows_share, :] = wo[p, s, :, :heads_cols]
    small[...] = jnp.zeros_like(small)

    def head(c, _):
        rows = pl.ds(pl.multiple_of(c * ROWS, ROWS), ROWS)
        h = own[rows, :].astype(f32)
        for s in range(slots):
            h = h + nt(rel[s, rows, :], ws[s])
        unit, inv = normalise(h)
        n = unit * s1[...] + b1[...]
        unit1[rows, :] = unit
        inv1[rows, :] = inv
        normed[rows, :] = n
        nlow[rows, :] = n.astype(bf16)
        acc[rows, :] = n
        return 0

    lax.fori_loop(0, tokens // ROWS, head, 0)

    def out_copy(which, target, p, slot):
        return pltpu.make_async_copy(stage.at[which, slot], target.at[:, pl.ds(pl.multiple_of(p * wide, 128), wide)], ssem.at[which, slot])

    def forward(p, _):
        slot = lax.rem(p, 2)
        cols = pl.ds(pl.multiple_of(p * wide, 128), wide)
        for i in range(pair):
            load_own(p * pair + i).wait()
            load(p * pair + i).wait()

        @pl.when(p >= 2)
        def _():
            out_copy(0, act_hbm, p - 2, slot).wait()

        halves = [slice(i, i + tokens // 2) for i in range(0, tokens, tokens // 2)]
        gates = [nt(nlow[r, :], w[p, :, :width]) for r in halves]
        ups = [nt(nlow[r, :], w[p, :, width : 2 * width]) for r in halves]
        for r, gp, up in zip(halves, gates, ups):
            g[r, cols] = gp
            u[r, cols] = up
            a = (gp * jax.nn.sigmoid(gp) * up).astype(bf16)
            stage[0, slot, r, :] = a
            acc[r, :] += nn(a, w[p, :, 2 * width :])
        out_copy(0, act_hbm, p, slot).start()
        return 0

    lax.fori_loop(0, steps, forward, 0)

    def middle(c, _):
        rows = pl.ds(pl.multiple_of(c * ROWS, ROWS), ROWS)
        unit, inv = normalise(acc[rows, :])
        layer_out[rows, :] = (unit * s2[...] + b2[...]).astype(bf16)
        up = cot[rows, :].astype(f32)
        d = norm_back(up, unit, inv, s2[...])
        small[2:3, :] += jnp.sum(up * unit, axis=0, keepdims=True)
        small[3:4, :] += jnp.sum(up, axis=0, keepdims=True)
        flow[rows, :] = d.astype(bf16)
        acc[rows, :] = d
        return 0

    lax.fori_loop(0, tokens // ROWS, middle, 0)
    for p in range(max(steps - 2, 0), steps):
        out_copy(0, act_hbm, p, p % 2).wait()

    def backward(p, _):
        slot = lax.rem(p, 2)
        cols = pl.ds(pl.multiple_of(p * wide, 128), wide)

        @pl.when(p >= 2)
        def _():
            out_copy(0, gg_hbm, p - 2, slot).wait()
            out_copy(1, ug_hbm, p - 2, slot).wait()

        halves = [slice(i, i + tokens // 2) for i in range(0, tokens, tokens // 2)]
        outer = [nt(flow[r, :], w[p, :, 2 * width :]) for r in halves]
        for r, da in zip(halves, outer):
            gp, up = g[r, cols], u[r, cols]
            sig = jax.nn.sigmoid(gp)
            both = da * sig
            dg = (both * up * (1.0 + gp * (1.0 - sig))).astype(bf16)
            du = (both * gp).astype(bf16)
            stage[0, slot, r, :] = dg
            stage[1, slot, r, :] = du
            acc[r, :] += nn(dg, w[p, :, :width]) + nn(du, w[p, :, width : 2 * width])
        out_copy(0, gg_hbm, p, slot).start()
        out_copy(1, ug_hbm, p, slot).start()
        return 0

    lax.fori_loop(0, steps, backward, 0)

    def tail(c, _):
        rows = pl.ds(pl.multiple_of(c * ROWS, ROWS), ROWS)
        up, unit = acc[rows, :], unit1[rows, :]
        d = norm_back(up, unit, inv1[rows, :], s1[...])
        small[0:1, :] += jnp.sum(up * unit, axis=0, keepdims=True)
        small[1:2, :] += jnp.sum(up, axis=0, keepdims=True)
        grad_one[rows, :] = d
        low = d.astype(bf16)
        brt[:, rows] = d.T.astype(bf16)
        for s in range(slots):
            back[s, rows, :] = nn(low, ws[s]).astype(bf16)
        return 0

    lax.fori_loop(0, tokens // ROWS, tail, 0)
    chunk[...] = jnp.zeros_like(chunk)
    room = chunk.shape[2]
    each = 4 * width // pieces // room
    for n in range(pieces * each):
        j, lane = divmod(n * room, width)
        chunk[n // each, n % each : n % each + 1, :] = small[j : j + 1, lane : lane + room]
    for p in range(max(steps - 2, 0), steps):
        out_copy(0, gg_hbm, p, p % 2).wait()
        out_copy(1, ug_hbm, p, p % 2).wait()


def ffn_layer(own, cot, norms, rel, w1, w_own, w2, room):
    slots, tokens, cols = rel.shape
    width = own.shape[1]
    pieces, share = w_own.shape[:2]
    units = pieces * slots * share
    pair = 2 if pieces % 2 == 0 else 1
    vm, hbm = pl.BlockSpec(memory_space=pltpu.VMEM), pl.BlockSpec(memory_space=pl.ANY)
    wide = jax.ShapeDtypeStruct((tokens, width), bf16)
    hidden = jax.ShapeDtypeStruct((tokens, units), bf16)
    return pl.pallas_call(
        functools.partial(ffn_kernel, slots=slots, pieces=pieces, share=share),
        out_shape=(wide, jax.ShapeDtypeStruct((tokens, width), f32), wide, wide, jax.ShapeDtypeStruct((width, tokens), bf16))
        + (jax.ShapeDtypeStruct((slots, tokens, cols), bf16), jax.ShapeDtypeStruct((pieces, 16, room), f32), hidden, hidden, hidden),
        in_specs=[vm] * 7 + [hbm] * 3,
        out_specs=(vm,) * 7 + (hbm,) * 3,
        scratch_shapes=[
            pltpu.VMEM((pieces // pair, pair * slots * share, 3 * width), bf16),
            pltpu.VMEM((pieces, slots, width // pieces, 256), bf16),
            pltpu.VMEM((slots, width, cols), bf16),
            pltpu.VMEM((tokens, units), f32),
            pltpu.VMEM((tokens, units), f32),
            pltpu.VMEM((tokens, width), f32),
            pltpu.VMEM((tokens, width), f32),
            pltpu.VMEM((tokens, 1), f32),
            pltpu.VMEM((tokens, width), f32),
            pltpu.VMEM((8, width), f32),
            pltpu.VMEM((2, 2, tokens, pair * slots * share), bf16),
            pltpu.SemaphoreType.DMA((pieces,)),
            pltpu.SemaphoreType.DMA((pieces,)),
            pltpu.SemaphoreType.DMA,
            pltpu.SemaphoreType.DMA((2, 2)),
        ],
        compiler_params=pltpu.CompilerParams(vmem_limit_bytes=60 << 20),
        cost_estimate=pl.CostEstimate(flops=16 << 30, bytes_accessed=30 << 20, transcendentals=3 << 20),
        name="ffn_layer",
    )(own, cot, *norms, rel, w1, w_own, w2)


def wgrad_kernel(*refs, slots, share, add):
    gg, ug, act, brt, nlow, flow, rel, small = refs[1:9]
    got = refs[9] if add else None
    width = nlow.shape[1]
    cols = rel.shape[2]
    edge = 3 * width + cols
    blk = slots * share
    out = refs[-1] if add else refs[-1].at[0]
    room = out.shape[1] - edge

    def put(rows, lanes, value):
        if add:
            value = value + got[0, rows, lanes].astype(f32)
        out[rows, lanes] = value.astype(bf16)

    terms = [tn(gg[...], nlow[...]), tn(ug[...], nlow[...]), tn(act[...], flow[...])]
    for s in range(slots):
        place = lax.rem(refs[0][1] - s + slots, slots)
        rows = pl.ds(pl.multiple_of(place * share, 32 if share % 32 == 0 else 4), share)
        for i in range(3):
            put(rows, slice(i * width, (i + 1) * width), terms[i][s * share : (s + 1) * share])
        put(rows, slice(3 * width, edge), nn(brt[...], rel[s]))
        put(rows, slice(edge, edge + room), jnp.concatenate([small[0], jnp.zeros((share - 16, room), f32)], axis=0))
    if add:
        first, second, rest = refs[10:13]
        top = first.shape[0]

        @pl.when(pl.program_id(0) == 0)
        def _():
            first[...] = out[:top, :]

        @pl.when(pl.program_id(0) == 1)
        def _():
            second[...] = out[:top, :]

        rest[0] = out[top:, :]


def wgrad(me, start, gg, ug, act, brt, nlow, flow, rel, small, got, pieces, share, span):
    slots = rel.shape[0]
    tokens, width = nlow.shape
    blk = slots * share
    top = slots // 2 * share

    def piece(i, me):
        return jnp.bitwise_xor(2 * i + start, me[0])

    both = pl.BlockSpec((1, blk, span), lambda i, me: (i, 0, 0))
    in_specs = [pl.BlockSpec((tokens, blk), lambda i, me: (0, piece(i, me)))] * 3
    in_specs += [pl.BlockSpec((width // pieces, tokens), lambda i, me: (piece(i, me), 0))]
    in_specs += [pl.BlockSpec((tokens, width), lambda i, me: (0, 0))] * 2
    in_specs += [pl.BlockSpec(rel.shape, lambda i, me: (0, 0, 0)), pl.BlockSpec((1,) + small.shape[1:], lambda i, me: (piece(i, me), 0, 0))]
    args = [stay(gg), stay(ug), stay(act), brt, nlow, flow, rel, small]
    if got is None:
        out_shape, out_specs, scratch = jax.ShapeDtypeStruct((2, blk, span), bf16), both, []
    else:
        in_specs.append(both)
        args.append(got)
        half = jax.ShapeDtypeStruct((top, span), bf16)
        out_shape = (half, half, jax.ShapeDtypeStruct((2, blk - top, span), bf16))
        fixed = pl.BlockSpec((top, span), lambda i, me: (0, 0))
        out_specs = (fixed, fixed, pl.BlockSpec((1, blk - top, span), lambda i, me: (i, 0, 0)))
        scratch = [pltpu.VMEM((blk, span), bf16)]
    return pl.pallas_call(
        functools.partial(wgrad_kernel, slots=slots, share=share, add=got is not None),
        out_shape=out_shape,
        grid_spec=pltpu.PrefetchScalarGridSpec(num_scalar_prefetch=1, grid=(2,), in_specs=in_specs, out_specs=out_specs, scratch_shapes=scratch),
        compiler_params=pltpu.CompilerParams(vmem_limit_bytes=40 << 20),
        cost_estimate=pl.CostEstimate(flops=2 << 30, bytes_accessed=10 << 20, transcendentals=0),
        name="wgrad",
    )(me, *args)


def final_kernel(gate, up, down, out_part, query, key, value, edge, gate_up_sum, down_sum, out_sum, qkv_sum, small_sum, *, heads, pieces, share, room):
    cols = heads * HD
    gate_up_sum[:, 0, :] = gate[...].astype(f32).T
    gate_up_sum[:, 1, :] = up[...].astype(f32).T
    down_sum[...] = down[...].astype(f32)
    out_sum[...] = out_part[...].astype(f32).T[:cols]
    for k, source in enumerate((query, key)):
        turned = source[...].astype(f32).T
        for h in range(heads):
            for half in range(2):
                start = 128 * half + HALF * h
                qkv_sum[k, HD * h + HALF * half : HD * h + HALF * (half + 1), :] = turned[start : start + HALF, :]
    qkv_sum[2, :, :] = value[...].astype(f32).T[:cols]

    @pl.when(pl.program_id(0) == 0)
    def _():
        width = small_sum.shape[1]
        each = 4 * width // pieces // room
        for n in range(pieces * each):
            j, lane = divmod(n * room, width)
            row = n // each * share + n % each
            base = row // 16 * 16
            block = edge[base : base + 16, 128 - room :].astype(f32)
            small_sum[j : j + 1, lane : lane + room] = block[row - base : row - base + 1, :]


def final_sums(main, width, span, heads, pieces):
    units = main.shape[0]
    lanes = 128
    steps = width // lanes
    cols = heads * HD
    room = span - 3 * width - cols
    tall = units // steps

    def band(first, size):
        return pl.BlockSpec((tall, size), lambda i, n=first // size: (i, n))

    in_specs = [pl.BlockSpec((units, lanes), lambda i: (0, i)), pl.BlockSpec((units, lanes), lambda i: (0, i + steps))]
    in_specs += [band(2 * width, width), band(3 * width, 256)] + [band(span + 256 * k, 256) for k in range(3)]
    in_specs += [pl.BlockSpec((units, lanes), lambda i: (0, span // lanes - 1))]
    return pl.pallas_call(
        functools.partial(final_kernel, heads=heads, pieces=pieces, share=units // pieces, room=room),
        grid=(steps,),
        out_shape=(
            jax.ShapeDtypeStruct((width, 2, units), f32),
            jax.ShapeDtypeStruct((units, width), f32),
            jax.ShapeDtypeStruct((cols, width), f32),
            jax.ShapeDtypeStruct((3, cols, width), f32),
            jax.ShapeDtypeStruct((4, width), f32),
        ),
        in_specs=in_specs,
        out_specs=(
            pl.BlockSpec((lanes, 2, units), lambda i: (i, 0, 0)),
            pl.BlockSpec((tall, width), lambda i: (i, 0)),
            pl.BlockSpec((cols, tall), lambda i: (0, i)),
            pl.BlockSpec((3, cols, tall), lambda i: (0, 0, i)),
            pl.BlockSpec((4, width), lambda i: (0, 0)),
        ),
        cost_estimate=pl.CostEstimate(flops=1 << 20, bytes_accessed=15 << 20, transcendentals=0),
        name="final_sums",
    )(*[main] * 8)


ROPE_BASE = 1000.0


def rotate_axis(size, step):
    return [(i, (i + step) % size) for i in range(size)]


def line_axis(size, step):
    return [(i, i + step) for i in range(size) if 0 <= i + step < size]


def flip_axis(size, bit):
    return [(i, i ^ bit) for i in range(size)]


def after(value, *others):
    return lax.optimization_barrier((value, *others))[0]


def low_sum(left, right):
    return (left.astype(f32) + right.astype(f32)).astype(bf16)


def body(
    dp_size,
    tp_size,
    tokens,
    lengths,
    w_qkv,
    w_out,
    norm1_scale,
    norm1_shift,
    w_gate_up,
    w_down,
    norm2_scale,
    norm2_shift,
    cotangent,
):
    own = tokens[0]
    rows_here, width = own.shape
    docs = lengths.shape[1]
    seq = rows_here * tp_size
    cols_here = w_qkv.shape[2]
    heads = cols_here // HD
    units = w_gate_up.shape[2]
    pieces = min(dp_size, 8)
    groups = None if pieces == dp_size else [list(range(i, i + pieces)) for i in range(0, dp_size, pieces)]
    share = units // pieces
    rows_share = width // pieces
    span = -(-(3 * width + cols_here) // 128) * 128
    me = lax.rem(lax.axis_index("dp"), pieces)
    z = lax.axis_index("tensor")

    def flip(array, bit):
        return lax.ppermute(array, "dp", flip_axis(dp_size, bit))

    def shift(array, step):
        return lax.ppermute(array, "tensor", rotate_axis(tp_size, step))

    def along(array, step):
        return lax.ppermute(array, "tensor", line_axis(tp_size, step))

    def gather_dp(array):
        return lax.all_gather(array, "dp", axis=0, axis_index_groups=groups)

    def rope_order(matrix):
        halves = matrix.reshape(rows_share, heads, 2, HALF).transpose(0, 2, 1, 3).reshape(rows_share, 2, heads * HALF)
        return jnp.pad(halves, ((0, 0), (0, 0), (0, 128 - heads * HALF))).reshape(rows_share, 256)

    qkv_slice = lax.dynamic_slice_in_dim(w_qkv, me * rows_share, rows_share, 0)
    out_slice = lax.dynamic_slice_in_dim(w_out, me * rows_share, rows_share, 1)
    piece_one = jnp.concatenate([rope_order(qkv_slice[:, 0]), rope_order(qkv_slice[:, 1]), out_slice.T, qkv_slice[:, 2]], axis=1)
    gate_slice = lax.dynamic_slice_in_dim(w_gate_up, me * share, share, 2)
    down_slice = lax.dynamic_slice_in_dim(w_down, me * share, share, 0)
    piece_two = jnp.concatenate([gate_slice[:, 0].T, gate_slice[:, 1].T, down_slice], axis=1)
    piece_one, piece_two = lax.optimization_barrier((piece_one, piece_two))
    ones = [piece_one] + [shift(piece_one, s) for s in range(1, tp_size)]
    piece_two = after(piece_two, *ones[1:])
    twos = [shift(piece_two, s) for s in range(1, tp_size)]
    w1 = gather_dp(jnp.stack(ones))
    row_lengths, gate_up_late, down_late = after(lengths[0], ones[-1]), after(w_gate_up, ones[-1]), after(w_down, ones[-1])
    w_own = jnp.concatenate([gate_up_late[:, 0].T, gate_up_late[:, 1].T, down_late], axis=1).reshape(pieces, share, 3 * width)

    tables = doc_tables(row_lengths, seq, z * rows_here, rows_here)
    segment, position = tables[:2]
    info = make_info(tables, me)
    inverse = ROPE_BASE ** (-2.0 * lax.rem(jnp.arange(128), HALF).astype(f32) / HD)
    angles = position[:, None] * inverse[None, :]
    cosine, sine = jnp.cos(angles), jnp.sin(angles)
    seg_col = segment[:, None]

    twos, cosine, sine, seg_col, info, w_own = lax.optimization_barrier((twos, cosine, sine, seg_col, info, w_own))
    w2 = gather_dp(jnp.concatenate(twos, axis=0))

    own_late = after(own, *ones[1:])
    before, behind = along(own_late, 1), along(own_late, -1)

    *held, qh = project(own, w1, cosine, sine, seg_col, docs, heads, 0, tp_size)
    held, before, behind = lax.optimization_barrier((held, before, behind))
    before2, behind2 = along(before, 1), along(behind, -1)
    held = project(behind, w1, cosine, sine, seg_col, docs, heads, 1, tp_size, held)
    held = project(before, w1, cosine, sine, seg_col, docs, heads, 3, tp_size, held)
    held, behind2, before2 = lax.optimization_barrier((held, behind2, before2))
    toks = [own, behind, jnp.where(z < tp_size // 2, behind2, before2), before]
    held = project(toks[2], w1, cosine, sine, seg_col, docs, heads, 2, tp_size, held)
    lse, rel = attn_fwd(info, seg_col, qh, held[0], held[2], docs)
    saved = (qh, held[0].reshape(tp_size, seq, -1), held[1].reshape(tp_size, seq, -1), lse, rel)
    norms = [v.reshape(1, width) for v in (norm1_scale, norm1_shift, norm2_scale, norm2_shift)]
    room = span - 3 * width - cols_here
    layer_out, grad_one, nlow, flow, brt, back, chunk, act, gg, ug = ffn_layer(own, cotangent[0], norms, rel, w1, w_own, w2, room)

    half = tp_size // 2

    me_array = jnp.stack([me, z]).astype(jnp.int32)
    fixed = (gg, ug, act, brt, nlow, flow, rel, chunk)
    far_sent = wgrad(me_array, 5, *fixed, None, pieces, share, span)
    near_sent = wgrad(after(me_array, far_sent), 1, *fixed, None, pieces, share, span)
    far_keep, far_give, far_rest = wgrad(after(me_array, near_sent), 4, *fixed, flip(far_sent, 1), pieces, share, span)
    near_keep, near_give, near_rest = wgrad(after(me_array, far_rest), 0, *fixed, flip(near_sent, 1), pieces, share, span)

    back, far_give, far_rest, near_give = lax.optimization_barrier((back, far_give, far_rest, near_give))
    got = [flip(far_give, 2), flip(far_rest, 4), flip(near_give, 2)]
    backward = functools.partial(attn_bwd, info, toks, w1, cosine, sine, seg_col, saved)
    cut = tp_size - 1
    dw_low, *carry = backward(back, docs, heads, pieces, 0, cut)
    got, dw_low, carry, back_late = lax.optimization_barrier((got, dw_low, carry, back))
    next_b = low_sum(near_rest, got[1])
    give_a, next_a = low_sum(far_keep, got[0]), low_sum(near_keep, got[2])
    back_late, next_a, give_a, next_b = lax.optimization_barrier((back_late, next_a, give_a, next_b))
    got_a, got_b, got_low = flip(give_a, 4), flip(next_b[1], 2), flip(dw_low.reshape((pieces // 2, 2) + dw_low.shape[1:])[:, 1], 1)
    dw_high, *dx = backward(back_late, docs, heads, pieces, cut, tp_size, carry)
    got_a, got_b, got_low, dw_high, dx = lax.optimization_barrier((got_a, got_b, got_low, dw_high, dx))
    parts_two = jnp.concatenate([low_sum(next_a, got_a), low_sum(next_b[0], got_b)], axis=0)
    share_two = lax.psum_scatter(parts_two, "tensor", scatter_dimension=0, tiled=True)

    def pairs_of(array):
        return array.reshape((pieces // 2, 2) + array.shape[1:])

    got_high = flip(pairs_of(dw_high)[:, 1], 1)
    low = low_sum(pairs_of(dw_low)[:, 0], got_low).reshape((2, 2) + dw_low.shape[1:])
    got_a = flip(low[:, 1, :half], 2)
    high = low_sum(pairs_of(dw_high)[:, 0], got_high).reshape((2, 2) + dw_high.shape[1:])
    high = jnp.concatenate([low[:, :, half:], high], axis=2)
    got_b = flip(high[1], 4)
    next_a, next_b = low_sum(low[:, 0, :half], got_a), low_sum(high[0], got_b)
    got_a, got_b = flip(next_a[1], 4), flip(next_b[1], 2)

    def by_slot(low, high):
        low, high = low.reshape(half, -1, low.shape[-1]), high.reshape(tp_size - half, -1, high.shape[-1])
        return [low[i] for i in range(half)] + [high[i] for i in range(tp_size - half)]

    def total(own_part, moved):
        return functools.reduce(lambda x, y: x + y.astype(f32), moved, own_part.astype(f32)).astype(bf16)

    parts_one = by_slot(low_sum(next_a[0], got_a), low_sum(next_b[0], got_b))
    moved_one = [shift(parts_one[s], -s) for s in range(1, tp_size)]
    share_one = total(parts_one[0], moved_one)
    share_two, share_one, dx = lax.optimization_barrier((share_two, share_one, dx))
    from_left = lax.ppermute(dx[2], "tensor", [(i, i + 1) for i in range(half)])
    from_right = lax.ppermute(dx[2], "tensor", [(i + half, i + half - 1) for i in range(half)])
    near_right, near_left = low_sum(dx[1], from_left), low_sum(dx[3], from_right)
    input_grad = grad_one + dx[0] + along(near_right, 1).astype(f32) + along(near_left, -1).astype(f32)

    def finish(array):
        if groups is not None:
            across = [[g * pieces + i for g in range(dp_size // pieces)] for i in range(pieces)]
            array = lax.psum(array.astype(f32), "dp", axis_index_groups=across).astype(bf16)
        return gather_dp(array)

    main = finish(jnp.concatenate([share_two, share_one], axis=1)).reshape(units, -1)
    gate_up_sum, down_sum, out_sum, qkv_turned, small_out = final_sums(main, width, span, heads, pieces)
    qkv_sum = qkv_turned.transpose(2, 0, 1)
    return (
        layer_out[None],
        input_grad[None],
        qkv_sum,
        out_sum,
        small_out[0],
        small_out[1],
        gate_up_sum,
        down_sum,
        small_out[2],
        small_out[3],
    )


def solution(mesh):
    in_specs = (
        P("dp", "tensor", None),
        P("dp", None),
        P(None, None, "tensor"),
        P("tensor", None),
        P(),
        P(),
        P(None, None, "tensor"),
        P("tensor", None),
        P(),
        P(),
        P("dp", "tensor", None),
    )
    out_specs = (
        P("dp", "tensor", None),
        P("dp", "tensor", None),
        P(None, None, "tensor"),
        P("tensor", None),
        P(),
        P(),
        P(None, None, "tensor"),
        P("tensor", None),
        P(),
        P(),
    )
    return jax.shard_map(
        functools.partial(body, mesh.shape["dp"], mesh.shape["tensor"]),
        mesh=mesh,
        in_specs=in_specs,
        out_specs=out_specs,
        check_vma=False,
    )
```

```python
import functools

import jax
import jax.numpy as jnp
from jax import lax
from jax.experimental import pallas as pl
from jax.experimental.pallas import tpu as pltpu
from jax.sharding import PartitionSpec as P

TILE = 256
HALF = 32
HD = 64
BIG = 1e30
f32, bf16 = jnp.float32, jnp.bfloat16


def nt(a, b):
    return lax.dot_general(a, b, (((1,), (1,)), ((), ())), preferred_element_type=f32)


def nn(a, b):
    return jnp.dot(a, b, preferred_element_type=f32)


def stay(array):
    return pltpu.with_memory_space_constraint(array, pltpu.HBM)


def tile_rows(tile, base, count):
    return pl.ds(pl.multiple_of(lax.rem(tile - base + count, count) * TILE, TILE), TILE)


def over_tiles(info, lo, hi, tiles, scan):
    def one(t, _):
        live = [(t >= info[3 + u]) & (t < info[3 + tiles + u]) for u in range(tiles)]
        every = functools.reduce(jnp.logical_and, live)

        @pl.when(every)
        def _():
            scan(t, slice(0, tiles * TILE))

        @pl.when(jnp.logical_not(every))
        def _():
            def single(u, _):
                @pl.when((t >= info[3 + u]) & (t < info[3 + tiles + u]))
                def _():
                    scan(t, pl.ds(pl.multiple_of(u * TILE, TILE), TILE))

                return 0

            lax.fori_loop(0, tiles, single, 0)

        return 0

    lax.fori_loop(lo, hi, one, 0)


def project_kernel(*refs, docs, heads, slot):
    tok, w, cos, sin, seg = refs[:5]
    outs = refs[5:] if slot == 0 else refs[8:]
    ka, va, vt = outs[:3]
    here, width = tok.shape
    used = heads * HALF
    cols = heads * HD
    lane = lax.broadcasted_iota(jnp.int32, (TILE, 128), 1)
    filler = lax.broadcasted_iota(jnp.int32, (80 - HD, here), 0)

    def weight(start, stop):
        return w[:, 0, :, start:stop].reshape(width, stop - start)

    for h in range(heads):
        vt[0, 0, 80 * h + HD : 80 * (h + 1), :] = jnp.where(filler == 0, 1.0, 0.0).astype(bf16)

    def tile(c, _):
        rows = pl.ds(pl.multiple_of(c * TILE, TILE), TILE)
        x = tok[rows, :]
        co, si = cos[rows, :], sin[rows, :]
        hit = (lane - used) == seg[rows, :]
        if slot == 0:
            p = nn(x, weight(0, 256))
            ra = (p[:, :128] * co - p[:, 128:] * si).astype(bf16).astype(f32) * HD**-0.5
            rb = (p[:, 128:] * co + p[:, :128] * si).astype(bf16).astype(f32) * HD**-0.5
            for h in range(heads):
                keep = (lane >= HALF * h) & (lane < HALF * (h + 1))
                outs[3][0, h, rows, :128] = jnp.where(keep, ra, jnp.where(hit, -BIG, 0.0)).astype(bf16)
                outs[3][0, h, rows, 128:] = jnp.where(keep, rb, 0.0).astype(bf16)
        p = nn(x, weight(256, 512))
        other = (lane >= used) & (lane < used + docs) & jnp.logical_not(hit)
        ra, rb = p[:, :128] * co - p[:, 128:] * si, p[:, 128:] * co + p[:, :128] * si
        ka[0, 0, rows, :128] = jnp.where(lane < used, ra, jnp.where(other, 1.0, 0.0)).astype(bf16)
        ka[0, 0, rows, 128:] = rb.astype(bf16)
        v = nn(x, weight(512 + cols, 512 + 2 * cols))
        va[0, 0, rows, :] = v.astype(bf16)
        turned = v.T.astype(bf16)
        for h in range(heads):
            vt[0, 0, 80 * h : 80 * h + HD, rows] = turned[HD * h : HD * (h + 1), :]
        return 0

    lax.fori_loop(0, here // TILE, tile, 0)


def project(tok, w, cos, sin, seg, docs, heads, slot, slots, held=()):
    here, width = tok.shape
    cols = heads * HD
    shapes = [(here, 256), (here, cols), (80 * heads, here)]
    out_shape = [pltpu.HBM((slots, slots) + s, bf16) for s in shapes]
    out_specs = [pl.BlockSpec((1, 1) + s, lambda g: (g, slot, 0, 0)) for s in shapes]
    if slot == 0:
        out_shape.append(pltpu.HBM((slots, heads, here, 256), bf16))
        out_specs.append(pl.BlockSpec((1, heads, here, 256), lambda g: (g, 0, 0, 0)))
    rows = pl.BlockSpec((here, cos.shape[1]), lambda g: (slot, 0))
    return pl.pallas_call(
        functools.partial(project_kernel, docs=docs, heads=heads, slot=slot),
        grid=(slots,),
        out_shape=tuple(out_shape),
        in_specs=[
            pl.BlockSpec((here, width), lambda g: (0, 0)),
            pl.BlockSpec((w.shape[0], 1) + w.shape[2:], lambda g: (0, g, 0, 0)),
            rows,
            rows,
            pl.BlockSpec((here, 1), lambda g: (slot, 0)),
        ]
        + [pl.BlockSpec(memory_space=pl.ANY)] * len(held),
        out_specs=tuple(out_specs),
        input_output_aliases={5 + n: n for n in range(len(held))},
        compiler_params=pltpu.CompilerParams(vmem_limit_bytes=20 << 20),
        cost_estimate=pl.CostEstimate(flops=2 << 30, bytes_accessed=8 << 20, transcendentals=0),
        name="project",
    )(tok, w, cos, sin, seg, *[stay(a) for a in held])


def attn_fwd_kernel(info, seg, qh, ka, vt, lse, mixed, acc, top, *, docs, heads):
    here = qh.shape[2]
    tiles = here // TILE
    count = ka.shape[1] * tiles
    lo, hi, base = info[0], info[1], info[2]
    acc[...] = jnp.zeros_like(acc)
    top[...] = jnp.full_like(top, -3e38)

    def scan(t, mine):
        c = lax.rem(t - base + count, count)
        slot = c // tiles
        rows = pl.ds(pl.multiple_of(lax.rem(c, tiles) * TILE, TILE), TILE)
        kk = ka[0, slot, rows, :]
        scores = [nt(kk, qh[0, h, mine, :]) for h in range(heads)]
        olds = [top[h : h + 1, mine] for h in range(heads)]
        news = [jnp.maximum(olds[h], jnp.max(scores[h], axis=0, keepdims=True)) for h in range(heads)]
        probs = [jnp.exp(scores[h] - news[h]).astype(bf16) for h in range(heads)]
        adds = [nn(vt[0, slot, 80 * h : 80 * h + 80, rows], probs[h]) for h in range(heads)]
        for h in range(heads):
            top[h : h + 1, mine] = news[h]
            acc[h, :, mine] = acc[h, :, mine] * jnp.exp(olds[h] - news[h]) + adds[h]

    over_tiles(info, lo, hi, tiles, scan)
    good = seg[...] < docs - 1
    total = [jnp.where(top[h : h + 1, :] > -1e29, acc[h, HD : HD + 1, :], 1.0) for h in range(heads)]
    outs = jnp.concatenate([acc[h, :HD, :] / total[h] for h in range(heads)], axis=0).T
    mixed[0] = jnp.where(good, outs, 0.0).astype(bf16)
    stats = [top[h : h + 1, :] + jnp.log(total[h]) for h in range(heads)]
    lse[0] = jnp.concatenate(stats + [jnp.zeros((8 - heads, here), f32)], axis=0)


def attn_fwd(info, seg, qh, ka, vt, docs):
    slots, heads, here = qh.shape[:3]
    cols = heads * HD

    def part(shape):
        return pl.BlockSpec((1,) + shape[1:], lambda g: (g,) + (0,) * (len(shape) - 1))

    shapes = [((slots, 8, here), f32), ((slots, here, cols), bf16)]
    return pl.pallas_call(
        functools.partial(attn_fwd_kernel, docs=docs, heads=heads),
        grid=(slots,),
        out_shape=tuple(jax.ShapeDtypeStruct(s, d) for s, d in shapes),
        in_specs=[pl.BlockSpec(memory_space=pltpu.SMEM), pl.BlockSpec((here, 1), lambda g: (0, 0))] + [part(a.shape) for a in (qh, ka, vt)],
        out_specs=tuple(part(s) for s, _ in shapes),
        scratch_shapes=[pltpu.VMEM((heads, 80, here), f32), pltpu.VMEM((8, here), f32)],
        compiler_params=pltpu.CompilerParams(vmem_limit_bytes=24 << 20),
        cost_estimate=pl.CostEstimate(flops=12 << 30, bytes_accessed=12 << 20, transcendentals=4 << 20),
        name="attn_fwd",
    )(info, seg, stay(qh), stay(ka), stay(vt))


def attn_bwd_kernel(info, *refs, docs, heads, slots, pieces):
    toks = refs[:slots]
    cos, sin, seg, qh, ka, va, lse, mixed, do = refs[slots : slots + 9]
    dw, dkv, dq, tokt, dqt, dwa, doh, delta, dka, dva = refs[slots + 9 :]
    here, width = toks[0].shape
    seq = here * slots
    count = seq // TILE
    used = heads * HALF
    cols = heads * HD
    tiles = here // TILE
    lo, hi, base, me = info[0], info[1], info[2], info[3 + 2 * tiles]

    @pl.when(pl.program_id(0) == 0)
    def _():
        dkv[...] = jnp.zeros_like(dkv)
        dwa[:, 512 + cols :] = jnp.zeros((width, dwa.shape[1] - 512 - cols), f32)
        for s in range(slots):
            for c in range(here // TILE):
                start = s * here + c * TILE
                tokt[:, start : start + TILE] = toks[s][c * TILE : (c + 1) * TILE, :].astype(f32).T.astype(bf16)

    g = pl.program_id(0)

    wlane = lax.broadcasted_iota(jnp.int32, (here, cols), 1)
    lane = lax.broadcasted_iota(jnp.int32, (TILE, 128), 1)
    dqt[...] = jnp.zeros_like(dqt)
    d = jnp.where(seg[:here, :] < docs - 1, do[0].astype(f32), 0.0)
    prod = d * mixed[0].astype(f32)
    prod_high = prod.astype(bf16)
    prod_low = (prod - prod_high.astype(f32)).astype(bf16)
    pick = (lax.broadcasted_iota(jnp.int32, (8, cols), 1) // HD == lax.broadcasted_iota(jnp.int32, (8, cols), 0)).astype(bf16)
    delta[...] = nt(pick, prod_high) + nt(pick, prod_low)
    for h in range(heads):
        doh[h] = jnp.where((wlane >= HD * h) & (wlane < HD * (h + 1)), d, 0.0).astype(bf16)

    def unrotate(a, b, rows):
        a, b = a.astype(bf16).astype(f32), b.astype(bf16).astype(f32)
        co, si = cos[rows, :], sin[rows, :]
        keep = lane < used
        both = [jnp.where(keep, a * co + b * si, 0.0), jnp.where(keep, b * co - a * si, 0.0)]
        return jnp.concatenate(both, axis=1).astype(bf16)

    def scan(t, mine):
        rows = tile_rows(t, base, count)
        kk, vv = ka[0, rows, :], va[0, rows, :]
        kt = kk.astype(f32).T.astype(bf16)
        qs, dd = [qh[0, h, mine, :] for h in range(heads)], [doh[h, mine, :] for h in range(heads)]
        probs = [jnp.exp(nt(kk, qs[h]) - lse[0, h : h + 1, mine]) for h in range(heads)]
        ds = [(probs[h] * (nt(vv, dd[h]) - delta[h : h + 1, mine])).astype(bf16) for h in range(heads)]
        dva[...] += sum(nn(probs[h].astype(bf16), dd[h]) for h in range(heads))
        dka[...] += sum(nn(ds[h], qs[h]) for h in range(heads))
        for h in range(heads):
            kth = jnp.concatenate([kt[HALF * h : HALF * (h + 1)], kt[128 + HALF * h : 128 + HALF * (h + 1)]], axis=0)
            g = nn(kth, ds[h])
            dqt[HALF * h : HALF * (h + 1), mine] += g[:HALF]
            dqt[128 + HALF * h : 128 + HALF * (h + 1), mine] += g[HALF:]

    def k_tile(t, _):
        rows = tile_rows(t, base, count)
        dka[...] = jnp.zeros_like(dka)
        dva[...] = jnp.zeros_like(dva)
        over_tiles(info, t, t + 1, tiles, scan)
        dkv[g, rows, :256] = unrotate(dka[:, :128], dka[:, 128:], rows)
        dkv[g, rows, 256:] = dva[...].astype(bf16)
        return 0

    lax.fori_loop(lo, hi, k_tile, 0)
    for c in range(here // TILE):
        rows = slice(c * TILE, (c + 1) * TILE)
        gq = dqt[:, rows].T * HD**-0.5
        dq[g, rows, :] = unrotate(gq[:, :128], gq[:, 128:], rows)
    dwa[:, :256] = nn(tokt[:, :here], dq[g])
    dwa[:, 256 : 512 + cols] = nn(tokt[...], dkv[g])
    share = width // pieces
    for r in range(pieces):
        p = jnp.bitwise_xor(me, r)
        dw[r, 0] = dwa[pl.ds(pl.multiple_of(p * share, 8), share), :].astype(bf16)


def attn_bwd(info, toks, cos, sin, seg, saved, do, docs, heads, pieces, start, stop):
    slots = len(toks)
    here, width = toks[0].shape
    seq = here * slots
    cols = heads * HD
    span = -(-(512 + cols) // 128) * 128
    count = stop - start

    def whole(shape):
        return pl.BlockSpec(shape, lambda g: (0,) * len(shape))

    def part(array):
        return pl.BlockSpec((1,) + array.shape[1:], lambda g: (g + start,) + (0,) * (array.ndim - 1))

    kept = [((count, seq, 256 + cols), bf16), ((count, here, 256), bf16)]
    return pl.pallas_call(
        functools.partial(attn_bwd_kernel, docs=docs, heads=heads, slots=slots, pieces=pieces),
        grid=(count,),
        out_shape=(jax.ShapeDtypeStruct((pieces, count, width // pieces, span), bf16),) + tuple(jax.ShapeDtypeStruct(s, d) for s, d in kept),
        in_specs=[pl.BlockSpec(memory_space=pltpu.SMEM)]
        + [whole((here, width))] * slots
        + [whole(cos.shape), whole(sin.shape), pl.BlockSpec((here, 1), lambda g: (0, 0))]
        + [part(a) for a in (*saved, do)],
        out_specs=(pl.BlockSpec((pieces, 1, width // pieces, span), lambda g: (0, g, 0, 0)),) + tuple(whole(s) for s, _ in kept),
        scratch_shapes=[
            pltpu.VMEM((width, seq), bf16),
            pltpu.VMEM((256, here), f32),
            pltpu.VMEM((width, span), f32),
            pltpu.VMEM((heads, here, cols), bf16),
            pltpu.VMEM((8, here), f32),
            pltpu.VMEM((TILE, 256), f32),
            pltpu.VMEM((TILE, cols), f32),
        ],
        compiler_params=pltpu.CompilerParams(vmem_limit_bytes=40 << 20),
        cost_estimate=pl.CostEstimate(flops=10 * count << 30, bytes_accessed=6 * count << 20, transcendentals=count << 20),
        name="attn_bwd",
    )(info, *toks, cos, sin, seg, *saved, do)


def token_grads_kernel(info, w, *refs, cols, split):
    dkv, dq, (own, rest) = refs[:split], refs[split : 2 * split], refs[2 * split :]
    here = rest.shape[1]
    width = own.shape[1]
    tiles = here // TILE
    count = pl.num_programs(0) * tiles
    s = pl.program_id(0)
    begin = lax.rem(info[2] + s * tiles, count)
    live = (begin + tiles > info[0]) & (begin < info[1])

    def weight(group, start, stop):
        return w[:, group, :, start:stop].reshape(width, stop - start)

    def keys():
        total, group = jnp.zeros((here, width), f32), 0
        for part in dkv:
            for n in range(part.shape[0]):
                total = total + nt(part[n, :, :256], weight(group, 256, 512)) + nt(part[n, :, 256:], weight(group, 512 + cols, 512 + 2 * cols))
                group += 1
        return total

    @pl.when(jnp.logical_not(live))
    def _():
        rest[0] = jnp.zeros((here, width), bf16)

    @pl.when(live)
    def _():
        rest[0] = keys().astype(bf16)

    @pl.when(s == 0)
    def _():
        total, group = jnp.where(live, keys(), 0.0), 0
        for part in dq:
            for n in range(part.shape[0]):
                total = total + nt(part[n], weight(group, 0, 256))
                group += 1
        own[...] = total


def token_grads(info, w, dkv, dq, cols, slots):
    width = w.shape[0] * w.shape[2]
    here = dq[0].shape[1]

    def slot(array):
        return pl.BlockSpec((array.shape[0], here, array.shape[2]), lambda s: (0, s, 0))

    def whole(shape):
        return pl.BlockSpec(shape, lambda s: (0,) * len(shape))

    return pl.pallas_call(
        functools.partial(token_grads_kernel, cols=cols, split=len(dkv)),
        grid=(slots,),
        out_shape=(jax.ShapeDtypeStruct((here, width), f32), jax.ShapeDtypeStruct((slots, here, width), bf16)),
        in_specs=[pl.BlockSpec(memory_space=pltpu.SMEM), whole(w.shape)] + [slot(a) for a in dkv] + [whole(a.shape) for a in dq],
        out_specs=(whole((here, width)), pl.BlockSpec((1, here, width), lambda s: (s, 0, 0))),
        compiler_params=pltpu.CompilerParams(vmem_limit_bytes=40 << 20),
        cost_estimate=pl.CostEstimate(flops=8 << 30, bytes_accessed=20 << 20, transcendentals=0),
        name="token_grads",
    )(info, w, *dkv, *dq)


def doc_tables(lengths, seq, first, here):
    docs = lengths.shape[0]
    ends = jnp.cumsum(lengths)
    starts = ends - lengths
    place = lax.rem(jnp.arange(seq, dtype=jnp.int32) + first, seq)
    segment = jnp.sum((place[:, None] >= ends[None, :]).astype(jnp.int32), axis=1)
    member = segment[:, None] == jnp.arange(docs, dtype=jnp.int32)[None, :]
    offset = jnp.sum(jnp.where(member, starts[None, :], 0), axis=1)
    position = (place - offset).astype(f32)
    live = ends[docs - 2]
    tops = first + TILE * jnp.arange(here // TILE, dtype=jnp.int32)
    last = jnp.minimum(tops + TILE, live) - 1
    lo = jnp.max(jnp.where(starts[None, :] <= tops[:, None], starts[None, :], 0), axis=1) // TILE
    hi = jnp.minimum(jnp.min(jnp.where(ends[None, :] > last[:, None], ends[None, :], seq), axis=1), live)
    hi = jnp.where(tops < live, (hi + TILE - 1) // TILE, lo)
    span = [jnp.min(jnp.where(hi > lo, lo, seq), keepdims=True), jnp.max(jnp.where(hi > lo, hi, 0), keepdims=True)]
    return segment, position, jnp.concatenate([*span, jnp.reshape(first // TILE, (1,)), lo, hi])


def make_info(tables, me):
    return jnp.concatenate([tables[2], jnp.reshape(me, (1,))]).astype(jnp.int32)


EPSILON = 1e-05
ROWS = 256


def tn(left, right):
    return lax.dot_general(left, right, (((0,), (0,)), ((), ())), preferred_element_type=f32)


def row_mean(values):
    return jnp.mean(values, axis=-1, keepdims=True)


def normalise(values):
    centered = values - row_mean(values)
    inv = lax.rsqrt(row_mean(centered * centered) + EPSILON)
    return centered * inv, inv


def norm_back(upstream, unit, inv, scale):
    scaled = upstream * scale
    return inv * (scaled - row_mean(scaled) - unit * row_mean(scaled * unit))


def ffn_kernel(*refs, slots, pieces, share):
    own, cot, s1, b1, s2, b2, rel, w1_hbm, wown_hbm, w2_hbm = refs[:10]
    layer_out, grad_one, nlow, flow, brt, back, chunk, act_hbm, gg_hbm, ug_hbm = refs[10:20]
    w, wo, ws, g, u, normed, unit1, inv1, acc, small, stage, wsem, psem, osem, ssem = refs[20:]
    tokens, width = own.shape
    heads_cols = rel.shape[2]
    blk = slots * share
    pair = 2 if pieces % 2 == 0 else 1
    steps, wide = pieces // pair, pair * blk
    rows_share = width // pieces

    def load_own(p):
        return pltpu.make_async_copy(wown_hbm.at[p], w.at[p // pair, pl.ds(p % pair * blk, share)], psem.at[p])

    def load(p):
        return pltpu.make_async_copy(w2_hbm.at[p], w.at[p // pair, pl.ds(p % pair * blk + share, blk - share)], wsem.at[p])

    first = pltpu.make_async_copy(w1_hbm.at[:, :, :, pl.ds(512, wo.shape[3])], wo, osem)
    first.start()
    for p in range(pieces):
        load_own(p).start()
        load(p).start()
    first.wait()
    for s in range(slots):
        for p in range(pieces):
            ws[s, p * rows_share : (p + 1) * rows_share, :] = wo[p, s, :, :heads_cols]
    small[...] = jnp.zeros_like(small)

    def head(c, _):
        rows = pl.ds(pl.multiple_of(c * ROWS, ROWS), ROWS)
        h = own[rows, :].astype(f32)
        for s in range(slots):
            h = h + nt(rel[s, rows, :], ws[s])
        unit, inv = normalise(h)
        n = unit * s1[...] + b1[...]
        unit1[rows, :] = unit
        inv1[rows, :] = inv
        normed[rows, :] = n
        nlow[rows, :] = n.astype(bf16)
        acc[rows, :] = n
        return 0

    lax.fori_loop(0, tokens // ROWS, head, 0)

    def out_copy(which, target, p, slot):
        return pltpu.make_async_copy(stage.at[which, slot], target.at[:, pl.ds(pl.multiple_of(p * wide, 128), wide)], ssem.at[which, slot])

    def forward(p, _):
        slot = lax.rem(p, 2)
        cols = pl.ds(pl.multiple_of(p * wide, 128), wide)
        for i in range(pair):
            load_own(p * pair + i).wait()
            load(p * pair + i).wait()

        @pl.when(p >= 2)
        def _():
            out_copy(0, act_hbm, p - 2, slot).wait()

        halves = [slice(i, i + tokens // 2) for i in range(0, tokens, tokens // 2)]
        gates = [nt(nlow[r, :], w[p, :, :width]) for r in halves]
        ups = [nt(nlow[r, :], w[p, :, width : 2 * width]) for r in halves]
        for r, gp, up in zip(halves, gates, ups):
            g[r, cols] = gp
            u[r, cols] = up
            a = (gp * jax.nn.sigmoid(gp) * up).astype(bf16)
            stage[0, slot, r, :] = a
            acc[r, :] += nn(a, w[p, :, 2 * width :])
        out_copy(0, act_hbm, p, slot).start()
        return 0

    lax.fori_loop(0, steps, forward, 0)

    def middle(c, _):
        rows = pl.ds(pl.multiple_of(c * ROWS, ROWS), ROWS)
        unit, inv = normalise(acc[rows, :])
        layer_out[rows, :] = (unit * s2[...] + b2[...]).astype(bf16)
        up = cot[rows, :].astype(f32)
        d = norm_back(up, unit, inv, s2[...])
        small[2:3, :] += jnp.sum(up * unit, axis=0, keepdims=True)
        small[3:4, :] += jnp.sum(up, axis=0, keepdims=True)
        flow[rows, :] = d.astype(bf16)
        acc[rows, :] = d
        return 0

    lax.fori_loop(0, tokens // ROWS, middle, 0)
    for p in range(max(steps - 2, 0), steps):
        out_copy(0, act_hbm, p, p % 2).wait()

    def backward(p, _):
        slot = lax.rem(p, 2)
        cols = pl.ds(pl.multiple_of(p * wide, 128), wide)

        @pl.when(p >= 2)
        def _():
            out_copy(0, gg_hbm, p - 2, slot).wait()
            out_copy(1, ug_hbm, p - 2, slot).wait()

        halves = [slice(i, i + tokens // 2) for i in range(0, tokens, tokens // 2)]
        outer = [nt(flow[r, :], w[p, :, 2 * width :]) for r in halves]
        for r, da in zip(halves, outer):
            gp, up = g[r, cols], u[r, cols]
            sig = jax.nn.sigmoid(gp)
            both = da * sig
            dg = (both * up * (1.0 + gp * (1.0 - sig))).astype(bf16)
            du = (both * gp).astype(bf16)
            stage[0, slot, r, :] = dg
            stage[1, slot, r, :] = du
            acc[r, :] += nn(dg, w[p, :, :width]) + nn(du, w[p, :, width : 2 * width])
        out_copy(0, gg_hbm, p, slot).start()
        out_copy(1, ug_hbm, p, slot).start()
        return 0

    lax.fori_loop(0, steps, backward, 0)

    def tail(c, _):
        rows = pl.ds(pl.multiple_of(c * ROWS, ROWS), ROWS)
        up, unit = acc[rows, :], unit1[rows, :]
        d = norm_back(up, unit, inv1[rows, :], s1[...])
        small[0:1, :] += jnp.sum(up * unit, axis=0, keepdims=True)
        small[1:2, :] += jnp.sum(up, axis=0, keepdims=True)
        grad_one[rows, :] = d
        low = d.astype(bf16)
        brt[:, rows] = d.T.astype(bf16)
        for s in range(slots):
            back[s, rows, :] = nn(low, ws[s]).astype(bf16)
        return 0

    lax.fori_loop(0, tokens // ROWS, tail, 0)
    chunk[...] = jnp.zeros_like(chunk)
    room = chunk.shape[2]
    each = 4 * width // pieces // room
    for n in range(pieces * each):
        j, lane = divmod(n * room, width)
        chunk[n // each, n % each : n % each + 1, :] = small[j : j + 1, lane : lane + room]
    for p in range(max(steps - 2, 0), steps):
        out_copy(0, gg_hbm, p, p % 2).wait()
        out_copy(1, ug_hbm, p, p % 2).wait()


def ffn_layer(own, cot, norms, rel, w1, w_own, w2, room):
    slots, tokens, cols = rel.shape
    width = own.shape[1]
    pieces, share = w_own.shape[:2]
    units = pieces * slots * share
    pair = 2 if pieces % 2 == 0 else 1
    vm, hbm = pl.BlockSpec(memory_space=pltpu.VMEM), pl.BlockSpec(memory_space=pl.ANY)
    wide = jax.ShapeDtypeStruct((tokens, width), bf16)
    hidden = jax.ShapeDtypeStruct((tokens, units), bf16)
    return pl.pallas_call(
        functools.partial(ffn_kernel, slots=slots, pieces=pieces, share=share),
        out_shape=(wide, jax.ShapeDtypeStruct((tokens, width), f32), wide, wide, jax.ShapeDtypeStruct((width, tokens), bf16))
        + (jax.ShapeDtypeStruct((slots, tokens, cols), bf16), jax.ShapeDtypeStruct((pieces, 16, room), f32), hidden, hidden, hidden),
        in_specs=[vm] * 7 + [hbm] * 3,
        out_specs=(vm,) * 7 + (hbm,) * 3,
        scratch_shapes=[
            pltpu.VMEM((pieces // pair, pair * slots * share, 3 * width), bf16),
            pltpu.VMEM((pieces, slots, width // pieces, 256), bf16),
            pltpu.VMEM((slots, width, cols), bf16),
            pltpu.VMEM((tokens, units), f32),
            pltpu.VMEM((tokens, units), f32),
            pltpu.VMEM((tokens, width), f32),
            pltpu.VMEM((tokens, width), f32),
            pltpu.VMEM((tokens, 1), f32),
            pltpu.VMEM((tokens, width), f32),
            pltpu.VMEM((8, width), f32),
            pltpu.VMEM((2, 2, tokens, pair * slots * share), bf16),
            pltpu.SemaphoreType.DMA((pieces,)),
            pltpu.SemaphoreType.DMA((pieces,)),
            pltpu.SemaphoreType.DMA,
            pltpu.SemaphoreType.DMA((2, 2)),
        ],
        compiler_params=pltpu.CompilerParams(vmem_limit_bytes=60 << 20),
        cost_estimate=pl.CostEstimate(flops=16 << 30, bytes_accessed=30 << 20, transcendentals=3 << 20),
        name="ffn_layer",
    )(own, cot, *norms, rel, w1, w_own, w2)


def wgrad_kernel(*refs, slots, share, add):
    gg, ug, act, brt, nlow, flow, rel, small = refs[1:9]
    got = refs[9] if add else None
    width = nlow.shape[1]
    cols = rel.shape[2]
    edge = 3 * width + cols
    blk = slots * share
    out = refs[-1] if add else refs[-1].at[0]
    room = out.shape[1] - edge

    def put(rows, lanes, value):
        if add:
            value = value + got[0, rows, lanes].astype(f32)
        out[rows, lanes] = value.astype(bf16)

    terms = [tn(gg[...], nlow[...]), tn(ug[...], nlow[...]), tn(act[...], flow[...])]
    for s in range(slots):
        place = lax.rem(refs[0][1] - s + slots, slots)
        rows = pl.ds(pl.multiple_of(place * share, 32 if share % 32 == 0 else 4), share)
        for i in range(3):
            put(rows, slice(i * width, (i + 1) * width), terms[i][s * share : (s + 1) * share])
        put(rows, slice(3 * width, edge), nn(brt[...], rel[s]))
        put(rows, slice(edge, edge + room), jnp.concatenate([small[0], jnp.zeros((share - 16, room), f32)], axis=0))
    if add:
        first, second, rest = refs[10:13]
        top = first.shape[0]

        @pl.when(pl.program_id(0) == 0)
        def _():
            first[...] = out[:top, :]

        @pl.when(pl.program_id(0) == 1)
        def _():
            second[...] = out[:top, :]

        rest[0] = out[top:, :]


def wgrad(me, start, gg, ug, act, brt, nlow, flow, rel, small, got, pieces, share, span):
    slots = rel.shape[0]
    tokens, width = nlow.shape
    blk = slots * share
    top = slots // 2 * share

    def piece(i, me):
        return jnp.bitwise_xor(2 * i + start, me[0])

    both = pl.BlockSpec((1, blk, span), lambda i, me: (i, 0, 0))
    in_specs = [pl.BlockSpec((tokens, blk), lambda i, me: (0, piece(i, me)))] * 3
    in_specs += [pl.BlockSpec((width // pieces, tokens), lambda i, me: (piece(i, me), 0))]
    in_specs += [pl.BlockSpec((tokens, width), lambda i, me: (0, 0))] * 2
    in_specs += [pl.BlockSpec(rel.shape, lambda i, me: (0, 0, 0)), pl.BlockSpec((1,) + small.shape[1:], lambda i, me: (piece(i, me), 0, 0))]
    args = [stay(gg), stay(ug), stay(act), brt, nlow, flow, rel, small]
    if got is None:
        out_shape, out_specs, scratch = jax.ShapeDtypeStruct((2, blk, span), bf16), both, []
    else:
        in_specs.append(both)
        args.append(got)
        half = jax.ShapeDtypeStruct((top, span), bf16)
        out_shape = (half, half, jax.ShapeDtypeStruct((2, blk - top, span), bf16))
        fixed = pl.BlockSpec((top, span), lambda i, me: (0, 0))
        out_specs = (fixed, fixed, pl.BlockSpec((1, blk - top, span), lambda i, me: (i, 0, 0)))
        scratch = [pltpu.VMEM((blk, span), bf16)]
    return pl.pallas_call(
        functools.partial(wgrad_kernel, slots=slots, share=share, add=got is not None),
        out_shape=out_shape,
        grid_spec=pltpu.PrefetchScalarGridSpec(num_scalar_prefetch=1, grid=(2,), in_specs=in_specs, out_specs=out_specs, scratch_shapes=scratch),
        compiler_params=pltpu.CompilerParams(vmem_limit_bytes=24 << 20),
        cost_estimate=pl.CostEstimate(flops=2 << 30, bytes_accessed=10 << 20, transcendentals=0),
        name="wgrad",
    )(me, *args)


def final_kernel(gate, up, down, out_part, query, key, value, edge, gate_up_sum, down_sum, out_sum, qkv_sum, small_sum, *, heads, pieces, share, room):
    cols = heads * HD
    gate_up_sum[:, 0, :] = gate[...].astype(f32).T
    gate_up_sum[:, 1, :] = up[...].astype(f32).T
    down_sum[...] = down[...].astype(f32)
    out_sum[...] = out_part[...].astype(f32).T[:cols]
    for k, source in enumerate((query, key)):
        turned = source[...].astype(f32).T
        for h in range(heads):
            for half in range(2):
                start = 128 * half + HALF * h
                qkv_sum[k, HD * h + HALF * half : HD * h + HALF * (half + 1), :] = turned[start : start + HALF, :]
    qkv_sum[2, :, :] = value[...].astype(f32).T[:cols]

    @pl.when(pl.program_id(0) == 0)
    def _():
        width = small_sum.shape[1]
        each = 4 * width // pieces // room
        for n in range(pieces * each):
            j, lane = divmod(n * room, width)
            row = n // each * share + n % each
            base = row // 16 * 16
            block = edge[base : base + 16, 128 - room :].astype(f32)
            small_sum[j : j + 1, lane : lane + room] = block[row - base : row - base + 1, :]


def final_sums(main, width, span, heads, pieces):
    units = main.shape[0]
    lanes = 128
    steps = width // lanes
    cols = heads * HD
    room = span - 3 * width - cols
    tall = units // steps

    def band(first, size):
        return pl.BlockSpec((tall, size), lambda i, n=first // size: (i, n))

    in_specs = [pl.BlockSpec((units, lanes), lambda i: (0, i)), pl.BlockSpec((units, lanes), lambda i: (0, i + steps))]
    in_specs += [band(2 * width, width), band(3 * width, 256)] + [band(span + 256 * k, 256) for k in range(3)]
    in_specs += [pl.BlockSpec((units, lanes), lambda i: (0, span // lanes - 1))]
    return pl.pallas_call(
        functools.partial(final_kernel, heads=heads, pieces=pieces, share=units // pieces, room=room),
        grid=(steps,),
        out_shape=(
            jax.ShapeDtypeStruct((width, 2, units), f32),
            jax.ShapeDtypeStruct((units, width), f32),
            jax.ShapeDtypeStruct((cols, width), f32),
            jax.ShapeDtypeStruct((3, cols, width), f32),
            jax.ShapeDtypeStruct((4, width), f32),
        ),
        in_specs=in_specs,
        out_specs=(
            pl.BlockSpec((lanes, 2, units), lambda i: (i, 0, 0)),
            pl.BlockSpec((tall, width), lambda i: (i, 0)),
            pl.BlockSpec((cols, tall), lambda i: (0, i)),
            pl.BlockSpec((3, cols, tall), lambda i: (0, 0, i)),
            pl.BlockSpec((4, width), lambda i: (0, 0)),
        ),
        cost_estimate=pl.CostEstimate(flops=1 << 20, bytes_accessed=15 << 20, transcendentals=0),
        name="final_sums",
    )(*[main] * 8)


ROPE_BASE = 1000.0


def rotate_axis(size, step):
    return [(i, (i + step) % size) for i in range(size)]


def line_axis(size, step):
    return [(i, i + step) for i in range(size) if 0 <= i + step < size]


def flip_axis(size, bit):
    return [(i, i ^ bit) for i in range(size)]


def after(value, *others):
    return lax.optimization_barrier((value, *others))[0]


def low_sum(left, right):
    return (left.astype(f32) + right.astype(f32)).astype(bf16)


def body(
    dp_size,
    tp_size,
    tokens,
    lengths,
    w_qkv,
    w_out,
    norm1_scale,
    norm1_shift,
    w_gate_up,
    w_down,
    norm2_scale,
    norm2_shift,
    cotangent,
):
    own = tokens[0]
    rows_here, width = own.shape
    docs = lengths.shape[1]
    seq = rows_here * tp_size
    cols_here = w_qkv.shape[2]
    heads = cols_here // HD
    units = w_gate_up.shape[2]
    pieces = min(dp_size, 8)
    groups = None if pieces == dp_size else [list(range(i, i + pieces)) for i in range(0, dp_size, pieces)]
    share = units // pieces
    rows_share = width // pieces
    span = -(-(3 * width + cols_here) // 128) * 128
    me = lax.rem(lax.axis_index("dp"), pieces)
    z = lax.axis_index("tensor")

    def flip(array, bit):
        return lax.ppermute(array, "dp", flip_axis(dp_size, bit))

    def shift(array, step):
        return lax.ppermute(array, "tensor", rotate_axis(tp_size, step))

    def along(array, step):
        return lax.ppermute(array, "tensor", line_axis(tp_size, step))

    def gather_dp(array):
        return lax.all_gather(array, "dp", axis=0, axis_index_groups=groups)

    def rope_order(matrix):
        halves = matrix.reshape(rows_share, heads, 2, HALF).transpose(0, 2, 1, 3).reshape(rows_share, 2, heads * HALF)
        return jnp.pad(halves, ((0, 0), (0, 0), (0, 128 - heads * HALF))).reshape(rows_share, 256)

    qkv_slice = lax.dynamic_slice_in_dim(w_qkv, me * rows_share, rows_share, 0)
    out_slice = lax.dynamic_slice_in_dim(w_out, me * rows_share, rows_share, 1)
    piece_one = jnp.concatenate([rope_order(qkv_slice[:, 0]), rope_order(qkv_slice[:, 1]), out_slice.T, qkv_slice[:, 2]], axis=1)
    gate_slice = lax.dynamic_slice_in_dim(w_gate_up, me * share, share, 2)
    down_slice = lax.dynamic_slice_in_dim(w_down, me * share, share, 0)
    piece_two = jnp.concatenate([gate_slice[:, 0].T, gate_slice[:, 1].T, down_slice], axis=1)
    piece_one, piece_two = lax.optimization_barrier((piece_one, piece_two))
    ones = [piece_one] + [shift(piece_one, s) for s in range(1, tp_size)]
    piece_two = after(piece_two, *ones[1:])
    twos = [shift(piece_two, s) for s in range(1, tp_size)]
    w1 = gather_dp(jnp.stack(ones))
    row_lengths, gate_up_late, down_late = after(lengths[0], ones[-1]), after(w_gate_up, ones[-1]), after(w_down, ones[-1])
    w_own = jnp.concatenate([gate_up_late[:, 0].T, gate_up_late[:, 1].T, down_late], axis=1).reshape(pieces, share, 3 * width)

    tables = doc_tables(row_lengths, seq, z * rows_here, rows_here)
    segment, position = tables[:2]
    info = make_info(tables, me)
    inverse = ROPE_BASE ** (-2.0 * lax.rem(jnp.arange(128), HALF).astype(f32) / HD)
    angles = position[:, None] * inverse[None, :]
    cosine, sine = jnp.cos(angles), jnp.sin(angles)
    seg_col = segment[:, None]

    twos, cosine, sine, seg_col, info, w_own = lax.optimization_barrier((twos, cosine, sine, seg_col, info, w_own))
    w2 = gather_dp(jnp.concatenate(twos, axis=0))

    own_late = after(own, *ones[1:])
    before, behind = along(own_late, 1), along(own_late, -1)

    *held, qh = project(own, w1, cosine, sine, seg_col, docs, heads, 0, tp_size)
    held, before, behind = lax.optimization_barrier((held, before, behind))
    before2, behind2 = along(before, 1), along(behind, -1)
    held = project(behind, w1, cosine, sine, seg_col, docs, heads, 1, tp_size, held)
    held = project(before, w1, cosine, sine, seg_col, docs, heads, 3, tp_size, held)
    held, behind2, before2 = lax.optimization_barrier((held, behind2, before2))
    toks = [own, behind, jnp.where(z < tp_size // 2, behind2, before2), before]
    held = project(toks[2], w1, cosine, sine, seg_col, docs, heads, 2, tp_size, held)
    lse, rel = attn_fwd(info, seg_col, qh, held[0], held[2], docs)
    saved = (qh, held[0].reshape(tp_size, seq, -1), held[1].reshape(tp_size, seq, -1), lse, rel)
    norms = [v.reshape(1, width) for v in (norm1_scale, norm1_shift, norm2_scale, norm2_shift)]
    room = span - 3 * width - cols_here
    layer_out, grad_one, nlow, flow, brt, back, chunk, act, gg, ug = ffn_layer(own, cotangent[0], norms, rel, w1, w_own, w2, room)

    half = tp_size // 2

    me_array = jnp.stack([me, z]).astype(jnp.int32)
    fixed = (gg, ug, act, brt, nlow, flow, rel, chunk)
    far_sent = wgrad(me_array, 5, *fixed, None, pieces, share, span)
    near_sent = wgrad(after(me_array, far_sent), 1, *fixed, None, pieces, share, span)
    far_keep, far_give, far_rest = wgrad(after(me_array, near_sent), 4, *fixed, flip(far_sent, 1), pieces, share, span)
    near_keep, near_give, near_rest = wgrad(after(me_array, far_rest), 0, *fixed, flip(near_sent, 1), pieces, share, span)

    back, near_give = lax.optimization_barrier((back, near_give))
    got = [flip(far_give, 2), flip(far_rest, 4), flip(near_give, 2)]
    backward = functools.partial(attn_bwd, info, toks, cosine, sine, seg_col, saved)
    cut = tp_size - 1
    dw_low, kv_low, q_low = backward(back, docs, heads, pieces, 0, cut)
    got, dw_low, back_late = lax.optimization_barrier((got, dw_low, back))
    next_b = low_sum(near_rest, got[1])
    give_a, next_a = low_sum(far_keep, got[0]), low_sum(near_keep, got[2])
    back_late, next_a, give_a, next_b = lax.optimization_barrier((back_late, next_a, give_a, next_b))
    got_a, got_b, got_low = flip(give_a, 4), flip(next_b[1], 2), flip(dw_low.reshape((pieces // 2, 2) + dw_low.shape[1:])[:, 1], 1)
    dw_high, kv_high, q_high = backward(back_late, docs, heads, pieces, cut, tp_size)
    got_a, got_b, got_low, dw_high, kv_high = lax.optimization_barrier((got_a, got_b, got_low, dw_high, kv_high))
    parts_two = jnp.concatenate([low_sum(next_a, got_a), low_sum(next_b[0], got_b)], axis=0)
    share_two = lax.psum_scatter(parts_two, "tensor", scatter_dimension=0, tiled=True)

    def pairs_of(array):
        return array.reshape((pieces // 2, 2) + array.shape[1:])

    got_high = flip(pairs_of(dw_high)[:, 1], 1)
    dx_own, dx = token_grads(info, w1, (kv_low, kv_high), (q_low, q_high), cols_here, tp_size)
    low = low_sum(pairs_of(dw_low)[:, 0], got_low).reshape((2, 2) + dw_low.shape[1:])
    got_a = flip(low[:, 1, :half], 2)
    high = low_sum(pairs_of(dw_high)[:, 0], got_high).reshape((2, 2) + dw_high.shape[1:])
    high = jnp.concatenate([low[:, :, half:], high], axis=2)
    got_b = flip(high[1], 4)
    next_a, next_b = low_sum(low[:, 0, :half], got_a), low_sum(high[0], got_b)
    got_a, got_b = flip(next_a[1], 4), flip(next_b[1], 2)

    def by_slot(low, high):
        low, high = low.reshape(half, -1, low.shape[-1]), high.reshape(tp_size - half, -1, high.shape[-1])
        return [low[i] for i in range(half)] + [high[i] for i in range(tp_size - half)]

    def total(own_part, moved):
        return functools.reduce(lambda x, y: x + y.astype(f32), moved, own_part.astype(f32)).astype(bf16)

    parts_one = by_slot(low_sum(next_a[0], got_a), low_sum(next_b[0], got_b))
    moved_one = [shift(parts_one[s], -s) for s in range(1, tp_size)]
    moved_one, dx = lax.optimization_barrier((moved_one, dx))
    share_one = total(parts_one[0], moved_one)
    from_left = lax.ppermute(dx[2], "tensor", [(i, i + 1) for i in range(half)])
    from_right = lax.ppermute(dx[2], "tensor", [(i + half, i + half - 1) for i in range(half)])
    near_right, near_left = low_sum(dx[1], from_left), low_sum(dx[3], from_right)
    from_before, from_behind = along(near_right, 1), along(near_left, -1)

    def finish(array):
        if groups is not None:
            across = [[g * pieces + i for g in range(dp_size // pieces)] for i in range(pieces)]
            array = lax.psum(array.astype(f32), "dp", axis_index_groups=across).astype(bf16)
        return gather_dp(array)

    main = finish(jnp.concatenate([share_two, share_one], axis=1)).reshape(units, -1)
    gate_up_sum, down_sum, out_sum, qkv_turned, small_out = final_sums(main, width, span, heads, pieces)
    qkv_sum = qkv_turned.transpose(2, 0, 1)
    from_before, from_behind, small_out = lax.optimization_barrier((from_before, from_behind, small_out))
    input_grad = grad_one + dx_own + from_before.astype(f32) + from_behind.astype(f32)
    return (
        layer_out[None],
        input_grad[None],
        qkv_sum,
        out_sum,
        small_out[0],
        small_out[1],
        gate_up_sum,
        down_sum,
        small_out[2],
        small_out[3],
    )


def solution(mesh):
    in_specs = (
        P("dp", "tensor", None),
        P("dp", None),
        P(None, None, "tensor"),
        P("tensor", None),
        P(),
        P(),
        P(None, None, "tensor"),
        P("tensor", None),
        P(),
        P(),
        P("dp", "tensor", None),
    )
    out_specs = (
        P("dp", "tensor", None),
        P("dp", "tensor", None),
        P(None, None, "tensor"),
        P("tensor", None),
        P(),
        P(),
        P(None, None, "tensor"),
        P("tensor", None),
        P(),
        P(),
    )
    return jax.shard_map(
        functools.partial(body, mesh.shape["dp"], mesh.shape["tensor"]),
        mesh=mesh,
        in_specs=in_specs,
        out_specs=out_specs,
        check_vma=False,
    )
```

```python
import functools

import jax
import jax.numpy as jnp
from jax import lax
from jax.experimental import pallas as pl
from jax.experimental.pallas import tpu as pltpu
from jax.sharding import PartitionSpec as P

TILE = 256
HALF = 32
HD = 64
BIG = 1e30
f32, bf16 = jnp.float32, jnp.bfloat16


def nt(a, b):
    return lax.dot_general(a, b, (((1,), (1,)), ((), ())), preferred_element_type=f32)


def nn(a, b):
    return jnp.dot(a, b, preferred_element_type=f32)


def stay(array):
    return pltpu.with_memory_space_constraint(array, pltpu.HBM)


def tile_rows(tile, base, count):
    return pl.ds(pl.multiple_of(lax.rem(tile - base + count, count) * TILE, TILE), TILE)


def over_tiles(info, lo, hi, tiles, scan):
    def one(t, _):
        live = [(t >= info[3 + u]) & (t < info[3 + tiles + u]) for u in range(tiles)]
        every = functools.reduce(jnp.logical_and, live)

        @pl.when(every)
        def _():
            scan(t, slice(0, tiles * TILE))

        @pl.when(jnp.logical_not(every))
        def _():
            def single(u, _):
                @pl.when((t >= info[3 + u]) & (t < info[3 + tiles + u]))
                def _():
                    scan(t, pl.ds(pl.multiple_of(u * TILE, TILE), TILE))

                return 0

            lax.fori_loop(0, tiles, single, 0)

        return 0

    lax.fori_loop(lo, hi, one, 0)


def project_kernel(*refs, docs, heads, slot):
    tok, w, cos, sin, seg = refs[:5]
    outs = refs[5:] if slot == 0 else refs[8:]
    ka, va, vt = outs[:3]
    here, width = tok.shape
    used = heads * HALF
    cols = heads * HD
    lane = lax.broadcasted_iota(jnp.int32, (TILE, 128), 1)
    filler = lax.broadcasted_iota(jnp.int32, (80 - HD, here), 0)

    def weight(start, stop):
        return w[:, 0, :, start:stop].reshape(width, stop - start)

    for h in range(heads):
        vt[0, 0, 80 * h + HD : 80 * (h + 1), :] = jnp.where(filler == 0, 1.0, 0.0).astype(bf16)

    def tile(c, _):
        rows = pl.ds(pl.multiple_of(c * TILE, TILE), TILE)
        x = tok[rows, :]
        co, si = cos[rows, :], sin[rows, :]
        hit = (lane - used) == seg[rows, :]
        if slot == 0:
            p = nn(x, weight(0, 256))
            ra = (p[:, :128] * co - p[:, 128:] * si).astype(bf16).astype(f32) * HD**-0.5
            rb = (p[:, 128:] * co + p[:, :128] * si).astype(bf16).astype(f32) * HD**-0.5
            for h in range(heads):
                keep = (lane >= HALF * h) & (lane < HALF * (h + 1))
                outs[3][0, h, rows, :128] = jnp.where(keep, ra, jnp.where(hit, -BIG, 0.0)).astype(bf16)
                outs[3][0, h, rows, 128:] = jnp.where(keep, rb, 0.0).astype(bf16)
        p = nn(x, weight(256, 512))
        other = (lane >= used) & (lane < used + docs) & jnp.logical_not(hit)
        ra, rb = p[:, :128] * co - p[:, 128:] * si, p[:, 128:] * co + p[:, :128] * si
        ka[0, 0, rows, :128] = jnp.where(lane < used, ra, jnp.where(other, 1.0, 0.0)).astype(bf16)
        ka[0, 0, rows, 128:] = rb.astype(bf16)
        v = nn(x, weight(512 + cols, 512 + 2 * cols))
        va[0, 0, rows, :] = v.astype(bf16)
        turned = v.T.astype(bf16)
        for h in range(heads):
            vt[0, 0, 80 * h : 80 * h + HD, rows] = turned[HD * h : HD * (h + 1), :]
        return 0

    lax.fori_loop(0, here // TILE, tile, 0)


def project(tok, w, cos, sin, seg, docs, heads, slot, slots, held=()):
    here, width = tok.shape
    cols = heads * HD
    shapes = [(here, 256), (here, cols), (80 * heads, here)]
    out_shape = [pltpu.HBM((slots, slots) + s, bf16) for s in shapes]
    out_specs = [pl.BlockSpec((1, 1) + s, lambda g: (g, slot, 0, 0)) for s in shapes]
    if slot == 0:
        out_shape.append(pltpu.HBM((slots, heads, here, 256), bf16))
        out_specs.append(pl.BlockSpec((1, heads, here, 256), lambda g: (g, 0, 0, 0)))
    rows = pl.BlockSpec((here, cos.shape[1]), lambda g: (slot, 0))
    return pl.pallas_call(
        functools.partial(project_kernel, docs=docs, heads=heads, slot=slot),
        grid=(slots,),
        out_shape=tuple(out_shape),
        in_specs=[
            pl.BlockSpec((here, width), lambda g: (0, 0)),
            pl.BlockSpec((w.shape[0], 1) + w.shape[2:], lambda g: (0, g, 0, 0)),
            rows,
            rows,
            pl.BlockSpec((here, 1), lambda g: (slot, 0)),
        ]
        + [pl.BlockSpec(memory_space=pl.ANY)] * len(held),
        out_specs=tuple(out_specs),
        input_output_aliases={5 + n: n for n in range(len(held))},
        compiler_params=pltpu.CompilerParams(vmem_limit_bytes=20 << 20),
        cost_estimate=pl.CostEstimate(flops=2 << 30, bytes_accessed=8 << 20, transcendentals=0),
        name="project",
    )(tok, w, cos, sin, seg, *[stay(a) for a in held])


def attn_fwd_kernel(info, seg, qh, ka, vt, lse, mixed, acc, top, *, docs, heads):
    here = qh.shape[2]
    tiles = here // TILE
    count = ka.shape[1] * tiles
    lo, hi, base = info[0], info[1], info[2]
    acc[...] = jnp.zeros_like(acc)
    top[...] = jnp.full_like(top, -3e38)

    def scan(t, mine):
        c = lax.rem(t - base + count, count)
        slot = c // tiles
        rows = pl.ds(pl.multiple_of(lax.rem(c, tiles) * TILE, TILE), TILE)
        kk = ka[0, slot, rows, :]
        scores = [nt(kk, qh[0, h, mine, :]) for h in range(heads)]
        olds = [top[h : h + 1, mine] for h in range(heads)]
        news = [jnp.maximum(olds[h], jnp.max(scores[h], axis=0, keepdims=True)) for h in range(heads)]
        probs = [jnp.exp(scores[h] - news[h]).astype(bf16) for h in range(heads)]
        adds = [nn(vt[0, slot, 80 * h : 80 * h + 80, rows], probs[h]) for h in range(heads)]
        for h in range(heads):
            top[h : h + 1, mine] = news[h]
            acc[h, :, mine] = acc[h, :, mine] * jnp.exp(olds[h] - news[h]) + adds[h]

    over_tiles(info, lo, hi, tiles, scan)
    good = seg[...] < docs - 1
    total = [jnp.where(top[h : h + 1, :] > -1e29, acc[h, HD : HD + 1, :], 1.0) for h in range(heads)]
    outs = jnp.concatenate([acc[h, :HD, :] / total[h] for h in range(heads)], axis=0).T
    mixed[0] = jnp.where(good, outs, 0.0).astype(bf16)
    stats = [top[h : h + 1, :] + jnp.log(total[h]) for h in range(heads)]
    lse[0] = jnp.concatenate(stats + [jnp.zeros((8 - heads, here), f32)], axis=0)


def attn_fwd(info, seg, qh, ka, vt, docs):
    slots, heads, here = qh.shape[:3]
    cols = heads * HD

    def part(shape):
        return pl.BlockSpec((1,) + shape[1:], lambda g: (g,) + (0,) * (len(shape) - 1))

    shapes = [((slots, 8, here), f32), ((slots, here, cols), bf16)]
    return pl.pallas_call(
        functools.partial(attn_fwd_kernel, docs=docs, heads=heads),
        grid=(slots,),
        out_shape=tuple(jax.ShapeDtypeStruct(s, d) for s, d in shapes),
        in_specs=[pl.BlockSpec(memory_space=pltpu.SMEM), pl.BlockSpec((here, 1), lambda g: (0, 0))] + [part(a.shape) for a in (qh, ka, vt)],
        out_specs=tuple(part(s) for s, _ in shapes),
        scratch_shapes=[pltpu.VMEM((heads, 80, here), f32), pltpu.VMEM((8, here), f32)],
        compiler_params=pltpu.CompilerParams(vmem_limit_bytes=24 << 20),
        cost_estimate=pl.CostEstimate(flops=12 << 30, bytes_accessed=12 << 20, transcendentals=4 << 20),
        name="attn_fwd",
    )(info, seg, stay(qh), stay(ka), stay(vt))


def attn_bwd_kernel(info, *refs, docs, heads, slots, pieces):
    toks = refs[:slots]
    cos, sin, seg, qh, ka, va, lse, mixed, do = refs[slots : slots + 9]
    dw, dkv, dq, tokt, dqt, dwa, doh, delta, dka, dva = refs[slots + 9 :]
    here, width = toks[0].shape
    seq = here * slots
    count = seq // TILE
    used = heads * HALF
    cols = heads * HD
    tiles = here // TILE
    lo, hi, base, me = info[0], info[1], info[2], info[3 + 2 * tiles]

    @pl.when(pl.program_id(0) == 0)
    def _():
        dkv[...] = jnp.zeros_like(dkv)
        dwa[:, 512 + cols :] = jnp.zeros((width, dwa.shape[1] - 512 - cols), f32)
        for s in range(slots):
            for c in range(here // TILE):
                start = s * here + c * TILE
                tokt[:, start : start + TILE] = toks[s][c * TILE : (c + 1) * TILE, :].astype(f32).T.astype(bf16)

    g = pl.program_id(0)

    wlane = lax.broadcasted_iota(jnp.int32, (here, cols), 1)
    lane = lax.broadcasted_iota(jnp.int32, (TILE, 128), 1)
    dqt[...] = jnp.zeros_like(dqt)
    d = jnp.where(seg[:here, :] < docs - 1, do[0].astype(f32), 0.0)
    prod = d * mixed[0].astype(f32)
    prod_high = prod.astype(bf16)
    prod_low = (prod - prod_high.astype(f32)).astype(bf16)
    pick = (lax.broadcasted_iota(jnp.int32, (8, cols), 1) // HD == lax.broadcasted_iota(jnp.int32, (8, cols), 0)).astype(bf16)
    delta[...] = nt(pick, prod_high) + nt(pick, prod_low)
    for h in range(heads):
        doh[h] = jnp.where((wlane >= HD * h) & (wlane < HD * (h + 1)), d, 0.0).astype(bf16)

    def unrotate(a, b, rows):
        a, b = a.astype(bf16).astype(f32), b.astype(bf16).astype(f32)
        co, si = cos[rows, :], sin[rows, :]
        keep = lane < used
        both = [jnp.where(keep, a * co + b * si, 0.0), jnp.where(keep, b * co - a * si, 0.0)]
        return jnp.concatenate(both, axis=1).astype(bf16)

    def scan(t, mine):
        rows = tile_rows(t, base, count)
        kk, vv = ka[0, rows, :], va[0, rows, :]
        kt = kk.astype(f32).T.astype(bf16)
        qs, dd = [qh[0, h, mine, :] for h in range(heads)], [doh[h, mine, :] for h in range(heads)]
        probs = [jnp.exp(nt(kk, qs[h]) - lse[0, h : h + 1, mine]) for h in range(heads)]
        ds = [(probs[h] * (nt(vv, dd[h]) - delta[h : h + 1, mine])).astype(bf16) for h in range(heads)]
        dva[...] += sum(nn(probs[h].astype(bf16), dd[h]) for h in range(heads))
        dka[...] += sum(nn(ds[h], qs[h]) for h in range(heads))
        for h in range(heads):
            kth = jnp.concatenate([kt[HALF * h : HALF * (h + 1)], kt[128 + HALF * h : 128 + HALF * (h + 1)]], axis=0)
            g = nn(kth, ds[h])
            dqt[HALF * h : HALF * (h + 1), mine] += g[:HALF]
            dqt[128 + HALF * h : 128 + HALF * (h + 1), mine] += g[HALF:]

    def k_tile(t, _):
        rows = tile_rows(t, base, count)
        dka[...] = jnp.zeros_like(dka)
        dva[...] = jnp.zeros_like(dva)
        over_tiles(info, t, t + 1, tiles, scan)
        dkv[g, rows, :256] = unrotate(dka[:, :128], dka[:, 128:], rows)
        dkv[g, rows, 256:] = dva[...].astype(bf16)
        return 0

    lax.fori_loop(lo, hi, k_tile, 0)
    for c in range(here // TILE):
        rows = slice(c * TILE, (c + 1) * TILE)
        gq = dqt[:, rows].T * HD**-0.5
        dq[g, rows, :] = unrotate(gq[:, :128], gq[:, 128:], rows)
    dwa[:, :256] = nn(tokt[:, :here], dq[g])
    dwa[:, 256 : 512 + cols] = nn(tokt[...], dkv[g])
    share = width // pieces
    for r in range(pieces):
        p = jnp.bitwise_xor(me, r)
        dw[r, 0] = dwa[pl.ds(pl.multiple_of(p * share, 8), share), :].astype(bf16)


def attn_bwd(info, toks, cos, sin, seg, saved, do, docs, heads, pieces, start, stop):
    slots = len(toks)
    here, width = toks[0].shape
    seq = here * slots
    cols = heads * HD
    span = -(-(512 + cols) // 128) * 128
    count = stop - start

    def whole(shape):
        return pl.BlockSpec(shape, lambda g: (0,) * len(shape))

    def part(array):
        return pl.BlockSpec((1,) + array.shape[1:], lambda g: (g + start,) + (0,) * (array.ndim - 1))

    kept = [((count, seq, 256 + cols), bf16), ((count, here, 256), bf16)]
    return pl.pallas_call(
        functools.partial(attn_bwd_kernel, docs=docs, heads=heads, slots=slots, pieces=pieces),
        grid=(count,),
        out_shape=(jax.ShapeDtypeStruct((pieces, count, width // pieces, span), bf16),) + tuple(jax.ShapeDtypeStruct(s, d) for s, d in kept),
        in_specs=[pl.BlockSpec(memory_space=pltpu.SMEM)]
        + [whole((here, width))] * slots
        + [whole(cos.shape), whole(sin.shape), pl.BlockSpec((here, 1), lambda g: (0, 0))]
        + [part(a) for a in (*saved, do)],
        out_specs=(pl.BlockSpec((pieces, 1, width // pieces, span), lambda g: (0, g, 0, 0)),) + tuple(whole(s) for s, _ in kept),
        scratch_shapes=[
            pltpu.VMEM((width, seq), bf16),
            pltpu.VMEM((256, here), f32),
            pltpu.VMEM((width, span), f32),
            pltpu.VMEM((heads, here, cols), bf16),
            pltpu.VMEM((8, here), f32),
            pltpu.VMEM((TILE, 256), f32),
            pltpu.VMEM((TILE, cols), f32),
        ],
        compiler_params=pltpu.CompilerParams(vmem_limit_bytes=40 << 20),
        cost_estimate=pl.CostEstimate(flops=10 * count << 30, bytes_accessed=6 * count << 20, transcendentals=count << 20),
        name="attn_bwd",
    )(info, *toks, cos, sin, seg, *saved, do)


def token_grads_kernel(info, w, *refs, cols, split):
    dkv, dq, (own, rest) = refs[:split], refs[split : 2 * split], refs[2 * split :]
    here = rest.shape[1]
    width = own.shape[1]
    tiles = here // TILE
    count = pl.num_programs(0) * tiles
    s = pl.program_id(0)
    begin = lax.rem(info[2] + s * tiles, count)
    live = (begin + tiles > info[0]) & (begin < info[1])

    def weight(group, start, stop):
        return w[:, group, :, start:stop].reshape(width, stop - start)

    def keys():
        total, group = jnp.zeros((here, width), f32), 0
        for part in dkv:
            for n in range(part.shape[0]):
                total = total + nt(part[n, :, :256], weight(group, 256, 512)) + nt(part[n, :, 256:], weight(group, 512 + cols, 512 + 2 * cols))
                group += 1
        return total

    @pl.when(jnp.logical_not(live))
    def _():
        rest[0] = jnp.zeros((here, width), bf16)

    @pl.when(live)
    def _():
        rest[0] = keys().astype(bf16)

    @pl.when(s == 0)
    def _():
        total, group = jnp.where(live, keys(), 0.0), 0
        for part in dq:
            for n in range(part.shape[0]):
                total = total + nt(part[n], weight(group, 0, 256))
                group += 1
        own[...] = total


def token_grads(info, w, dkv, dq, cols, slots):
    width = w.shape[0] * w.shape[2]
    here = dq[0].shape[1]

    def slot(array):
        return pl.BlockSpec((array.shape[0], here, array.shape[2]), lambda s: (0, s, 0))

    def whole(shape):
        return pl.BlockSpec(shape, lambda s: (0,) * len(shape))

    return pl.pallas_call(
        functools.partial(token_grads_kernel, cols=cols, split=len(dkv)),
        grid=(slots,),
        out_shape=(jax.ShapeDtypeStruct((here, width), f32), jax.ShapeDtypeStruct((slots, here, width), bf16)),
        in_specs=[pl.BlockSpec(memory_space=pltpu.SMEM), whole(w.shape)] + [slot(a) for a in dkv] + [whole(a.shape) for a in dq],
        out_specs=(whole((here, width)), pl.BlockSpec((1, here, width), lambda s: (s, 0, 0))),
        compiler_params=pltpu.CompilerParams(vmem_limit_bytes=40 << 20),
        cost_estimate=pl.CostEstimate(flops=8 << 30, bytes_accessed=20 << 20, transcendentals=0),
        name="token_grads",
    )(info, w, *dkv, *dq)


def doc_tables(lengths, seq, first, here):
    docs = lengths.shape[0]
    ends = jnp.cumsum(lengths)
    starts = ends - lengths
    place = lax.rem(jnp.arange(seq, dtype=jnp.int32) + first, seq)
    segment = jnp.sum((place[:, None] >= ends[None, :]).astype(jnp.int32), axis=1)
    member = segment[:, None] == jnp.arange(docs, dtype=jnp.int32)[None, :]
    offset = jnp.sum(jnp.where(member, starts[None, :], 0), axis=1)
    position = (place - offset).astype(f32)
    live = ends[docs - 2]
    tops = first + TILE * jnp.arange(here // TILE, dtype=jnp.int32)
    last = jnp.minimum(tops + TILE, live) - 1
    lo = jnp.max(jnp.where(starts[None, :] <= tops[:, None], starts[None, :], 0), axis=1) // TILE
    hi = jnp.minimum(jnp.min(jnp.where(ends[None, :] > last[:, None], ends[None, :], seq), axis=1), live)
    hi = jnp.where(tops < live, (hi + TILE - 1) // TILE, lo)
    span = [jnp.min(jnp.where(hi > lo, lo, seq), keepdims=True), jnp.max(jnp.where(hi > lo, hi, 0), keepdims=True)]
    return segment, position, jnp.concatenate([*span, jnp.reshape(first // TILE, (1,)), lo, hi])


def make_info(tables, me):
    return jnp.concatenate([tables[2], jnp.reshape(me, (1,))]).astype(jnp.int32)


EPSILON = 1e-05
ROWS = 256


def tn(left, right):
    return lax.dot_general(left, right, (((0,), (0,)), ((), ())), preferred_element_type=f32)


def row_mean(values):
    return jnp.mean(values, axis=-1, keepdims=True)


def normalise(values):
    centered = values - row_mean(values)
    inv = lax.rsqrt(row_mean(centered * centered) + EPSILON)
    return centered * inv, inv


def norm_back(upstream, unit, inv, scale):
    scaled = upstream * scale
    return inv * (scaled - row_mean(scaled) - unit * row_mean(scaled * unit))


def ffn_kernel(*refs, slots, pieces, share):
    own, cot, s1, b1, s2, b2, rel, w1_hbm, wown_hbm, w2_hbm = refs[:10]
    layer_out, grad_one, nlow, flow, brt, back, chunk, act_hbm, gg_hbm, ug_hbm = refs[10:20]
    w, wo, ws, g, u, normed, unit1, inv1, acc, small, stage, wsem, psem, osem, ssem = refs[20:]
    tokens, width = own.shape
    heads_cols = rel.shape[2]
    blk = slots * share
    pair = 2 if pieces % 2 == 0 else 1
    steps, wide = pieces // pair, pair * blk
    rows_share = width // pieces

    def load_own(p):
        return pltpu.make_async_copy(wown_hbm.at[p], w.at[p // pair, pl.ds(p % pair * blk, share)], psem.at[p])

    def load(p):
        return pltpu.make_async_copy(w2_hbm.at[p], w.at[p // pair, pl.ds(p % pair * blk + share, blk - share)], wsem.at[p])

    first = pltpu.make_async_copy(w1_hbm.at[:, :, :, pl.ds(512, wo.shape[3])], wo, osem)
    first.start()
    for p in range(pieces):
        load_own(p).start()
        load(p).start()
    first.wait()
    for s in range(slots):
        for p in range(pieces):
            ws[s, p * rows_share : (p + 1) * rows_share, :] = wo[p, s, :, :heads_cols]
    small[...] = jnp.zeros_like(small)

    def head(c, _):
        rows = pl.ds(pl.multiple_of(c * ROWS, ROWS), ROWS)
        h = own[rows, :].astype(f32)
        for s in range(slots):
            h = h + nt(rel[s, rows, :], ws[s])
        unit, inv = normalise(h)
        n = unit * s1[...] + b1[...]
        unit1[rows, :] = unit
        inv1[rows, :] = inv
        normed[rows, :] = n
        nlow[rows, :] = n.astype(bf16)
        acc[rows, :] = n
        return 0

    lax.fori_loop(0, tokens // ROWS, head, 0)

    def out_copy(which, target, p, slot):
        return pltpu.make_async_copy(stage.at[which, slot], target.at[:, pl.ds(pl.multiple_of(p * wide, 128), wide)], ssem.at[which, slot])

    def forward(p, _):
        slot = lax.rem(p, 2)
        cols = pl.ds(pl.multiple_of(p * wide, 128), wide)
        for i in range(pair):
            load_own(p * pair + i).wait()
            load(p * pair + i).wait()

        @pl.when(p >= 2)
        def _():
            out_copy(0, act_hbm, p - 2, slot).wait()

        halves = [slice(i, i + tokens // 2) for i in range(0, tokens, tokens // 2)]
        gates = [nt(nlow[r, :], w[p, :, :width]) for r in halves]
        ups = [nt(nlow[r, :], w[p, :, width : 2 * width]) for r in halves]
        for r, gp, up in zip(halves, gates, ups):
            g[r, cols] = gp
            u[r, cols] = up
            a = (gp * jax.nn.sigmoid(gp) * up).astype(bf16)
            stage[0, slot, r, :] = a
            acc[r, :] += nn(a, w[p, :, 2 * width :])
        out_copy(0, act_hbm, p, slot).start()
        return 0

    lax.fori_loop(0, steps, forward, 0)

    def middle(c, _):
        rows = pl.ds(pl.multiple_of(c * ROWS, ROWS), ROWS)
        unit, inv = normalise(acc[rows, :])
        layer_out[rows, :] = (unit * s2[...] + b2[...]).astype(bf16)
        up = cot[rows, :].astype(f32)
        d = norm_back(up, unit, inv, s2[...])
        small[2:3, :] += jnp.sum(up * unit, axis=0, keepdims=True)
        small[3:4, :] += jnp.sum(up, axis=0, keepdims=True)
        flow[rows, :] = d.astype(bf16)
        acc[rows, :] = d
        return 0

    lax.fori_loop(0, tokens // ROWS, middle, 0)
    for p in range(max(steps - 2, 0), steps):
        out_copy(0, act_hbm, p, p % 2).wait()

    def backward(p, _):
        slot = lax.rem(p, 2)
        cols = pl.ds(pl.multiple_of(p * wide, 128), wide)

        @pl.when(p >= 2)
        def _():
            out_copy(0, gg_hbm, p - 2, slot).wait()
            out_copy(1, ug_hbm, p - 2, slot).wait()

        halves = [slice(i, i + tokens // 2) for i in range(0, tokens, tokens // 2)]
        outer = [nt(flow[r, :], w[p, :, 2 * width :]) for r in halves]
        for r, da in zip(halves, outer):
            gp, up = g[r, cols], u[r, cols]
            sig = jax.nn.sigmoid(gp)
            both = da * sig
            dg = (both * up * (1.0 + gp * (1.0 - sig))).astype(bf16)
            du = (both * gp).astype(bf16)
            stage[0, slot, r, :] = dg
            stage[1, slot, r, :] = du
            acc[r, :] += nn(dg, w[p, :, :width]) + nn(du, w[p, :, width : 2 * width])
        out_copy(0, gg_hbm, p, slot).start()
        out_copy(1, ug_hbm, p, slot).start()
        return 0

    lax.fori_loop(0, steps, backward, 0)

    def tail(c, _):
        rows = pl.ds(pl.multiple_of(c * ROWS, ROWS), ROWS)
        up, unit = acc[rows, :], unit1[rows, :]
        d = norm_back(up, unit, inv1[rows, :], s1[...])
        small[0:1, :] += jnp.sum(up * unit, axis=0, keepdims=True)
        small[1:2, :] += jnp.sum(up, axis=0, keepdims=True)
        grad_one[rows, :] = d
        low = d.astype(bf16)
        brt[:, rows] = d.T.astype(bf16)
        for s in range(slots):
            back[s, rows, :] = nn(low, ws[s]).astype(bf16)
        return 0

    lax.fori_loop(0, tokens // ROWS, tail, 0)
    chunk[...] = jnp.zeros_like(chunk)
    room = chunk.shape[2]
    each = 4 * width // pieces // room
    for n in range(pieces * each):
        j, lane = divmod(n * room, width)
        chunk[n // each, n % each : n % each + 1, :] = small[j : j + 1, lane : lane + room]
    for p in range(max(steps - 2, 0), steps):
        out_copy(0, gg_hbm, p, p % 2).wait()
        out_copy(1, ug_hbm, p, p % 2).wait()


def ffn_layer(own, cot, norms, rel, w1, w_own, w2, room):
    slots, tokens, cols = rel.shape
    width = own.shape[1]
    pieces, share = w_own.shape[:2]
    units = pieces * slots * share
    pair = 2 if pieces % 2 == 0 else 1
    vm, hbm = pl.BlockSpec(memory_space=pltpu.VMEM), pl.BlockSpec(memory_space=pl.ANY)
    wide = jax.ShapeDtypeStruct((tokens, width), bf16)
    hidden = jax.ShapeDtypeStruct((tokens, units), bf16)
    return pl.pallas_call(
        functools.partial(ffn_kernel, slots=slots, pieces=pieces, share=share),
        out_shape=(wide, jax.ShapeDtypeStruct((tokens, width), f32), wide, wide, jax.ShapeDtypeStruct((width, tokens), bf16))
        + (jax.ShapeDtypeStruct((slots, tokens, cols), bf16), jax.ShapeDtypeStruct((pieces, 16, room), f32), hidden, hidden, hidden),
        in_specs=[vm] * 7 + [hbm] * 3,
        out_specs=(vm,) * 7 + (hbm,) * 3,
        scratch_shapes=[
            pltpu.VMEM((pieces // pair, pair * slots * share, 3 * width), bf16),
            pltpu.VMEM((pieces, slots, width // pieces, 256), bf16),
            pltpu.VMEM((slots, width, cols), bf16),
            pltpu.VMEM((tokens, units), f32),
            pltpu.VMEM((tokens, units), f32),
            pltpu.VMEM((tokens, width), f32),
            pltpu.VMEM((tokens, width), f32),
            pltpu.VMEM((tokens, 1), f32),
            pltpu.VMEM((tokens, width), f32),
            pltpu.VMEM((8, width), f32),
            pltpu.VMEM((2, 2, tokens, pair * slots * share), bf16),
            pltpu.SemaphoreType.DMA((pieces,)),
            pltpu.SemaphoreType.DMA((pieces,)),
            pltpu.SemaphoreType.DMA,
            pltpu.SemaphoreType.DMA((2, 2)),
        ],
        compiler_params=pltpu.CompilerParams(vmem_limit_bytes=50 << 20),
        cost_estimate=pl.CostEstimate(flops=16 << 30, bytes_accessed=30 << 20, transcendentals=3 << 20),
        name="ffn_layer",
    )(own, cot, *norms, rel, w1, w_own, w2)


def wgrad_kernel(*refs, slots, share, add):
    gg, ug, act, brt, nlow, flow, rel, small = refs[1:9]
    got = refs[9] if add else None
    width = nlow.shape[1]
    cols = rel.shape[2]
    edge = 3 * width + cols
    blk = slots * share
    out = refs[-1] if add else refs[-1].at[0]
    room = out.shape[1] - edge

    def put(rows, lanes, value):
        if add:
            value = value + got[0, rows, lanes].astype(f32)
        out[rows, lanes] = value.astype(bf16)

    terms = [tn(gg[...], nlow[...]), tn(ug[...], nlow[...]), tn(act[...], flow[...])]
    for s in range(slots):
        place = lax.rem(refs[0][1] - s + slots, slots)
        rows = pl.ds(pl.multiple_of(place * share, 32 if share % 32 == 0 else 4), share)
        for i in range(3):
            put(rows, slice(i * width, (i + 1) * width), terms[i][s * share : (s + 1) * share])
        put(rows, slice(3 * width, edge), nn(brt[...], rel[s]))
        put(rows, slice(edge, edge + room), jnp.concatenate([small[0], jnp.zeros((share - 16, room), f32)], axis=0))
    if add:
        first, second, rest = refs[10:13]
        top = first.shape[0]

        @pl.when(pl.program_id(0) == 0)
        def _():
            first[...] = out[:top, :]

        @pl.when(pl.program_id(0) == 1)
        def _():
            second[...] = out[:top, :]

        rest[0] = out[top:, :]


def wgrad(me, start, gg, ug, act, brt, nlow, flow, rel, small, got, pieces, share, span):
    slots = rel.shape[0]
    tokens, width = nlow.shape
    blk = slots * share
    top = slots // 2 * share

    def piece(i, me):
        return jnp.bitwise_xor(2 * i + start, me[0])

    both = pl.BlockSpec((1, blk, span), lambda i, me: (i, 0, 0))
    in_specs = [pl.BlockSpec((tokens, blk), lambda i, me: (0, piece(i, me)))] * 3
    in_specs += [pl.BlockSpec((width // pieces, tokens), lambda i, me: (piece(i, me), 0))]
    in_specs += [pl.BlockSpec((tokens, width), lambda i, me: (0, 0))] * 2
    in_specs += [pl.BlockSpec(rel.shape, lambda i, me: (0, 0, 0)), pl.BlockSpec((1,) + small.shape[1:], lambda i, me: (piece(i, me), 0, 0))]
    args = [stay(gg), stay(ug), stay(act), brt, nlow, flow, rel, small]
    if got is None:
        out_shape, out_specs, scratch = jax.ShapeDtypeStruct((2, blk, span), bf16), both, []
    else:
        in_specs.append(both)
        args.append(got)
        half = jax.ShapeDtypeStruct((top, span), bf16)
        out_shape = (half, half, jax.ShapeDtypeStruct((2, blk - top, span), bf16))
        fixed = pl.BlockSpec((top, span), lambda i, me: (0, 0))
        out_specs = (fixed, fixed, pl.BlockSpec((1, blk - top, span), lambda i, me: (i, 0, 0)))
        scratch = [pltpu.VMEM((blk, span), bf16)]
    return pl.pallas_call(
        functools.partial(wgrad_kernel, slots=slots, share=share, add=got is not None),
        out_shape=out_shape,
        grid_spec=pltpu.PrefetchScalarGridSpec(num_scalar_prefetch=1, grid=(2,), in_specs=in_specs, out_specs=out_specs, scratch_shapes=scratch),
        compiler_params=pltpu.CompilerParams(vmem_limit_bytes=24 << 20),
        cost_estimate=pl.CostEstimate(flops=2 << 30, bytes_accessed=10 << 20, transcendentals=0),
        name="wgrad",
    )(me, *args)


def final_kernel(gate, up, down, out_part, query, key, value, edge, gate_up_sum, down_sum, out_sum, qkv_sum, small_sum, *, heads, pieces, share, room):
    cols = heads * HD
    gate_up_sum[:, 0, :] = gate[...].astype(f32).T
    gate_up_sum[:, 1, :] = up[...].astype(f32).T
    down_sum[...] = down[...].astype(f32)
    out_sum[...] = out_part[...].astype(f32).T[:cols]
    for k, source in enumerate((query, key)):
        turned = source[...].astype(f32).T
        for h in range(heads):
            for half in range(2):
                start = 128 * half + HALF * h
                qkv_sum[k, HD * h + HALF * half : HD * h + HALF * (half + 1), :] = turned[start : start + HALF, :]
    qkv_sum[2, :, :] = value[...].astype(f32).T[:cols]

    @pl.when(pl.program_id(0) == 0)
    def _():
        width = small_sum.shape[1]
        each = 4 * width // pieces // room
        for n in range(pieces * each):
            j, lane = divmod(n * room, width)
            row = n // each * share + n % each
            base = row // 16 * 16
            block = edge[base : base + 16, 128 - room :].astype(f32)
            small_sum[j : j + 1, lane : lane + room] = block[row - base : row - base + 1, :]


def final_sums(main, width, span, heads, pieces):
    units = main.shape[0]
    lanes = 128
    steps = width // lanes
    cols = heads * HD
    room = span - 3 * width - cols
    tall = units // steps

    def band(first, size):
        return pl.BlockSpec((tall, size), lambda i, n=first // size: (i, n))

    in_specs = [pl.BlockSpec((units, lanes), lambda i: (0, i)), pl.BlockSpec((units, lanes), lambda i: (0, i + steps))]
    in_specs += [band(2 * width, width), band(3 * width, 256)] + [band(span + 256 * k, 256) for k in range(3)]
    in_specs += [pl.BlockSpec((units, lanes), lambda i: (0, span // lanes - 1))]
    return pl.pallas_call(
        functools.partial(final_kernel, heads=heads, pieces=pieces, share=units // pieces, room=room),
        grid=(steps,),
        out_shape=(
            jax.ShapeDtypeStruct((width, 2, units), f32),
            jax.ShapeDtypeStruct((units, width), f32),
            jax.ShapeDtypeStruct((cols, width), f32),
            jax.ShapeDtypeStruct((3, cols, width), f32),
            jax.ShapeDtypeStruct((4, width), f32),
        ),
        in_specs=in_specs,
        out_specs=(
            pl.BlockSpec((lanes, 2, units), lambda i: (i, 0, 0)),
            pl.BlockSpec((tall, width), lambda i: (i, 0)),
            pl.BlockSpec((cols, tall), lambda i: (0, i)),
            pl.BlockSpec((3, cols, tall), lambda i: (0, 0, i)),
            pl.BlockSpec((4, width), lambda i: (0, 0)),
        ),
        cost_estimate=pl.CostEstimate(flops=1 << 20, bytes_accessed=15 << 20, transcendentals=0),
        name="final_sums",
    )(*[main] * 8)


ROPE_BASE = 1000.0


def rotate_axis(size, step):
    return [(i, (i + step) % size) for i in range(size)]


def line_axis(size, step):
    return [(i, i + step) for i in range(size) if 0 <= i + step < size]


def flip_axis(size, bit):
    return [(i, i ^ bit) for i in range(size)]


def after(value, *others):
    return lax.optimization_barrier((value, *others))[0]


def low_sum(left, right):
    return (left.astype(f32) + right.astype(f32)).astype(bf16)


def body(
    dp_size,
    tp_size,
    tokens,
    lengths,
    w_qkv,
    w_out,
    norm1_scale,
    norm1_shift,
    w_gate_up,
    w_down,
    norm2_scale,
    norm2_shift,
    cotangent,
):
    own = tokens[0]
    rows_here, width = own.shape
    docs = lengths.shape[1]
    seq = rows_here * tp_size
    cols_here = w_qkv.shape[2]
    heads = cols_here // HD
    units = w_gate_up.shape[2]
    pieces = min(dp_size, 8)
    groups = None if pieces == dp_size else [list(range(i, i + pieces)) for i in range(0, dp_size, pieces)]
    share = units // pieces
    rows_share = width // pieces
    span = -(-(3 * width + cols_here) // 128) * 128
    me = lax.rem(lax.axis_index("dp"), pieces)
    z = lax.axis_index("tensor")

    def flip(array, bit):
        return lax.ppermute(array, "dp", flip_axis(dp_size, bit))

    def shift(array, step):
        return lax.ppermute(array, "tensor", rotate_axis(tp_size, step))

    def along(array, step):
        return lax.ppermute(array, "tensor", line_axis(tp_size, step))

    def gather_dp(array):
        return lax.all_gather(array, "dp", axis=0, axis_index_groups=groups)

    def rope_order(matrix):
        halves = matrix.reshape(rows_share, heads, 2, HALF).transpose(0, 2, 1, 3).reshape(rows_share, 2, heads * HALF)
        return jnp.pad(halves, ((0, 0), (0, 0), (0, 128 - heads * HALF))).reshape(rows_share, 256)

    qkv_slice = lax.dynamic_slice_in_dim(w_qkv, me * rows_share, rows_share, 0)
    out_slice = lax.dynamic_slice_in_dim(w_out, me * rows_share, rows_share, 1)
    piece_one = jnp.concatenate([rope_order(qkv_slice[:, 0]), rope_order(qkv_slice[:, 1]), out_slice.T, qkv_slice[:, 2]], axis=1)
    gate_slice = lax.dynamic_slice_in_dim(w_gate_up, me * share, share, 2)
    down_slice = lax.dynamic_slice_in_dim(w_down, me * share, share, 0)
    piece_two = jnp.concatenate([gate_slice[:, 0].T, gate_slice[:, 1].T, down_slice], axis=1)
    piece_one, piece_two = lax.optimization_barrier((piece_one, piece_two))
    ones = [piece_one] + [shift(piece_one, s) for s in range(1, tp_size)]
    piece_two = after(piece_two, *ones[1:])
    twos = [shift(piece_two, s) for s in range(1, tp_size)]
    w1 = gather_dp(jnp.stack(ones))
    row_lengths, gate_up_late, down_late = after(lengths[0], ones[-1]), after(w_gate_up, ones[-1]), after(w_down, ones[-1])
    w_own = jnp.concatenate([gate_up_late[:, 0].T, gate_up_late[:, 1].T, down_late], axis=1).reshape(pieces, share, 3 * width)

    tables = doc_tables(row_lengths, seq, z * rows_here, rows_here)
    segment, position = tables[:2]
    info = make_info(tables, me)
    inverse = ROPE_BASE ** (-2.0 * lax.rem(jnp.arange(128), HALF).astype(f32) / HD)
    angles = position[:, None] * inverse[None, :]
    cosine, sine = jnp.cos(angles), jnp.sin(angles)
    seg_col = segment[:, None]

    twos, cosine, sine, seg_col, info, w_own = lax.optimization_barrier((twos, cosine, sine, seg_col, info, w_own))
    w2 = gather_dp(jnp.concatenate(twos, axis=0))

    own_late = after(own, *ones[1:])
    before, behind = along(own_late, 1), along(own_late, -1)

    *held, qh = project(own, w1, cosine, sine, seg_col, docs, heads, 0, tp_size)
    held, before, behind = lax.optimization_barrier((held, before, behind))
    before2, behind2 = along(before, 1), along(behind, -1)
    held = project(behind, w1, cosine, sine, seg_col, docs, heads, 1, tp_size, held)
    held = project(before, w1, cosine, sine, seg_col, docs, heads, 3, tp_size, held)
    held, behind2, before2 = lax.optimization_barrier((held, behind2, before2))
    toks = [own, behind, jnp.where(z < tp_size // 2, behind2, before2), before]
    held = project(toks[2], w1, cosine, sine, seg_col, docs, heads, 2, tp_size, held)
    lse, rel = attn_fwd(info, seg_col, qh, held[0], held[2], docs)
    saved = (qh, held[0].reshape(tp_size, seq, -1), held[1].reshape(tp_size, seq, -1), lse, rel)
    norms = [v.reshape(1, width) for v in (norm1_scale, norm1_shift, norm2_scale, norm2_shift)]
    room = span - 3 * width - cols_here
    layer_out, grad_one, nlow, flow, brt, back, chunk, act, gg, ug = ffn_layer(own, cotangent[0], norms, rel, w1, w_own, w2, room)

    half = tp_size // 2

    me_array = jnp.stack([me, z]).astype(jnp.int32)
    fixed = (gg, ug, act, brt, nlow, flow, rel, chunk)
    far_sent = wgrad(me_array, 5, *fixed, None, pieces, share, span)
    near_sent = wgrad(after(me_array, far_sent), 1, *fixed, None, pieces, share, span)
    far_keep, far_give, far_rest = wgrad(after(me_array, near_sent), 4, *fixed, flip(far_sent, 1), pieces, share, span)
    near_keep, near_give, near_rest = wgrad(after(me_array, far_rest), 0, *fixed, flip(near_sent, 1), pieces, share, span)

    back, near_give = lax.optimization_barrier((back, near_give))
    got = [flip(far_give, 2), flip(far_rest, 4), flip(near_give, 2)]
    backward = functools.partial(attn_bwd, info, toks, cosine, sine, seg_col, saved)
    cut = tp_size - 1
    dw_low, kv_low, q_low = backward(back, docs, heads, pieces, 0, cut)
    got, dw_low, back_late = lax.optimization_barrier((got, dw_low, back))
    next_b = low_sum(near_rest, got[1])
    give_a, next_a = low_sum(far_keep, got[0]), low_sum(near_keep, got[2])
    back_late, next_a, give_a, next_b = lax.optimization_barrier((back_late, next_a, give_a, next_b))
    got_a, got_b, got_low = flip(give_a, 4), flip(next_b[1], 2), flip(dw_low.reshape((pieces // 2, 2) + dw_low.shape[1:])[:, 1], 1)
    dw_high, kv_high, q_high = backward(back_late, docs, heads, pieces, cut, tp_size)
    got_a, got_b, got_low, dw_high, kv_high = lax.optimization_barrier((got_a, got_b, got_low, dw_high, kv_high))
    parts_two = jnp.concatenate([low_sum(next_a, got_a), low_sum(next_b[0], got_b)], axis=0)
    share_two = lax.psum_scatter(parts_two, "tensor", scatter_dimension=0, tiled=True)

    def pairs_of(array):
        return array.reshape((pieces // 2, 2) + array.shape[1:])

    got_high = flip(pairs_of(dw_high)[:, 1], 1)
    dx_own, dx = token_grads(info, w1, (kv_low, kv_high), (q_low, q_high), cols_here, tp_size)
    low = low_sum(pairs_of(dw_low)[:, 0], got_low).reshape((2, 2) + dw_low.shape[1:])
    got_a = flip(low[:, 1, :half], 2)
    high = low_sum(pairs_of(dw_high)[:, 0], got_high).reshape((2, 2) + dw_high.shape[1:])
    high = jnp.concatenate([low[:, :, half:], high], axis=2)
    got_b = flip(high[1], 4)
    next_a, next_b = low_sum(low[:, 0, :half], got_a), low_sum(high[0], got_b)
    got_a, got_b = flip(next_a[1], 4), flip(next_b[1], 2)

    def by_slot(low, high):
        low, high = low.reshape(half, -1, low.shape[-1]), high.reshape(tp_size - half, -1, high.shape[-1])
        return [low[i] for i in range(half)] + [high[i] for i in range(tp_size - half)]

    def total(own_part, moved):
        return functools.reduce(lambda x, y: x + y.astype(f32), moved, own_part.astype(f32)).astype(bf16)

    parts_one = by_slot(low_sum(next_a[0], got_a), low_sum(next_b[0], got_b))
    moved_one = [shift(parts_one[s], -s) for s in range(1, tp_size)]
    moved_one, dx = lax.optimization_barrier((moved_one, dx))
    share_one = total(parts_one[0], moved_one)
    from_left = lax.ppermute(dx[2], "tensor", [(i, i + 1) for i in range(half)])
    from_right = lax.ppermute(dx[2], "tensor", [(i + half, i + half - 1) for i in range(half)])
    near_right, near_left = low_sum(dx[1], from_left), low_sum(dx[3], from_right)
    from_before, from_behind = along(near_right, 1), along(near_left, -1)

    def finish(array):
        if groups is not None:
            across = [[g * pieces + i for g in range(dp_size // pieces)] for i in range(pieces)]
            array = lax.psum(array.astype(f32), "dp", axis_index_groups=across).astype(bf16)
        return gather_dp(array)

    main = finish(jnp.concatenate([share_two, share_one], axis=1)).reshape(units, -1)
    gate_up_sum, down_sum, out_sum, qkv_turned, small_out = final_sums(main, width, span, heads, pieces)
    qkv_sum = qkv_turned.transpose(2, 0, 1)
    from_before, from_behind, small_out = lax.optimization_barrier((from_before, from_behind, small_out))
    input_grad = grad_one + dx_own + from_before.astype(f32) + from_behind.astype(f32)
    return (
        layer_out[None],
        input_grad[None],
        qkv_sum,
        out_sum,
        small_out[0],
        small_out[1],
        gate_up_sum,
        down_sum,
        small_out[2],
        small_out[3],
    )


def solution(mesh):
    in_specs = (
        P("dp", "tensor", None),
        P("dp", None),
        P(None, None, "tensor"),
        P("tensor", None),
        P(),
        P(),
        P(None, None, "tensor"),
        P("tensor", None),
        P(),
        P(),
        P("dp", "tensor", None),
    )
    out_specs = (
        P("dp", "tensor", None),
        P("dp", "tensor", None),
        P(None, None, "tensor"),
        P("tensor", None),
        P(),
        P(),
        P(None, None, "tensor"),
        P("tensor", None),
        P(),
        P(),
    )
    return jax.shard_map(
        functools.partial(body, mesh.shape["dp"], mesh.shape["tensor"]),
        mesh=mesh,
        in_specs=in_specs,
        out_specs=out_specs,
        check_vma=False,
    )
```

```python
import functools

import jax
import jax.numpy as jnp
from jax import lax
from jax.experimental import pallas as pl
from jax.experimental.pallas import tpu as pltpu
from jax.sharding import PartitionSpec as P

TILE = 256
HALF = 32
HD = 64
BIG = 1e30
f32, bf16 = jnp.float32, jnp.bfloat16


def nt(a, b):
    return lax.dot_general(a, b, (((1,), (1,)), ((), ())), preferred_element_type=f32)


def nn(a, b):
    return jnp.dot(a, b, preferred_element_type=f32)


def stay(array):
    return pltpu.with_memory_space_constraint(array, pltpu.HBM)


def tile_rows(tile, base, count):
    return pl.ds(pl.multiple_of(lax.rem(tile - base + count, count) * TILE, TILE), TILE)


def over_tiles(info, lo, hi, tiles, scan):
    def one(t, _):
        live = [(t >= info[3 + u]) & (t < info[3 + tiles + u]) for u in range(tiles)]
        every = functools.reduce(jnp.logical_and, live)

        @pl.when(every)
        def _():
            scan(t, slice(0, tiles * TILE))

        @pl.when(jnp.logical_not(every))
        def _():
            def single(u, _):
                @pl.when((t >= info[3 + u]) & (t < info[3 + tiles + u]))
                def _():
                    scan(t, pl.ds(pl.multiple_of(u * TILE, TILE), TILE))

                return 0

            lax.fori_loop(0, tiles, single, 0)

        return 0

    lax.fori_loop(lo, hi, one, 0)


def project_kernel(*refs, docs, heads, slot):
    tok, w, cos, sin, seg = refs[:5]
    outs = refs[5:] if slot == 0 else refs[8:]
    ka, va, vt = outs[:3]
    here, width = tok.shape
    used = heads * HALF
    cols = heads * HD
    lane = lax.broadcasted_iota(jnp.int32, (TILE, 128), 1)
    filler = lax.broadcasted_iota(jnp.int32, (80 - HD, here), 0)

    def weight(start, stop):
        return w[:, 0, :, start:stop].reshape(width, stop - start)

    for h in range(heads):
        vt[0, 0, 80 * h + HD : 80 * (h + 1), :] = jnp.where(filler == 0, 1.0, 0.0).astype(bf16)

    def tile(c, _):
        rows = pl.ds(pl.multiple_of(c * TILE, TILE), TILE)
        x = tok[rows, :]
        co, si = cos[rows, :], sin[rows, :]
        hit = (lane - used) == seg[rows, :]
        if slot == 0:
            p = nn(x, weight(0, 256))
            ra = (p[:, :128] * co - p[:, 128:] * si).astype(bf16).astype(f32) * HD**-0.5
            rb = (p[:, 128:] * co + p[:, :128] * si).astype(bf16).astype(f32) * HD**-0.5
            for h in range(heads):
                keep = (lane >= HALF * h) & (lane < HALF * (h + 1))
                outs[3][0, h, rows, :128] = jnp.where(keep, ra, jnp.where(hit, -BIG, 0.0)).astype(bf16)
                outs[3][0, h, rows, 128:] = jnp.where(keep, rb, 0.0).astype(bf16)
        p = nn(x, weight(256, 512))
        other = (lane >= used) & (lane < used + docs) & jnp.logical_not(hit)
        ra, rb = p[:, :128] * co - p[:, 128:] * si, p[:, 128:] * co + p[:, :128] * si
        ka[0, 0, rows, :128] = jnp.where(lane < used, ra, jnp.where(other, 1.0, 0.0)).astype(bf16)
        ka[0, 0, rows, 128:] = rb.astype(bf16)
        v = nn(x, weight(512 + cols, 512 + 2 * cols))
        va[0, 0, rows, :] = v.astype(bf16)
        turned = v.T.astype(bf16)
        for h in range(heads):
            vt[0, 0, 80 * h : 80 * h + HD, rows] = turned[HD * h : HD * (h + 1), :]
        return 0

    lax.fori_loop(0, here // TILE, tile, 0)


def project(tok, w, cos, sin, seg, docs, heads, slot, slots, held=()):
    here, width = tok.shape
    cols = heads * HD
    shapes = [(here, 256), (here, cols), (80 * heads, here)]
    out_shape = [pltpu.HBM((slots, slots) + s, bf16) for s in shapes]
    out_specs = [pl.BlockSpec((1, 1) + s, lambda g: (g, slot, 0, 0)) for s in shapes]
    if slot == 0:
        out_shape.append(pltpu.HBM((slots, heads, here, 256), bf16))
        out_specs.append(pl.BlockSpec((1, heads, here, 256), lambda g: (g, 0, 0, 0)))
    rows = pl.BlockSpec((here, cos.shape[1]), lambda g: (slot, 0))
    return pl.pallas_call(
        functools.partial(project_kernel, docs=docs, heads=heads, slot=slot),
        grid=(slots,),
        out_shape=tuple(out_shape),
        in_specs=[
            pl.BlockSpec((here, width), lambda g: (0, 0)),
            pl.BlockSpec((w.shape[0], 1) + w.shape[2:], lambda g: (0, g, 0, 0)),
            rows,
            rows,
            pl.BlockSpec((here, 1), lambda g: (slot, 0)),
        ]
        + [pl.BlockSpec(memory_space=pl.ANY)] * len(held),
        out_specs=tuple(out_specs),
        input_output_aliases={5 + n: n for n in range(len(held))},
        compiler_params=pltpu.CompilerParams(vmem_limit_bytes=20 << 20),
        cost_estimate=pl.CostEstimate(flops=2 << 30, bytes_accessed=8 << 20, transcendentals=0),
        name="project",
    )(tok, w, cos, sin, seg, *[stay(a) for a in held])


def attn_fwd_kernel(info, seg, qh, ka, vt, lse, mixed, acc, top, *, docs, heads):
    here = qh.shape[2]
    tiles = here // TILE
    count = ka.shape[1] * tiles
    lo, hi, base = info[0], info[1], info[2]
    acc[...] = jnp.zeros_like(acc)
    top[...] = jnp.full_like(top, -3e38)

    def scan(t, mine):
        c = lax.rem(t - base + count, count)
        slot = c // tiles
        rows = pl.ds(pl.multiple_of(lax.rem(c, tiles) * TILE, TILE), TILE)
        kk = ka[0, slot, rows, :]
        scores = [nt(kk, qh[0, h, mine, :]) for h in range(heads)]
        olds = [top[h : h + 1, mine] for h in range(heads)]
        news = [jnp.maximum(olds[h], jnp.max(scores[h], axis=0, keepdims=True)) for h in range(heads)]
        probs = [jnp.exp(scores[h] - news[h]).astype(bf16) for h in range(heads)]
        adds = [nn(vt[0, slot, 80 * h : 80 * h + 80, rows], probs[h]) for h in range(heads)]
        for h in range(heads):
            top[h : h + 1, mine] = news[h]
            acc[h, :, mine] = acc[h, :, mine] * jnp.exp(olds[h] - news[h]) + adds[h]

    over_tiles(info, lo, hi, tiles, scan)
    good = seg[...] < docs - 1
    total = [jnp.where(top[h : h + 1, :] > -1e29, acc[h, HD : HD + 1, :], 1.0) for h in range(heads)]
    outs = jnp.concatenate([acc[h, :HD, :] / total[h] for h in range(heads)], axis=0).T
    mixed[0] = jnp.where(good, outs, 0.0).astype(bf16)
    stats = [top[h : h + 1, :] + jnp.log(total[h]) for h in range(heads)]
    lse[0] = jnp.concatenate(stats + [jnp.zeros((8 - heads, here), f32)], axis=0)


def attn_fwd(info, seg, qh, ka, vt, docs):
    slots, heads, here = qh.shape[:3]
    cols = heads * HD

    def part(shape):
        return pl.BlockSpec((1,) + shape[1:], lambda g: (g,) + (0,) * (len(shape) - 1))

    shapes = [((slots, 8, here), f32), ((slots, here, cols), bf16)]
    return pl.pallas_call(
        functools.partial(attn_fwd_kernel, docs=docs, heads=heads),
        grid=(slots,),
        out_shape=tuple(jax.ShapeDtypeStruct(s, d) for s, d in shapes),
        in_specs=[pl.BlockSpec(memory_space=pltpu.SMEM), pl.BlockSpec((here, 1), lambda g: (0, 0))] + [part(a.shape) for a in (qh, ka, vt)],
        out_specs=tuple(part(s) for s, _ in shapes),
        scratch_shapes=[pltpu.VMEM((heads, 80, here), f32), pltpu.VMEM((8, here), f32)],
        compiler_params=pltpu.CompilerParams(vmem_limit_bytes=24 << 20),
        cost_estimate=pl.CostEstimate(flops=12 << 30, bytes_accessed=12 << 20, transcendentals=4 << 20),
        name="attn_fwd",
    )(info, seg, stay(qh), stay(ka), stay(vt))


def attn_bwd_kernel(info, *refs, docs, heads, slots, pieces):
    toks = refs[:slots]
    cos, sin, seg, qh, ka, va, lse, mixed, do = refs[slots : slots + 9]
    dw, dkv, dq, tokt, dqt, dwa, doh, delta, dka, dva = refs[slots + 9 :]
    here, width = toks[0].shape
    seq = here * slots
    count = seq // TILE
    used = heads * HALF
    cols = heads * HD
    tiles = here // TILE
    lo, hi, base, me = info[0], info[1], info[2], info[3 + 2 * tiles]

    @pl.when(pl.program_id(0) == 0)
    def _():
        dkv[...] = jnp.zeros_like(dkv)
        dwa[:, 512 + cols :] = jnp.zeros((width, dwa.shape[1] - 512 - cols), f32)
        for s in range(slots):
            for c in range(here // TILE):
                start = s * here + c * TILE
                tokt[:, start : start + TILE] = toks[s][c * TILE : (c + 1) * TILE, :].astype(f32).T.astype(bf16)

    g = pl.program_id(0)

    wlane = lax.broadcasted_iota(jnp.int32, (here, cols), 1)
    lane = lax.broadcasted_iota(jnp.int32, (TILE, 128), 1)
    dqt[...] = jnp.zeros_like(dqt)
    d = jnp.where(seg[:here, :] < docs - 1, do[0].astype(f32), 0.0)
    prod = d * mixed[0].astype(f32)
    prod_high = prod.astype(bf16)
    prod_low = (prod - prod_high.astype(f32)).astype(bf16)
    pick = (lax.broadcasted_iota(jnp.int32, (8, cols), 1) // HD == lax.broadcasted_iota(jnp.int32, (8, cols), 0)).astype(bf16)
    delta[...] = nt(pick, prod_high) + nt(pick, prod_low)
    for h in range(heads):
        doh[h] = jnp.where((wlane >= HD * h) & (wlane < HD * (h + 1)), d, 0.0).astype(bf16)

    def unrotate(a, b, rows):
        a, b = a.astype(bf16).astype(f32), b.astype(bf16).astype(f32)
        co, si = cos[rows, :], sin[rows, :]
        keep = lane < used
        both = [jnp.where(keep, a * co + b * si, 0.0), jnp.where(keep, b * co - a * si, 0.0)]
        return jnp.concatenate(both, axis=1).astype(bf16)

    def scan(t, mine):
        rows = tile_rows(t, base, count)
        kk, vv = ka[0, rows, :], va[0, rows, :]
        kt = kk.astype(f32).T.astype(bf16)
        qs, dd = [qh[0, h, mine, :] for h in range(heads)], [doh[h, mine, :] for h in range(heads)]
        probs = [jnp.exp(nt(kk, qs[h]) - lse[0, h : h + 1, mine]) for h in range(heads)]
        ds = [(probs[h] * (nt(vv, dd[h]) - delta[h : h + 1, mine])).astype(bf16) for h in range(heads)]
        dva[...] += sum(nn(probs[h].astype(bf16), dd[h]) for h in range(heads))
        dka[...] += sum(nn(ds[h], qs[h]) for h in range(heads))
        for h in range(heads):
            kth = jnp.concatenate([kt[HALF * h : HALF * (h + 1)], kt[128 + HALF * h : 128 + HALF * (h + 1)]], axis=0)
            g = nn(kth, ds[h])
            dqt[HALF * h : HALF * (h + 1), mine] += g[:HALF]
            dqt[128 + HALF * h : 128 + HALF * (h + 1), mine] += g[HALF:]

    def k_tile(t, _):
        rows = tile_rows(t, base, count)
        dka[...] = jnp.zeros_like(dka)
        dva[...] = jnp.zeros_like(dva)
        over_tiles(info, t, t + 1, tiles, scan)
        dkv[g, rows, :256] = unrotate(dka[:, :128], dka[:, 128:], rows)
        dkv[g, rows, 256:] = dva[...].astype(bf16)
        return 0

    lax.fori_loop(lo, hi, k_tile, 0)
    for c in range(here // TILE):
        rows = slice(c * TILE, (c + 1) * TILE)
        gq = dqt[:, rows].T * HD**-0.5
        dq[g, rows, :] = unrotate(gq[:, :128], gq[:, 128:], rows)
    dwa[:, :256] = nn(tokt[:, :here], dq[g])
    dwa[:, 256 : 512 + cols] = nn(tokt[...], dkv[g])
    share = width // pieces
    for r in range(pieces):
        p = jnp.bitwise_xor(me, r)
        dw[r, 0] = dwa[pl.ds(pl.multiple_of(p * share, 8), share), :].astype(bf16)


def attn_bwd(info, toks, cos, sin, seg, saved, do, docs, heads, pieces, start, stop):
    slots = len(toks)
    here, width = toks[0].shape
    seq = here * slots
    cols = heads * HD
    span = -(-(512 + cols) // 128) * 128
    count = stop - start

    def whole(shape):
        return pl.BlockSpec(shape, lambda g: (0,) * len(shape))

    def part(array):
        return pl.BlockSpec((1,) + array.shape[1:], lambda g: (g + start,) + (0,) * (array.ndim - 1))

    kept = [((count, seq, 256 + cols), bf16), ((count, here, 256), bf16)]
    return pl.pallas_call(
        functools.partial(attn_bwd_kernel, docs=docs, heads=heads, slots=slots, pieces=pieces),
        grid=(count,),
        out_shape=(jax.ShapeDtypeStruct((pieces, count, width // pieces, span), bf16),) + tuple(jax.ShapeDtypeStruct(s, d) for s, d in kept),
        in_specs=[pl.BlockSpec(memory_space=pltpu.SMEM)]
        + [whole((here, width))] * slots
        + [whole(cos.shape), whole(sin.shape), pl.BlockSpec((here, 1), lambda g: (0, 0))]
        + [part(a) for a in (*saved, do)],
        out_specs=(pl.BlockSpec((pieces, 1, width // pieces, span), lambda g: (0, g, 0, 0)),) + tuple(whole(s) for s, _ in kept),
        scratch_shapes=[
            pltpu.VMEM((width, seq), bf16),
            pltpu.VMEM((256, here), f32),
            pltpu.VMEM((width, span), f32),
            pltpu.VMEM((heads, here, cols), bf16),
            pltpu.VMEM((8, here), f32),
            pltpu.VMEM((TILE, 256), f32),
            pltpu.VMEM((TILE, cols), f32),
        ],
        compiler_params=pltpu.CompilerParams(vmem_limit_bytes=40 << 20),
        cost_estimate=pl.CostEstimate(flops=10 * count << 30, bytes_accessed=6 * count << 20, transcendentals=count << 20),
        name="attn_bwd",
    )(info, *toks, cos, sin, seg, *saved, do)


def token_grads_kernel(info, w, *refs, cols, split):
    dkv, dq, (own, rest) = refs[:split], refs[split : 2 * split], refs[2 * split :]
    here = rest.shape[1]
    width = own.shape[1]
    tiles = here // TILE
    count = pl.num_programs(0) * tiles
    s = pl.program_id(0)
    begin = lax.rem(info[2] + s * tiles, count)
    live = (begin + tiles > info[0]) & (begin < info[1])

    def weight(group, start, stop):
        return w[:, group, :, start:stop].reshape(width, stop - start)

    def keys():
        total, group = jnp.zeros((here, width), f32), 0
        for part in dkv:
            for n in range(part.shape[0]):
                total = total + nt(part[n, :, :256], weight(group, 256, 512)) + nt(part[n, :, 256:], weight(group, 512 + cols, 512 + 2 * cols))
                group += 1
        return total

    @pl.when(jnp.logical_not(live))
    def _():
        rest[0] = jnp.zeros((here, width), bf16)

    @pl.when(live)
    def _():
        rest[0] = keys().astype(bf16)

    @pl.when(s == 0)
    def _():
        total, group = jnp.where(live, keys(), 0.0), 0
        for part in dq:
            for n in range(part.shape[0]):
                total = total + nt(part[n], weight(group, 0, 256))
                group += 1
        own[...] = total


def token_grads(info, w, dkv, dq, cols, slots):
    width = w.shape[0] * w.shape[2]
    here = dq[0].shape[1]

    def slot(array):
        return pl.BlockSpec((array.shape[0], here, array.shape[2]), lambda s: (0, s, 0))

    def whole(shape):
        return pl.BlockSpec(shape, lambda s: (0,) * len(shape))

    return pl.pallas_call(
        functools.partial(token_grads_kernel, cols=cols, split=len(dkv)),
        grid=(slots,),
        out_shape=(jax.ShapeDtypeStruct((here, width), f32), jax.ShapeDtypeStruct((slots, here, width), bf16)),
        in_specs=[pl.BlockSpec(memory_space=pltpu.SMEM), whole(w.shape)] + [slot(a) for a in dkv] + [whole(a.shape) for a in dq],
        out_specs=(whole((here, width)), pl.BlockSpec((1, here, width), lambda s: (s, 0, 0))),
        compiler_params=pltpu.CompilerParams(vmem_limit_bytes=40 << 20),
        cost_estimate=pl.CostEstimate(flops=8 << 30, bytes_accessed=20 << 20, transcendentals=0),
        name="token_grads",
    )(info, w, *dkv, *dq)


def doc_tables(lengths, seq, first, here):
    docs = lengths.shape[0]
    ends = jnp.cumsum(lengths)
    starts = ends - lengths
    place = lax.rem(jnp.arange(seq, dtype=jnp.int32) + first, seq)
    segment = jnp.sum((place[:, None] >= ends[None, :]).astype(jnp.int32), axis=1)
    member = segment[:, None] == jnp.arange(docs, dtype=jnp.int32)[None, :]
    offset = jnp.sum(jnp.where(member, starts[None, :], 0), axis=1)
    position = (place - offset).astype(f32)
    live = ends[docs - 2]
    tops = first + TILE * jnp.arange(here // TILE, dtype=jnp.int32)
    last = jnp.minimum(tops + TILE, live) - 1
    lo = jnp.max(jnp.where(starts[None, :] <= tops[:, None], starts[None, :], 0), axis=1) // TILE
    hi = jnp.minimum(jnp.min(jnp.where(ends[None, :] > last[:, None], ends[None, :], seq), axis=1), live)
    hi = jnp.where(tops < live, (hi + TILE - 1) // TILE, lo)
    span = [jnp.min(jnp.where(hi > lo, lo, seq), keepdims=True), jnp.max(jnp.where(hi > lo, hi, 0), keepdims=True)]
    return segment, position, jnp.concatenate([*span, jnp.reshape(first // TILE, (1,)), lo, hi])


def make_info(tables, me):
    return jnp.concatenate([tables[2], jnp.reshape(me, (1,))]).astype(jnp.int32)


EPSILON = 1e-05
ROWS = 256


def tn(left, right):
    return lax.dot_general(left, right, (((0,), (0,)), ((), ())), preferred_element_type=f32)


def row_mean(values):
    return jnp.mean(values, axis=-1, keepdims=True)


def normalise(values):
    centered = values - row_mean(values)
    inv = lax.rsqrt(row_mean(centered * centered) + EPSILON)
    return centered * inv, inv


def norm_back(upstream, unit, inv, scale):
    scaled = upstream * scale
    return inv * (scaled - row_mean(scaled) - unit * row_mean(scaled * unit))


def ffn_kernel(*refs, slots, pieces, share):
    own, cot, s1, b1, s2, b2, rel, w1_hbm, wown_hbm, w2_hbm = refs[:10]
    layer_out, grad_one, nlow, flow, brt, back, chunk, act_hbm, gg_hbm, ug_hbm = refs[10:20]
    w, wo, ws, g, u, normed, unit1, inv1, acc, small, stage, wsem, psem, osem, ssem = refs[20:]
    tokens, width = own.shape
    heads_cols = rel.shape[2]
    blk = slots * share
    pair = 2 if pieces % 2 == 0 else 1
    steps, wide = pieces // pair, pair * blk
    rows_share = width // pieces

    def load_own(p):
        return pltpu.make_async_copy(wown_hbm.at[p], w.at[p // pair, pl.ds(p % pair * blk, share)], psem.at[p])

    def load(p):
        return pltpu.make_async_copy(w2_hbm.at[p], w.at[p // pair, pl.ds(p % pair * blk + share, blk - share)], wsem.at[p])

    first = pltpu.make_async_copy(w1_hbm.at[:, :, :, pl.ds(512, wo.shape[3])], wo, osem)
    first.start()
    for p in range(pieces):
        load_own(p).start()
        load(p).start()
    first.wait()
    for s in range(slots):
        for p in range(pieces):
            ws[s, p * rows_share : (p + 1) * rows_share, :] = wo[p, s, :, :heads_cols]
    small[...] = jnp.zeros_like(small)

    def head(c, _):
        rows = pl.ds(pl.multiple_of(c * ROWS, ROWS), ROWS)
        h = own[rows, :].astype(f32)
        for s in range(slots):
            h = h + nt(rel[s, rows, :], ws[s])
        unit, inv = normalise(h)
        n = unit * s1[...] + b1[...]
        unit1[rows, :] = unit
        inv1[rows, :] = inv
        normed[rows, :] = n
        nlow[rows, :] = n.astype(bf16)
        acc[rows, :] = n
        return 0

    lax.fori_loop(0, tokens // ROWS, head, 0)

    def out_copy(which, target, p, slot):
        return pltpu.make_async_copy(stage.at[which, slot], target.at[:, pl.ds(pl.multiple_of(p * wide, 128), wide)], ssem.at[which, slot])

    def forward(p, _):
        slot = lax.rem(p, 2)
        cols = pl.ds(pl.multiple_of(p * wide, 128), wide)
        for i in range(pair):
            load_own(p * pair + i).wait()
            load(p * pair + i).wait()

        @pl.when(p >= 2)
        def _():
            out_copy(0, act_hbm, p - 2, slot).wait()

        halves = [slice(i, i + tokens // 2) for i in range(0, tokens, tokens // 2)]
        gates = [nt(nlow[r, :], w[p, :, :width]) for r in halves]
        ups = [nt(nlow[r, :], w[p, :, width : 2 * width]) for r in halves]
        for r, gp, up in zip(halves, gates, ups):
            g[r, cols] = gp
            u[r, cols] = up
            a = (gp * jax.nn.sigmoid(gp) * up).astype(bf16)
            stage[0, slot, r, :] = a
            acc[r, :] += nn(a, w[p, :, 2 * width :])
        out_copy(0, act_hbm, p, slot).start()
        return 0

    lax.fori_loop(0, steps, forward, 0)

    def middle(c, _):
        rows = pl.ds(pl.multiple_of(c * ROWS, ROWS), ROWS)
        unit, inv = normalise(acc[rows, :])
        layer_out[rows, :] = (unit * s2[...] + b2[...]).astype(bf16)
        up = cot[rows, :].astype(f32)
        d = norm_back(up, unit, inv, s2[...])
        small[2:3, :] += jnp.sum(up * unit, axis=0, keepdims=True)
        small[3:4, :] += jnp.sum(up, axis=0, keepdims=True)
        flow[rows, :] = d.astype(bf16)
        acc[rows, :] = d
        return 0

    lax.fori_loop(0, tokens // ROWS, middle, 0)
    for p in range(max(steps - 2, 0), steps):
        out_copy(0, act_hbm, p, p % 2).wait()

    def backward(p, _):
        slot = lax.rem(p, 2)
        cols = pl.ds(pl.multiple_of(p * wide, 128), wide)

        @pl.when(p >= 2)
        def _():
            out_copy(0, gg_hbm, p - 2, slot).wait()
            out_copy(1, ug_hbm, p - 2, slot).wait()

        halves = [slice(i, i + tokens // 2) for i in range(0, tokens, tokens // 2)]
        outer = [nt(flow[r, :], w[p, :, 2 * width :]) for r in halves]
        for r, da in zip(halves, outer):
            gp, up = g[r, cols], u[r, cols]
            sig = jax.nn.sigmoid(gp)
            both = da * sig
            dg = (both * up * (1.0 + gp * (1.0 - sig))).astype(bf16)
            du = (both * gp).astype(bf16)
            stage[0, slot, r, :] = dg
            stage[1, slot, r, :] = du
            acc[r, :] += nn(dg, w[p, :, :width]) + nn(du, w[p, :, width : 2 * width])
        out_copy(0, gg_hbm, p, slot).start()
        out_copy(1, ug_hbm, p, slot).start()
        return 0

    lax.fori_loop(0, steps, backward, 0)

    def tail(c, _):
        rows = pl.ds(pl.multiple_of(c * ROWS, ROWS), ROWS)
        up, unit = acc[rows, :], unit1[rows, :]
        d = norm_back(up, unit, inv1[rows, :], s1[...])
        small[0:1, :] += jnp.sum(up * unit, axis=0, keepdims=True)
        small[1:2, :] += jnp.sum(up, axis=0, keepdims=True)
        grad_one[rows, :] = d
        low = d.astype(bf16)
        brt[:, rows] = d.T.astype(bf16)
        for s in range(slots):
            back[s, rows, :] = nn(low, ws[s]).astype(bf16)
        return 0

    lax.fori_loop(0, tokens // ROWS, tail, 0)
    chunk[...] = jnp.zeros_like(chunk)
    room = chunk.shape[2]
    each = 4 * width // pieces // room
    for n in range(pieces * each):
        j, lane = divmod(n * room, width)
        chunk[n // each, n % each : n % each + 1, :] = small[j : j + 1, lane : lane + room]
    for p in range(max(steps - 2, 0), steps):
        out_copy(0, gg_hbm, p, p % 2).wait()
        out_copy(1, ug_hbm, p, p % 2).wait()


def ffn_layer(own, cot, norms, rel, w1, w_own, w2, room):
    slots, tokens, cols = rel.shape
    width = own.shape[1]
    pieces, share = w_own.shape[:2]
    units = pieces * slots * share
    pair = 2 if pieces % 2 == 0 else 1
    vm, hbm = pl.BlockSpec(memory_space=pltpu.VMEM), pl.BlockSpec(memory_space=pl.ANY)
    wide = jax.ShapeDtypeStruct((tokens, width), bf16)
    hidden = jax.ShapeDtypeStruct((tokens, units), bf16)
    return pl.pallas_call(
        functools.partial(ffn_kernel, slots=slots, pieces=pieces, share=share),
        out_shape=(wide, jax.ShapeDtypeStruct((tokens, width), f32), wide, wide, jax.ShapeDtypeStruct((width, tokens), bf16))
        + (jax.ShapeDtypeStruct((slots, tokens, cols), bf16), jax.ShapeDtypeStruct((pieces, 16, room), f32), hidden, hidden, hidden),
        in_specs=[vm] * 7 + [hbm] * 3,
        out_specs=(vm,) * 7 + (hbm,) * 3,
        scratch_shapes=[
            pltpu.VMEM((pieces // pair, pair * slots * share, 3 * width), bf16),
            pltpu.VMEM((pieces, slots, width // pieces, 256), bf16),
            pltpu.VMEM((slots, width, cols), bf16),
            pltpu.VMEM((tokens, units), f32),
            pltpu.VMEM((tokens, units), f32),
            pltpu.VMEM((tokens, width), f32),
            pltpu.VMEM((tokens, width), f32),
            pltpu.VMEM((tokens, 1), f32),
            pltpu.VMEM((tokens, width), f32),
            pltpu.VMEM((8, width), f32),
            pltpu.VMEM((2, 2, tokens, pair * slots * share), bf16),
            pltpu.SemaphoreType.DMA((pieces,)),
            pltpu.SemaphoreType.DMA((pieces,)),
            pltpu.SemaphoreType.DMA,
            pltpu.SemaphoreType.DMA((2, 2)),
        ],
        compiler_params=pltpu.CompilerParams(vmem_limit_bytes=50 << 20),
        cost_estimate=pl.CostEstimate(flops=16 << 30, bytes_accessed=30 << 20, transcendentals=3 << 20),
        name="ffn_layer",
    )(own, cot, *norms, rel, w1, w_own, w2)


def wgrad_kernel(*refs, slots, share, add):
    gg, ug, act, brt, nlow, flow, rel, small = refs[1:9]
    got = refs[9] if add else None
    width = nlow.shape[1]
    cols = rel.shape[2]
    edge = 3 * width + cols
    blk = slots * share
    out = refs[-1] if add else refs[-1].at[0]
    room = out.shape[1] - edge

    def put(rows, lanes, value):
        if add:
            value = value + got[0, rows, lanes].astype(f32)
        out[rows, lanes] = value.astype(bf16)

    terms = [tn(gg[...], nlow[...]), tn(ug[...], nlow[...]), tn(act[...], flow[...])]
    for s in range(slots):
        place = lax.rem(refs[0][1] - s + slots, slots)
        rows = pl.ds(pl.multiple_of(place * share, 32 if share % 32 == 0 else 4), share)
        for i in range(3):
            put(rows, slice(i * width, (i + 1) * width), terms[i][s * share : (s + 1) * share])
        put(rows, slice(3 * width, edge), nn(brt[...], rel[s]))
        put(rows, slice(edge, edge + room), jnp.concatenate([small[0], jnp.zeros((share - 16, room), f32)], axis=0))
    if add:
        first, second, rest = refs[10:13]
        top = first.shape[0]

        @pl.when(pl.program_id(0) == 0)
        def _():
            first[...] = out[:top, :]

        @pl.when(pl.program_id(0) == 1)
        def _():
            second[...] = out[:top, :]

        rest[0] = out[top:, :]


def wgrad(me, start, gg, ug, act, brt, nlow, flow, rel, small, got, pieces, share, span):
    slots = rel.shape[0]
    tokens, width = nlow.shape
    blk = slots * share
    top = slots // 2 * share

    def piece(i, me):
        return jnp.bitwise_xor(2 * i + start, me[0])

    both = pl.BlockSpec((1, blk, span), lambda i, me: (i, 0, 0))
    in_specs = [pl.BlockSpec((tokens, blk), lambda i, me: (0, piece(i, me)))] * 3
    in_specs += [pl.BlockSpec((width // pieces, tokens), lambda i, me: (piece(i, me), 0))]
    in_specs += [pl.BlockSpec((tokens, width), lambda i, me: (0, 0))] * 2
    in_specs += [pl.BlockSpec(rel.shape, lambda i, me: (0, 0, 0)), pl.BlockSpec((1,) + small.shape[1:], lambda i, me: (piece(i, me), 0, 0))]
    args = [stay(gg), stay(ug), stay(act), brt, nlow, flow, rel, small]
    if got is None:
        out_shape, out_specs, scratch = jax.ShapeDtypeStruct((2, blk, span), bf16), both, []
    else:
        in_specs.append(both)
        args.append(got)
        half = jax.ShapeDtypeStruct((top, span), bf16)
        out_shape = (half, half, jax.ShapeDtypeStruct((2, blk - top, span), bf16))
        fixed = pl.BlockSpec((top, span), lambda i, me: (0, 0))
        out_specs = (fixed, fixed, pl.BlockSpec((1, blk - top, span), lambda i, me: (i, 0, 0)))
        scratch = [pltpu.VMEM((blk, span), bf16)]
    return pl.pallas_call(
        functools.partial(wgrad_kernel, slots=slots, share=share, add=got is not None),
        out_shape=out_shape,
        grid_spec=pltpu.PrefetchScalarGridSpec(num_scalar_prefetch=1, grid=(2,), in_specs=in_specs, out_specs=out_specs, scratch_shapes=scratch),
        compiler_params=pltpu.CompilerParams(vmem_limit_bytes=24 << 20),
        cost_estimate=pl.CostEstimate(flops=2 << 30, bytes_accessed=10 << 20, transcendentals=0),
        name="wgrad",
    )(me, *args)


def final_kernel(gate, up, down, out_part, query, key, value, edge, gate_up_sum, down_sum, out_sum, qkv_sum, small_sum, *, heads, pieces, share, room):
    cols = heads * HD
    gate_up_sum[:, 0, :] = gate[...].astype(f32).T
    gate_up_sum[:, 1, :] = up[...].astype(f32).T
    down_sum[...] = down[...].astype(f32)
    out_sum[...] = out_part[...].astype(f32).T[:cols]
    for k, source in enumerate((query, key)):
        turned = source[...].astype(f32).T
        for h in range(heads):
            for half in range(2):
                start = 128 * half + HALF * h
                qkv_sum[k, HD * h + HALF * half : HD * h + HALF * (half + 1), :] = turned[start : start + HALF, :]
    qkv_sum[2, :, :] = value[...].astype(f32).T[:cols]

    @pl.when(pl.program_id(0) == 0)
    def _():
        width = small_sum.shape[1]
        each = 4 * width // pieces // room
        for n in range(pieces * each):
            j, lane = divmod(n * room, width)
            row = n // each * share + n % each
            base = row // 16 * 16
            block = edge[base : base + 16, 128 - room :].astype(f32)
            small_sum[j : j + 1, lane : lane + room] = block[row - base : row - base + 1, :]


def final_sums(main, width, span, heads, pieces):
    units = main.shape[0]
    lanes = 256
    steps = width // lanes
    cols = heads * HD
    room = span - 3 * width - cols
    tall = units // steps

    def band(first, size):
        return pl.BlockSpec((tall, size), lambda i, n=first // size: (i, n))

    in_specs = [pl.BlockSpec((units, lanes), lambda i: (0, i)), pl.BlockSpec((units, lanes), lambda i: (0, i + steps))]
    in_specs += [band(2 * width, width), band(3 * width, 256)] + [band(span + 256 * k, 256) for k in range(3)]
    in_specs += [pl.BlockSpec((units, 128), lambda i: (0, span // 128 - 1))]
    return pl.pallas_call(
        functools.partial(final_kernel, heads=heads, pieces=pieces, share=units // pieces, room=room),
        grid=(steps,),
        out_shape=(
            jax.ShapeDtypeStruct((width, 2, units), f32),
            jax.ShapeDtypeStruct((units, width), f32),
            jax.ShapeDtypeStruct((cols, width), f32),
            jax.ShapeDtypeStruct((3, cols, width), f32),
            jax.ShapeDtypeStruct((4, width), f32),
        ),
        in_specs=in_specs,
        out_specs=(
            pl.BlockSpec((lanes, 2, units), lambda i: (i, 0, 0)),
            pl.BlockSpec((tall, width), lambda i: (i, 0)),
            pl.BlockSpec((cols, tall), lambda i: (0, i)),
            pl.BlockSpec((3, cols, tall), lambda i: (0, 0, i)),
            pl.BlockSpec((4, width), lambda i: (0, 0)),
        ),
        cost_estimate=pl.CostEstimate(flops=1 << 20, bytes_accessed=15 << 20, transcendentals=0),
        name="final_sums",
    )(*[main] * 8)


ROPE_BASE = 1000.0


def rotate_axis(size, step):
    return [(i, (i + step) % size) for i in range(size)]


def line_axis(size, step):
    return [(i, i + step) for i in range(size) if 0 <= i + step < size]


def flip_axis(size, bit):
    return [(i, i ^ bit) for i in range(size)]


def after(value, *others):
    return lax.optimization_barrier((value, *others))[0]


def low_sum(left, right):
    return (left.astype(f32) + right.astype(f32)).astype(bf16)


def body(
    dp_size,
    tp_size,
    tokens,
    lengths,
    w_qkv,
    w_out,
    norm1_scale,
    norm1_shift,
    w_gate_up,
    w_down,
    norm2_scale,
    norm2_shift,
    cotangent,
):
    own = tokens[0]
    rows_here, width = own.shape
    docs = lengths.shape[1]
    seq = rows_here * tp_size
    cols_here = w_qkv.shape[2]
    heads = cols_here // HD
    units = w_gate_up.shape[2]
    pieces = min(dp_size, 8)
    groups = None if pieces == dp_size else [list(range(i, i + pieces)) for i in range(0, dp_size, pieces)]
    share = units // pieces
    rows_share = width // pieces
    span = -(-(3 * width + cols_here) // 128) * 128
    me = lax.rem(lax.axis_index("dp"), pieces)
    z = lax.axis_index("tensor")

    def flip(array, bit):
        return lax.ppermute(array, "dp", flip_axis(dp_size, bit))

    def shift(array, step):
        return lax.ppermute(array, "tensor", rotate_axis(tp_size, step))

    def along(array, step):
        return lax.ppermute(array, "tensor", line_axis(tp_size, step))

    def gather_dp(array):
        return lax.all_gather(array, "dp", axis=0, axis_index_groups=groups)

    def rope_order(matrix):
        halves = matrix.reshape(rows_share, heads, 2, HALF).transpose(0, 2, 1, 3).reshape(rows_share, 2, heads * HALF)
        return jnp.pad(halves, ((0, 0), (0, 0), (0, 128 - heads * HALF))).reshape(rows_share, 256)

    qkv_slice = lax.dynamic_slice_in_dim(w_qkv, me * rows_share, rows_share, 0)
    out_slice = lax.dynamic_slice_in_dim(w_out, me * rows_share, rows_share, 1)
    piece_one = jnp.concatenate([rope_order(qkv_slice[:, 0]), rope_order(qkv_slice[:, 1]), out_slice.T, qkv_slice[:, 2]], axis=1)
    gate_slice = lax.dynamic_slice_in_dim(w_gate_up, me * share, share, 2)
    down_slice = lax.dynamic_slice_in_dim(w_down, me * share, share, 0)
    piece_two = jnp.concatenate([gate_slice[:, 0].T, gate_slice[:, 1].T, down_slice], axis=1)
    piece_one, piece_two = lax.optimization_barrier((piece_one, piece_two))
    ones = [piece_one] + [shift(piece_one, s) for s in range(1, tp_size)]
    piece_two = after(piece_two, *ones[1:])
    twos = [shift(piece_two, s) for s in range(1, tp_size)]
    w1 = gather_dp(jnp.stack(ones))
    row_lengths, gate_up_late, down_late = after(lengths[0], ones[-1]), after(w_gate_up, ones[-1]), after(w_down, ones[-1])
    w_own = jnp.concatenate([gate_up_late[:, 0].T, gate_up_late[:, 1].T, down_late], axis=1).reshape(pieces, share, 3 * width)

    tables = doc_tables(row_lengths, seq, z * rows_here, rows_here)
    segment, position = tables[:2]
    info = make_info(tables, me)
    inverse = ROPE_BASE ** (-2.0 * lax.rem(jnp.arange(128), HALF).astype(f32) / HD)
    angles = position[:, None] * inverse[None, :]
    cosine, sine = jnp.cos(angles), jnp.sin(angles)
    seg_col = segment[:, None]

    twos, cosine, sine, seg_col, info, w_own = lax.optimization_barrier((twos, cosine, sine, seg_col, info, w_own))
    w2 = gather_dp(jnp.concatenate(twos, axis=0))

    own_late = after(own, *ones[1:])
    before, behind = along(own_late, 1), along(own_late, -1)

    *held, qh = project(own, w1, cosine, sine, seg_col, docs, heads, 0, tp_size)
    held, before, behind = lax.optimization_barrier((held, before, behind))
    before2, behind2 = along(before, 1), along(behind, -1)
    held = project(behind, w1, cosine, sine, seg_col, docs, heads, 1, tp_size, held)
    held = project(before, w1, cosine, sine, seg_col, docs, heads, 3, tp_size, held)
    held, behind2, before2 = lax.optimization_barrier((held, behind2, before2))
    toks = [own, behind, jnp.where(z < tp_size // 2, behind2, before2), before]
    held = project(toks[2], w1, cosine, sine, seg_col, docs, heads, 2, tp_size, held)
    lse, rel = attn_fwd(info, seg_col, qh, held[0], held[2], docs)
    saved = (qh, held[0].reshape(tp_size, seq, -1), held[1].reshape(tp_size, seq, -1), lse, rel)
    norms = [v.reshape(1, width) for v in (norm1_scale, norm1_shift, norm2_scale, norm2_shift)]
    room = span - 3 * width - cols_here
    layer_out, grad_one, nlow, flow, brt, back, chunk, act, gg, ug = ffn_layer(own, cotangent[0], norms, rel, w1, w_own, w2, room)

    half = tp_size // 2

    me_array = jnp.stack([me, z]).astype(jnp.int32)
    fixed = (gg, ug, act, brt, nlow, flow, rel, chunk)
    far_sent = wgrad(me_array, 5, *fixed, None, pieces, share, span)
    near_sent = wgrad(after(me_array, far_sent), 1, *fixed, None, pieces, share, span)
    far_keep, far_give, far_rest = wgrad(after(me_array, near_sent), 4, *fixed, flip(far_sent, 1), pieces, share, span)
    near_keep, near_give, near_rest = wgrad(after(me_array, far_rest), 0, *fixed, flip(near_sent, 1), pieces, share, span)

    back, near_give = lax.optimization_barrier((back, near_give))
    got = [flip(far_give, 2), flip(far_rest, 4), flip(near_give, 2)]
    backward = functools.partial(attn_bwd, info, toks, cosine, sine, seg_col, saved)
    cut = tp_size - 1
    dw_low, kv_low, q_low = backward(back, docs, heads, pieces, 0, cut)
    got, dw_low, back_late = lax.optimization_barrier((got, dw_low, back))
    next_b = low_sum(near_rest, got[1])
    give_a, next_a = low_sum(far_keep, got[0]), low_sum(near_keep, got[2])
    back_late, next_a, give_a, next_b = lax.optimization_barrier((back_late, next_a, give_a, next_b))
    got_a, got_b, got_low = flip(give_a, 4), flip(next_b[1], 2), flip(dw_low.reshape((pieces // 2, 2) + dw_low.shape[1:])[:, 1], 1)
    dw_high, kv_high, q_high = backward(back_late, docs, heads, pieces, cut, tp_size)
    got_a, got_b, got_low, dw_high, kv_high = lax.optimization_barrier((got_a, got_b, got_low, dw_high, kv_high))
    parts_two = jnp.concatenate([low_sum(next_a, got_a), low_sum(next_b[0], got_b)], axis=0)
    share_two = lax.psum_scatter(parts_two, "tensor", scatter_dimension=0, tiled=True)

    def pairs_of(array):
        return array.reshape((pieces // 2, 2) + array.shape[1:])

    got_high = flip(pairs_of(dw_high)[:, 1], 1)
    dx_own, dx = token_grads(info, w1, (kv_low, kv_high), (q_low, q_high), cols_here, tp_size)
    low = low_sum(pairs_of(dw_low)[:, 0], got_low).reshape((2, 2) + dw_low.shape[1:])
    got_a = flip(low[:, 1, :half], 2)
    high = low_sum(pairs_of(dw_high)[:, 0], got_high).reshape((2, 2) + dw_high.shape[1:])
    high = jnp.concatenate([low[:, :, half:], high], axis=2)
    got_b = flip(high[1], 4)
    next_a, next_b = low_sum(low[:, 0, :half], got_a), low_sum(high[0], got_b)
    got_a, got_b = flip(next_a[1], 4), flip(next_b[1], 2)

    def by_slot(low, high):
        low, high = low.reshape(half, -1, low.shape[-1]), high.reshape(tp_size - half, -1, high.shape[-1])
        return [low[i] for i in range(half)] + [high[i] for i in range(tp_size - half)]

    def total(own_part, moved):
        return functools.reduce(lambda x, y: x + y.astype(f32), moved, own_part.astype(f32)).astype(bf16)

    parts_one = by_slot(low_sum(next_a[0], got_a), low_sum(next_b[0], got_b))
    moved_one = [shift(parts_one[s], -s) for s in range(1, tp_size)]
    moved_one, dx = lax.optimization_barrier((moved_one, dx))
    share_one = total(parts_one[0], moved_one)
    from_left = lax.ppermute(dx[2], "tensor", [(i, i + 1) for i in range(half)])
    from_right = lax.ppermute(dx[2], "tensor", [(i + half, i + half - 1) for i in range(half)])
    near_right, near_left = low_sum(dx[1], from_left), low_sum(dx[3], from_right)
    from_before, from_behind = along(near_right, 1), along(near_left, -1)

    def finish(array):
        if groups is not None:
            across = [[g * pieces + i for g in range(dp_size // pieces)] for i in range(pieces)]
            array = lax.psum(array.astype(f32), "dp", axis_index_groups=across).astype(bf16)
        return gather_dp(array)

    main = finish(jnp.concatenate([share_two, share_one], axis=1)).reshape(units, -1)
    gate_up_sum, down_sum, out_sum, qkv_turned, small_out = final_sums(main, width, span, heads, pieces)
    qkv_sum = qkv_turned.transpose(2, 0, 1)
    from_before, from_behind, small_out = lax.optimization_barrier((from_before, from_behind, small_out))
    input_grad = grad_one + dx_own + from_before.astype(f32) + from_behind.astype(f32)
    return (
        layer_out[None],
        input_grad[None],
        qkv_sum,
        out_sum,
        small_out[0],
        small_out[1],
        gate_up_sum,
        down_sum,
        small_out[2],
        small_out[3],
    )


def solution(mesh):
    in_specs = (
        P("dp", "tensor", None),
        P("dp", None),
        P(None, None, "tensor"),
        P("tensor", None),
        P(),
        P(),
        P(None, None, "tensor"),
        P("tensor", None),
        P(),
        P(),
        P("dp", "tensor", None),
    )
    out_specs = (
        P("dp", "tensor", None),
        P("dp", "tensor", None),
        P(None, None, "tensor"),
        P("tensor", None),
        P(),
        P(),
        P(None, None, "tensor"),
        P("tensor", None),
        P(),
        P(),
    )
    return jax.shard_map(
        functools.partial(body, mesh.shape["dp"], mesh.shape["tensor"]),
        mesh=mesh,
        in_specs=in_specs,
        out_specs=out_specs,
        check_vma=False,
    )
```
